256 devices in a mesh: wide: 32 (over z, x_lo, core), narrow: 8 (over y, x_hi).
Axes of the slice: x: 4 (x_hi: 2, x_lo: 2; x = x_hi * 2 + x_lo), y: 4, z: 8, core: 2. Of those that a mesh axis runs over, the one named last changes fastest.
Arguments:
- design: float32 [384, 384, 384], P('wide', 'narrow'), may hold values from 0 to 1
- passive: int32 [384, 384, 384], P('wide', 'narrow'), may hold values 0 or 1
- displacement: float32 [3, 3, 128, 128, 128], P(None, None, 'wide', 'narrow'), may hold values from -6 to 6
- support: int32 [128, 128, 128], P('wide', 'narrow'), may hold values 0 or 1
- loading: int32 [128, 128, 128], P('wide', 'narrow'), may hold values 0 or 1
Outputs:
- residual: float32 [3, 3, 128, 128, 128], P(None, None, 'wide', 'narrow')
- compliance: float32 [3], replicated
- sensitivity: float32 [384, 384, 384], P('wide', 'narrow')
The draws below stay inside these ranges and needn't reach their ends.
All inputs are finite; a program needn't handle non-finite values. No bound on the sum of `passive` or of `support` or of `loading` on one device may be relied on, other than what follows from the above.
Results may differ from the reference program's by a relative error of at most 0.0001.
Values sent between devices are 32-bit elements; how exact they have to be, the bound alone decides.
A program may use at most 64 MiB of HBM per device.

```python
import math
import jax
import jax.numpy as jnp
import numpy as np
from jax import lax

ELEMENTS_THIRD = 128
RAD = 3
ELEMENTS_FIRST = 128
ELEMENTS_SECOND = 128
NX = 384
NY = 384
VOXELS_THIRD = 384


def plant(values, stream_key, least, largest):
    shape = values.shape
    index_at = [jax.random.randint(jax.random.fold_in(stream_key, axis), (), 0, shape[axis]) for axis in range(len(shape))]
    values = values.at[tuple(index_at)].set(least)
    longest = shape.index(max(shape))
    index_at[longest] = (index_at[longest] + 1) % shape[longest]
    return values.at[tuple(index_at)].set(largest)


def levels(key, shape, cuts, low, largest):
    def one(axis_at, shards_of):
        steps = jax.random.uniform(jax.random.fold_in(jax.random.fold_in(key, 6), axis_at), (shards_of,), jnp.float32, low / len(cuts), largest / len(cuts))
        return jnp.repeat(jnp.exp(steps), shape[axis_at] // shards_of).reshape((-1,) + (1,) * (len(shape) - axis_at - 1))

    factor_of = one(*cuts[0])
    for cut in cuts[1:]:
        factor_of = factor_of * one(*cut)
    return factor_of


def noise(own_key, shape, scale, most, split=(), held_as=jnp.bfloat16):
    gain = levels(own_key, shape, split, -0.22, 0.18) if split else 1.0
    entries = jax.random.normal(own_key, shape, jnp.float32) * scale * gain
    return jnp.minimum(jnp.maximum(entries, -most), most).astype(held_as)


def setup_inputs(seed: int = 0) -> dict:
    seeds = jax.random.split(jax.random.key(seed), 6)
    return {
        "design": jnp.clip(1.0 * jax.random.uniform(seeds[0], (NX, NY, VOXELS_THIRD), jnp.float32) ** levels(seeds[0], (NX, NY, VOXELS_THIRD), ((0, 32), (1, 8)), -0.2, 0.2), 0.0, 1.0),
        "passive": plant((jax.random.randint(seeds[1], (NX, NY, VOXELS_THIRD), 0, 8) < 1).astype(jnp.int32), jax.random.fold_in(seeds[1], 1), 0, 1),
        "displacement": noise(seeds[2], (3, 3, ELEMENTS_FIRST, ELEMENTS_SECOND, ELEMENTS_THIRD), 1.0, 6.0, ((2, 32), (3, 8)), jnp.float32),
        "support": plant((jax.random.randint(seeds[3], (ELEMENTS_FIRST, ELEMENTS_SECOND, ELEMENTS_THIRD), 0, 16) < 1).astype(jnp.int32), jax.random.fold_in(seeds[3], 1), 0, 1),
        "loading": plant((jax.random.randint(seeds[4], (ELEMENTS_FIRST, ELEMENTS_SECOND, ELEMENTS_THIRD), 0, 16) < 1).astype(jnp.int32), jax.random.fold_in(seeds[4], 1), 0, 1),
    }


sharpness = 8.0
thresholds = (0.7, 0.5, 0.3)
stiff_floor = 0.001
load_force = 4.0
poisson = 0.3

def element_matrix():
    inv_root = 1.0 / np.sqrt(3.0)
    elastic_scale = 1.0 / ((1.0 + poisson) * (1.0 - 2.0 * poisson))
    elastic = np.zeros((6, 6))
    for row_i in range(3):
        for col_j in range(3):
            elastic[row_i, col_j] = poisson
        elastic[row_i, row_i] = 1.0 - poisson
    for row_i in range(3, 6):
        elastic[row_i, row_i] = 0.5 - poisson
    elastic = elastic * elastic_scale
    corner_signs = [(2 * (corner // 4) - 1, 2 * (corner // 2 % 2) - 1, 2 * (corner % 2) - 1) for corner in range(8)]
    stiffness = np.zeros((24, 24))
    for gauss_a in (-inv_root, inv_root):
        for gauss_b in (-inv_root, inv_root):
            for gauss_c in (-inv_root, inv_root):
                gauss_point = (gauss_a, gauss_b, gauss_c)
                derivs = np.zeros((8, 3))
                for corner in range(8):
                    for along in range(3):
                        slope_value = corner_signs[corner][along] / 8.0
                        for second in range(3):
                            if second != along:
                                slope_value = slope_value * (1.0 + corner_signs[corner][second] * gauss_point[second])
                        derivs[corner, along] = 2.0 * slope_value
                strain = np.zeros((6, 24))
                for corner in range(8):
                    column = 3 * corner
                    strain[0, column] = derivs[corner, 0]
                    strain[1, column + 1] = derivs[corner, 1]
                    strain[2, column + 2] = derivs[corner, 2]
                    strain[3, column] = derivs[corner, 1]
                    strain[3, column + 1] = derivs[corner, 0]
                    strain[4, column + 1] = derivs[corner, 2]
                    strain[4, column + 2] = derivs[corner, 1]
                    strain[5, column] = derivs[corner, 2]
                    strain[5, column + 2] = derivs[corner, 0]
                stiffness = stiffness + strain.T @ elastic @ strain * 0.125
    return stiffness.astype(np.float32)

def blur_axis(padded, axis_dim, length):
    summed = float(1 - RAD + RAD) * lax.slice_in_dim(padded, 0, length, axis=axis_dim)
    for offset in range(1, 2 * RAD + 1):
        summed = summed + float(RAD + 1 - abs(offset - RAD)) * lax.slice_in_dim(padded, offset, offset + length, axis=axis_dim)
    return summed

def edge_weights(start_index, amount, extent):
    places = start_index + jnp.arange(amount, dtype=jnp.int32)
    summed = jnp.zeros((amount,), jnp.float32)
    for offset in range(-RAD, RAD + 1):
        inside = ((places + offset >= 0) & (places + offset < extent)).astype(jnp.float32)
        summed = summed + float(RAD + 1 - abs(offset)) * inside
    return summed

def smooth_field(source):
    padded = jnp.pad(source, RAD)
    rowwise = blur_axis(padded, 0, source.shape[0])
    colwise = blur_axis(rowwise, 1, source.shape[1])
    return blur_axis(colwise, 2, source.shape[2])

def project(blurred, threshold):
    low_end = float(math.tanh(sharpness * threshold))
    denominator = low_end + float(math.tanh(sharpness * (1.0 - threshold)))
    steep_part = jnp.tanh(sharpness * (blurred - threshold))
    return ((low_end + steep_part) / denominator, sharpness * (1.0 - steep_part * steep_part) / denominator)

def depth_averaging(fine_len, coarse_len):
    rows_index = jnp.arange(fine_len, dtype=jnp.int32)[:, None] // 3
    cols_index = jnp.arange(coarse_len, dtype=jnp.int32)[None, :]
    return (rows_index == cols_index).astype(jnp.float32)

def aggregate(fine_stiff, coarse_averaging, count_x, count_y):
    merged = jnp.dot(fine_stiff.reshape(-1, fine_stiff.shape[2]), coarse_averaging, precision=lax.Precision.HIGHEST)
    merged = merged.reshape(count_x, 3, count_y, 3, coarse_averaging.shape[1])
    return lax.optimization_barrier(jnp.sum(merged, axis=(1, 3))) / 27.0

def spread(coarse, coarse_averaging):
    count_x, count_y, count_z = coarse.shape
    deepened = jnp.dot(coarse.reshape(-1, count_z), coarse_averaging.T, precision=lax.Precision.HIGHEST)
    deepened = deepened.reshape(count_x, 1, count_y, 1, coarse_averaging.shape[0])
    return jnp.broadcast_to(deepened, (count_x, 3, count_y, 3, coarse_averaging.shape[0])).reshape(3 * count_x, 3 * count_y, coarse_averaging.shape[0])

def element_contributions(nodal_values, moduli, count_x, count_y, count_z, operator_matrix):
    batch = nodal_values.shape[0]
    corners = []
    for corner in range(8):
        along_x, along_y, along_z = (corner // 4, corner // 2 % 2, corner % 2)
        corners.append(nodal_values[:, :, along_x:along_x + count_x, along_y:along_y + count_y, along_z:along_z + count_z])
    stacked = jnp.stack(corners, axis=1).reshape(batch, 24, count_x, count_y, count_z)
    product = jnp.einsum('ij,bjxyz->bixyz', operator_matrix, stacked, precision=lax.Precision.HIGHEST)
    strain_energy = lax.optimization_barrier(jnp.sum(stacked * product, axis=1))
    return (strain_energy, moduli[:, None] * product)

def gather_global(external_loads, count_x, count_y, count_z):
    summed = jnp.zeros((external_loads.shape[0], 3, count_x + 1, count_y + 1, count_z + 1), jnp.float32)
    for corner in range(8):
        along_x, along_y, along_z = (corner // 4, corner // 2 % 2, corner % 2)
        summed = summed.at[:, :, along_x:along_x + count_x, along_y:along_y + count_y, along_z:along_z + count_z].add(external_loads[:, 3 * corner:3 * corner + 3])
    return summed

def reference(design, passive, displacement, support, loading):
    solid_mask = 1.0 - passive.astype(jnp.float32)
    freedom = 1.0 - support.astype(jnp.float32)
    load_values = load_force * loading.astype(jnp.float32)
    weights = edge_weights(0, NX, NX)[:, None, None] * edge_weights(0, NY, NY)[None, :, None] * edge_weights(0, VOXELS_THIRD, VOXELS_THIRD)[None, None, :]
    blurred = smooth_field(design) / weights
    coarse_averaging = depth_averaging(VOXELS_THIRD, ELEMENTS_THIRD)
    operator_matrix = jnp.asarray(element_matrix(), dtype=jnp.float32)
    zeros_field = jnp.zeros_like(load_values)
    applied = jnp.stack([zeros_field, zeros_field, -load_values])
    residuals = []
    compliances = []
    gradient = jnp.zeros_like(design)
    for level_index in range(3):
        density, slope_term = project(blurred, thresholds[level_index])
        density = density * solid_mask
        young_modulus = aggregate(stiff_floor + (1.0 - stiff_floor) * density ** 3, coarse_averaging, ELEMENTS_FIRST, ELEMENTS_SECOND)
        masked_moves = displacement[level_index] * freedom
        nodal_values = jnp.pad(masked_moves, ((0, 0), (0, 1), (0, 1), (0, 1)))[None]
        strain_energy, external_loads = element_contributions(nodal_values, young_modulus[None], ELEMENTS_FIRST, ELEMENTS_SECOND, ELEMENTS_THIRD, operator_matrix)
        global_gathered = gather_global(external_loads, ELEMENTS_FIRST, ELEMENTS_SECOND, ELEMENTS_THIRD)[0, :, :ELEMENTS_FIRST, :ELEMENTS_SECOND, :ELEMENTS_THIRD]
        residuals.append((applied - global_gathered) * freedom)
        compliance = jnp.sum(young_modulus * strain_energy[0])
        compliances.append(compliance)
        gradient = gradient - 3.0 * (1.0 - stiff_floor) / 27.0 * density ** 2 * spread(strain_energy[0] / compliance, coarse_averaging) * slope_term * solid_mask
    sensitivity = smooth_field(gradient / weights)
    return (jnp.stack(residuals), jnp.stack(compliances), sensitivity)
```

```python
import functools
import math

import jax
import jax.numpy as jnp
import numpy as np
from jax import lax
from jax.experimental import pallas as pl
from jax.experimental.pallas import tpu as pltpu
from jax.sharding import PartitionSpec as P

sharpness = 8.0
thresholds = (0.7, 0.5, 0.3)
stiff_floor = 0.001
load_force = 4.0
poisson = 0.3

F32, BF16 = jnp.float32, jnp.bfloat16
MESH = pl.DeviceIdType.MESH
ROWS, COLS, DEEP = 12, 48, 384
EX, EY, EZ = 4, 16, 128
DIRS = ((1, 0), (-1, 0), (0, 1), (0, -1), (1, 1), (1, -1), (-1, 1), (-1, -1))


def element_matrix():
    inv_root = 1.0 / np.sqrt(3.0)
    elastic = np.full((3, 3), poisson) + np.eye(3) * (1.0 - 2.0 * poisson)
    elastic = np.block(
        [[elastic, np.zeros((3, 3))], [np.zeros((3, 3)), np.eye(3) * (0.5 - poisson)]]
    ) / ((1.0 + poisson) * (1.0 - 2.0 * poisson))
    signs = [(2 * (c // 4) - 1, 2 * (c // 2 % 2) - 1, 2 * (c % 2) - 1) for c in range(8)]
    stiffness = np.zeros((24, 24))
    for ga in (-inv_root, inv_root):
        for gb in (-inv_root, inv_root):
            for gc in (-inv_root, inv_root):
                point = (ga, gb, gc)
                strain = np.zeros((6, 24))
                for c in range(8):
                    d = []
                    for along in range(3):
                        s = signs[c][along] / 4.0
                        for other in range(3):
                            if other != along:
                                s = s * (1.0 + signs[c][other] * point[other])
                        d.append(s)
                    col = 3 * c
                    strain[0, col], strain[1, col + 1], strain[2, col + 2] = d
                    strain[3, col], strain[3, col + 1] = d[1], d[0]
                    strain[4, col + 1], strain[4, col + 2] = d[2], d[1]
                    strain[5, col], strain[5, col + 2] = d[2], d[0]
                stiffness = stiffness + strain.T @ elastic @ strain * 0.125
    return stiffness


def mode_matrix():
    h = np.zeros((8, 8))
    for mode in range(8):
        for c in range(8):
            v = 1.0
            for bit in (4, 2, 1):
                if mode & bit:
                    v *= 1.0 if c & bit else -1.0
            h[mode, c] = v
    full = np.kron(h, np.eye(3))
    k = full @ element_matrix() @ full.T / 64.0
    return [
        [(j, float(k[i, j])) for j in range(24) if abs(k[i, j]) > 1e-9] for i in range(24)
    ]


def tent(values):
    p = [a + b for a, b in zip(values, values[1:])]
    q = [a + b for a, b in zip(p, p[2:])]
    r = [a + b for a, b in zip(q, q[1:])]
    return [a + b for a, b in zip(r, r[2:])]


def inverse_weight(place, extent):
    edge = jnp.minimum(place, extent - 1 - place)
    return jnp.where(
        edge >= 3, 1.0 / 16.0, jnp.where(edge == 2, 1.0 / 15.0, jnp.where(edge == 1, 1.0 / 13.0, 0.1))
    ).astype(F32)


def split(value):
    high = value.astype(BF16)
    return high, (value - high.astype(F32)).astype(BF16)


def times(value, matrix):
    high, low = split(value)
    return jnp.dot(high, matrix, preferred_element_type=F32) + jnp.dot(
        low, matrix, preferred_element_type=F32
    )


def level(bl, eta):
    low = math.tanh(sharpness * eta)
    den = low + math.tanh(sharpness * (1.0 - eta))
    t = jnp.tanh(bl * sharpness - sharpness * eta)
    rho = t * (1.0 / den) + low / den
    return rho, 1.0 - t * t


def slope_scale(eta):
    den = math.tanh(sharpness * eta) + math.tanh(sharpness * (1.0 - eta))
    return sharpness / den * 3.0 * (1.0 - stiff_floor) / 27.0


def kernel(
    wide, narrow,
    design, passive, disp, support, loading,
    res_out, comp_out, sens_out,
    D, XF, AH, AL, PA, BL, T, EN, ESP, GX, OUT, V, M, FS, FXR, FYR, FDR, U, SU, LO, RES, MOD, S3,
    WT, BAND, SPREAD, GATHER, AR1, AR2, RX,
    lsem, osem, dss, drs, mss, mrs, bss, brs, ess, ers, fss, frs, a1s, a1r, a2s, a2r,
):
    w = lax.axis_index("wide")
    n = lax.axis_index("narrow")
    zc, xl, core = w // 4, (w // 2) % 2, w % 2
    count1, count2 = wide // 2, 2 * narrow
    i1 = zc * 2 + core
    i2 = xl * narrow + n

    def within(dw, dn):
        ok = None
        for step, at, count in ((dw, w, wide), (dn, n, narrow)):
            if step:
                cond = at < count - 1 if step > 0 else at > 0
                ok = cond if ok is None else ok & cond
        return ok

    def peer1(k):
        j = (i1 + k) % count1
        return j, ((j // 2) * 4 + xl * 2 + j % 2, n)

    def peer2(k):
        j = (i2 + k) % count2
        return j, (zc * 4 + (j // narrow) * 2 + core, j % narrow)

    def around(dw, dn):
        return ((w + dw + wide) % wide, (n + dn + narrow) % narrow)

    barrier = pltpu.get_barrier_semaphore()
    total = count1 - 1 + count2 - 1
    for dw, dn in DIRS:
        total = total + within(dw, dn).astype(jnp.int32)

        @pl.when(within(dw, dn))
        def _(dw=dw, dn=dn):
            pl.semaphore_signal(barrier, 1, device_id=around(dw, dn), device_id_type=MESH)

    for k in range(1, count1):
        pl.semaphore_signal(barrier, 1, device_id=peer1(k)[1], device_id_type=MESH)
    for k in range(1, count2):
        pl.semaphore_signal(barrier, 1, device_id=peer2(k)[1], device_id_type=MESH)

    loads = [
        pltpu.make_async_copy(disp, U, lsem.at[0]),
        pltpu.make_async_copy(support, SU, lsem.at[1]),
        pltpu.make_async_copy(design, D.at[3:15, 8:56, :], lsem.at[2]),
        pltpu.make_async_copy(loading, LO, lsem.at[3]),
    ] + [
        pltpu.make_async_copy(passive.at[:, :, 128 * c : 128 * c + 128], PA.at[:, c], lsem.at[4 + c])
        for c in range(3)
    ]
    for copy in loads:
        copy.start()

    def near(shape):
        return lax.broadcasted_iota(jnp.int32, shape, 0), lax.broadcasted_iota(jnp.int32, shape, 1)

    a, b = near((DEEP, DEEP))
    BAND[...] = jnp.maximum(4 - jnp.abs(a - b), 0).astype(F32).astype(BF16)
    a, b = near((EZ, DEEP))
    gap = b - 3 * a
    SPREAD[...] = jnp.where((gap >= 0) & (gap < 3), 1.0, 0.0).astype(BF16)
    a, b = near((DEEP, EZ))
    gap = a - 3 * b
    GATHER[...] = jnp.where((gap >= 0) & (gap < 3), 1.0, 0.0).astype(BF16)
    a, b = near((24, DEEP))
    a = jnp.where(a == 23, -1, a)
    deep = inverse_weight(b, DEEP)
    for m in range(3):
        WT[m] = inverse_weight(n * COLS + 3 * a + m, narrow * COLS) * deep
    for x in range(18):
        RX[x] = inverse_weight(w * ROWS + x - 3, wide * ROWS)

    zero = functools.partial(jnp.zeros, dtype=F32)

    @pl.when(w == 0)
    def _():
        D[0:3] = zero((3, 64, DEEP))
        BL[0:3] = zero((3, 3, 32, DEEP))
        EN[:, 0] = zero((3, 32, 128))
        FXR[...] = zero((9, 16, 128))

    @pl.when(w == wide - 1)
    def _():
        D[15:18] = zero((3, 64, DEEP))
        BL[15:18] = zero((3, 3, 32, DEEP))
        EN[:, 5] = zero((3, 32, 128))
        M[:, 4] = zero((9, 24, 128))

    @pl.when(n == 0)
    def _():
        D[:, 0:8] = zero((18, 8, DEEP))
        BL[:, :, 0:8] = zero((18, 3, 8, DEEP))
        EN[:, :, 0:8] = zero((3, 6, 8, 128))
        FYR[...] = zero((9, 4, 8, 128))

    @pl.when(n == narrow - 1)
    def _():
        D[:, 56:64] = zero((18, 8, DEEP))
        BL[:, :, 24:32] = zero((18, 3, 8, DEEP))
        EN[:, :, 24:32] = zero((3, 6, 8, 128))
        M[:, :, 16:24] = zero((9, 5, 8, 128))

    @pl.when((n == 0) | (w == 0))
    def _():
        FDR[...] = zero((9, 8, 128))

    FS[...] = zero((9, 5, 24, 128))

    class Message:
        def __init__(self, src, dst, ss, rs, dw, dn):
            self.to, self.origin = within(dw, dn), within(-dw, -dn)
            self.copy = pltpu.make_async_remote_copy(
                src_ref=src, dst_ref=dst, send_sem=ss, recv_sem=rs,
                device_id=around(dw, dn), device_id_type=MESH,
            )

        def start(self):
            pl.when(self.to)(self.copy.start)

        def wait_send(self):
            pl.when(self.to)(self.copy.wait_send)

        def wait_recv(self):
            pl.when(self.origin)(self.copy.wait_recv)

    def x_part(dw, low, high, depth):
        if dw == 0:
            return pl.ds(low, high - low), pl.ds(low, high - low)
        if dw > 0:
            return pl.ds(high - depth, depth), pl.ds(low - depth, depth)
        return pl.ds(low, depth), pl.ds(high, depth)

    designs, fields, energies = [], [], []
    for d, (dw, dn) in enumerate(DIRS):
        sx, tx = x_part(dw, 0, ROWS, 3)
        tx = pl.ds(tx.start + 3, tx.size)
        sy, ty = x_part(dn, 0, COLS, 3)
        ty = pl.ds(ty.start + 8, ty.size)
        designs.append(
            Message(design.at[sx, sy, :], D.at[tx, ty, :], dss.at[d], drs.at[d], dw, dn)
        )
        sx, tx = x_part(dw, 3, 15, 3)
        sy, ty = x_part(dn, 8, 24, 1)
        fields.append(
            Message(BL.at[sx, :, sy, :], BL.at[tx, :, ty, :], bss.at[d], brs.at[d], dw, dn)
        )
        sx, tx = x_part(dw, 1, 5, 1)
        energies.append(
            Message(EN.at[:, sx, sy, :], EN.at[:, tx, ty, :], ess.at[d], ers.at[d], dw, dn)
        )
    moves, forces = [], []
    for d, (dw, dn) in enumerate(((-1, 0), (0, -1), (-1, -1))):
        sx, tx = x_part(dw, 0, 4, 1)
        sy, ty = x_part(dn, 0, 16, 1)
        moves.append(Message(M.at[:, sx, sy, :], M.at[:, tx, ty, :], mss.at[d], mrs.at[d], dw, dn))
    forces.append(Message(FS.at[:, 4, 0:16, :], FXR, fss.at[0], frs.at[0], 1, 0))
    forces.append(
        Message(FS.at[:, 0:4, 16:17, :], FYR.at[:, :, 0:1, :], fss.at[1], frs.at[1], 0, 1)
    )
    forces.append(Message(FS.at[:, 4, 16:17, :], FDR.at[:, 0:1, :], fss.at[2], frs.at[2], 1, 1))

    loads[0].wait()
    loads[1].wait()
    free = 1.0 - SU[...].astype(F32)
    for k in range(9):
        M[k, 0:4, 0:16] = U[k] * free

    pl.semaphore_wait(barrier, total)
    for message in moves:
        message.start()
    for message in designs:
        message.start()

    modes = mode_matrix()
    lane = lax.broadcasted_iota(jnp.int32, (8, 128), 1)
    for message in moves:
        message.wait_recv()

    def energy_step(i, _):
        r, l = i // 4, i % 4
        for t in range(2):
            hat = [None] * 24
            for comp in range(3):
                k = r * 3 + comp
                corner = {}
                for p in range(2):
                    for q in range(2):
                        v = M[k, l + p, pl.ds(8 * t + q, 8), :]
                        v1 = jnp.where(lane < 127, pltpu.roll(v, 127, axis=1), 0.0)
                        corner[p, q, 0], corner[p, q, 1] = v + v1, v1 - v
                for s in range(2):
                    y = {}
                    for p in range(2):
                        y[p, 0] = corner[p, 0, s] + corner[p, 1, s]
                        y[p, 1] = corner[p, 1, s] - corner[p, 0, s]
                    for q in range(2):
                        hat[3 * (2 * q + s) + comp] = y[0, q] + y[1, q]
                        hat[3 * (4 + 2 * q + s) + comp] = y[1, q] - y[0, q]
            energy = None
            for row in range(24):
                if not modes[row]:
                    continue
                value = None
                for j, factor in modes[row]:
                    term = hat[j] * factor
                    value = term if value is None else value + term
                V[i, row, 8 * t : 8 * t + 8] = value
                term = value * hat[row]
                energy = term if energy is None else energy + term
            EN[r, 1 + l, 8 + 8 * t : 16 + 8 * t] = energy
        return 0

    lax.fori_loop(0, 12, energy_step, 0)
    for message in energies:
        message.start()

    loads[2].wait()
    for message in designs:
        message.wait_recv()

    def x_step(t, _):
        rows = pl.ds(pl.multiple_of(8 * t, 8), 8)
        for c in range(3):
            out = tent([D[x, rows, 128 * c : 128 * c + 128] for x in range(18)])
            for x in range(ROWS):
                XF[x, c, rows, :] = out[x]
        return 0

    lax.fori_loop(0, 8, x_step, 0)

    def keep(x, parts):
        for m in range(3):
            block = jnp.concatenate(
                [jnp.concatenate([parts[m, t, c] for t in range(2)], axis=0) for c in range(3)], axis=1
            )
            high, low = split(block)
            AH[x, 16 * m : 16 * m + 16, :] = high
            AL[x, 16 * m : 16 * m + 16, :] = low

    def y_step(x, _):
        parts = {}
        for t in range(2):
            for c in range(3):
                out = tent([XF[x, c, pl.ds(8 + 24 * t + k, 8, stride=3), :] for k in range(-3, 6)])
                for m in range(3):
                    parts[m, t, c] = out[m]
        keep(x, parts)
        return 0

    lax.fori_loop(0, ROWS, y_step, 0)
    for copy in loads[4:]:
        copy.wait()

    def banded(g):
        rows = pl.ds(3 * g, 3)
        band = BAND[...]
        return jnp.dot(
            AH[rows].reshape(144, DEEP), band, preferred_element_type=F32
        ) + jnp.dot(AL[rows].reshape(144, DEEP), band, preferred_element_type=F32)

    def z_step(g, _):
        z = banded(g)
        for xr in range(3):
            x = 3 * g + xr
            for m in range(3):
                value = z[16 * (3 * xr + m) : 16 * (3 * xr + m) + 16] * (WT[m, 0:16] * RX[x + 3])
                for t in range(2):
                    for c in range(3):
                        void = PA[x, c, pl.ds(24 * t + m, 8, stride=3), :]
                        part = value[8 * t : 8 * t + 8, 128 * c : 128 * c + 128]
                        BL[x + 3, m, 8 + 8 * t : 16 + 8 * t, 128 * c : 128 * c + 128] = part * (
                            1.0 - void.astype(F32)
                        )
        return 0

    lax.fori_loop(0, 4, z_step, 0)
    for message in fields:
        message.start()

    def own_step(xe, _):
        sums = [None] * 3
        for xr in range(3):
            for m in range(3):
                bl = BL[3 + 3 * xe + xr, m, 8:24, :]
                for r in range(3):
                    rho, slope = level(bl, thresholds[r])
                    square = rho * rho
                    T[r, 3 + 3 * xe + xr, m, 0:16] = square * slope
                    cube = square * rho
                    sums[r] = cube if sums[r] is None else sums[r] + cube
        for r in range(3):
            S3[r, xe] = sums[r]
        return 0

    lax.fori_loop(0, 4, own_step, 0)
    moduli = times(S3[...].reshape(192, DEEP), GATHER[...]) * ((1.0 - stiff_floor) / 27.0) + stiff_floor
    MOD[...] = moduli.reshape(12, 16, 128)
    row8 = lax.broadcasted_iota(jnp.int32, (8, 128), 0)
    tile = zero((8, 128))
    for r in range(3):
        part = zero((8, 128))
        for l in range(4):
            for t in range(2):
                part = part + MOD[4 * r + l, 8 * t : 8 * t + 8] * EN[r, 1 + l, 8 + 8 * t : 16 + 8 * t]
        tile = jnp.where(row8 == r, jnp.sum(part, axis=0, keepdims=True), tile)
    AR1[i1] = tile

    def exchange(buf, ss, rs, me, count, peer):
        out = []
        for k in range(1, count):
            j, device = peer(k)
            send = pltpu.make_async_remote_copy(
                src_ref=buf.at[me], dst_ref=buf.at[me], send_sem=ss.at[k], recv_sem=rs.at[me],
                device_id=device, device_id_type=MESH,
            )
            recv = pltpu.make_async_remote_copy(
                src_ref=buf.at[j], dst_ref=buf.at[j], send_sem=ss.at[k], recv_sem=rs.at[j],
                device_id=device, device_id_type=MESH,
            )
            out.append((send, recv))
        return out

    phase1 = exchange(AR1, a1s, a1r, i1, count1, peer1)
    phase2 = exchange(AR2, a2s, a2r, i2, count2, peer2)
    for send, _ in phase1:
        send.start()

    def force_step(i, _):
        r, l = i // 4, i % 4
        for t in range(2):
            mod = MOD[i, 8 * t : 8 * t + 8]
            for comp in range(3):
                k = r * 3 + comp

                def mode(p, q, s):
                    row = 3 * (4 * p + 2 * q + s) + comp
                    return V[i, row, 8 * t : 8 * t + 8] * mod if modes[row] else None

                def minus(a, b):
                    return b * -1.0 if a is None else a - b

                def plus(a, b):
                    return b if a is None else a + b

                zz = {}
                for p in range(2):
                    for q in range(2):
                        v0, v1 = mode(p, q, 0), mode(p, q, 1)
                        high = jnp.where(lane > 0, pltpu.roll(plus(v0, v1), 1, axis=1), 0.0)
                        zz[p, q] = minus(v0, v1) + high
                for c in range(2):
                    y0, y1 = [
                        (zz[p, 1] + zz[p, 0]) if c else (zz[p, 0] - zz[p, 1]) for p in range(2)
                    ]
                    rows = pl.ds(8 * t + c, 8)
                    FS[k, l, rows, :] = FS[k, l, rows, :] + (y0 - y1)
                    FS[k, l + 1, rows, :] = FS[k, l + 1, rows, :] + (y0 + y1)
        return 0

    lax.fori_loop(0, 12, force_step, 0)
    for message in forces:
        message.start()

    for _, recv in phase1:
        recv.wait_recv()
    total1 = AR1[0]
    for j in range(1, count1):
        total1 = total1 + AR1[j]
    AR2[i2] = total1
    for send, _ in phase2:
        send.start()

    for message in energies:
        message.wait_recv()
    for r in range(3):
        for l in range(6):
            edge = jnp.where(row8 == 7, EN[r, l, 0:8], EN[r, l, 24:32])
            block = jnp.concatenate([EN[r, l, 8:24], edge], axis=0)
            ESP[r, l] = times(block, SPREAD[...])

    def own_terms(xe, _):
        for xr in range(3):
            x = 3 + 3 * xe + xr
            for m in range(3):
                scale = WT[m, 0:16] * RX[x]
                for r in range(3):
                    T[r, x, m, 0:16] = T[r, x, m, 0:16] * (ESP[r, 1 + xe, 0:16] * scale)
        return 0

    lax.fori_loop(0, 4, own_terms, 0)
    for message in fields:
        message.wait_recv()

    def terms(x, xe, m, bl, rows):
        scale = WT[m, rows] * RX[x]
        for r in range(3):
            rho, slope = level(bl, thresholds[r])
            T[r, x, m, rows] = rho * rho * slope * (ESP[r, xe, rows] * scale)

    for l in (0, 5):

        def row_terms(xr, _, l=l):
            for m in range(3):
                terms(3 * l + xr, l, m, BL[3 * l + xr, m, 8:24, :], slice(0, 16))
            return 0

        lax.fori_loop(0, 3, row_terms, 0)

    def column_terms(x, _):
        for m in range(3):
            edge = lax.broadcasted_iota(jnp.int32, (8, DEEP), 0) == 7
            bl = jnp.where(edge, BL[x, m, 0:8, :], BL[x, m, 24:32, :])
            terms(x, x // 3, m, bl, slice(16, 24))
        return 0

    lax.fori_loop(0, 18, column_terms, 0)

    for message in forces:
        message.wait_recv()
    loads[3].wait()
    for k in range(9):
        FS[k, 0, 0:16] = FS[k, 0, 0:16] + FXR[k]
        FS[k, 0:4, 0:8] = FS[k, 0:4, 0:8] + jnp.where(
            lax.broadcasted_iota(jnp.int32, (4, 8, 128), 1) == 0, FYR[k], 0.0
        )
        FS[k, 0, 0:8] = FS[k, 0, 0:8] + jnp.where(row8 == 0, FDR[k], 0.0)
    free = 1.0 - SU[...].astype(F32)
    load = LO[...].astype(F32) * (-load_force)
    for k in range(9):
        stiff = FS[k, 0:4, 0:16]
        RES[k] = ((load - stiff) if k % 3 == 2 else (0.0 - stiff)) * free
    res_copy = pltpu.make_async_copy(RES, res_out, osem.at[12])
    res_copy.start()

    for _, recv in phase2:
        recv.wait_recv()
    total2 = AR2[0]
    for j in range(1, count2):
        total2 = total2 + AR2[j]
    scales = []
    for r in range(3):
        comp_out[r] = jnp.sum(total2[r : r + 1])
        whole = jnp.sum(total2[r : r + 1], axis=1, keepdims=True)
        scales.append(jnp.broadcast_to(-slope_scale(thresholds[r]) / whole, (8, 128)))

    def x_back(m, _):
        for t in range(3):
            for c in range(3):
                lanes = slice(128 * c, 128 * c + 128)
                rows = slice(8 * t, 8 * t + 8)
                values = []
                for x in range(18):
                    v = T[0, x, m, rows, lanes] * scales[0]
                    v = v + T[1, x, m, rows, lanes] * scales[1]
                    values.append(v + T[2, x, m, rows, lanes] * scales[2])
                out = tent(values)
                for x in range(ROWS):
                    GX[x, m, c, 8 + 8 * t : 16 + 8 * t, :] = out[x]
                    if t == 2:
                        GX[x, m, c, 0:8, :] = out[x]
        return 0

    lax.fori_loop(0, 3, x_back, 0)

    def y_back(x, _):
        parts = {}
        for t in range(2):
            for c in range(3):
                out = tent([GX[x, k % 3, c, pl.ds(8 + 8 * t + k // 3, 8), :] for k in range(-3, 6)])
                for m in range(3):
                    parts[m, t, c] = out[m]
        keep(x, parts)
        return 0

    lax.fori_loop(0, ROWS, y_back, 0)

    def out_copy(g, c):
        return pltpu.make_async_copy(
            OUT.at[pl.ds(3 * g, 3), c],
            sens_out.at[pl.ds(3 * g, 3), :, 128 * c : 128 * c + 128],
            osem.at[3 * g + c],
        )

    def z_back(g, _):
        z = banded(g)
        for xr in range(3):
            for m in range(3):
                for t in range(2):
                    for c in range(3):
                        at = 16 * (3 * xr + m) + 8 * t
                        OUT[3 * g + xr, c, pl.ds(24 * t + m, 8, stride=3), :] = z[
                            at : at + 8, 128 * c : 128 * c + 128
                        ]
        for c in range(3):
            out_copy(g, c).start()
        return 0

    lax.fori_loop(0, 4, z_back, 0)

    for message in designs + moves + fields + energies + forces:
        message.wait_send()
    for send, _ in phase1 + phase2:
        send.wait_send()
    res_copy.wait()
    for g in range(4):
        for c in range(3):
            out_copy(g, c).wait()


def solution(mesh):
    wide, narrow = mesh.shape["wide"], mesh.shape["narrow"]

    def local(design, passive, displacement, support, loading):
        sems = pltpu.SemaphoreType.DMA
        residual, compliance, sensitivity = pl.pallas_call(
            functools.partial(kernel, wide, narrow),
            out_shape=(
                jax.ShapeDtypeStruct((9, EX, EY, EZ), F32),
                jax.ShapeDtypeStruct((3,), F32),
                jax.ShapeDtypeStruct((ROWS, COLS, DEEP), F32),
            ),
            in_specs=[pl.BlockSpec(memory_space=pl.ANY)] * 5,
            out_specs=(
                pl.BlockSpec(memory_space=pl.ANY),
                pl.BlockSpec(memory_space=pltpu.SMEM),
                pl.BlockSpec(memory_space=pl.ANY),
            ),
            scratch_shapes=[
                pltpu.VMEM((18, 64, DEEP), F32),
                pltpu.VMEM((ROWS, 3, 64, 128), F32),
                pltpu.VMEM((ROWS, COLS, DEEP), BF16),
                pltpu.VMEM((ROWS, COLS, DEEP), BF16),
                pltpu.VMEM((ROWS, 3, COLS, 128), jnp.int32),
                pltpu.VMEM((18, 3, 32, DEEP), F32),
                pltpu.VMEM((3, 18, 3, 24, DEEP), F32),
                pltpu.VMEM((3, 6, 32, 128), F32),
                pltpu.VMEM((3, 6, 24, DEEP), F32),
                pltpu.VMEM((ROWS, 3, 3, 32, 128), F32),
                pltpu.VMEM((ROWS, 3, COLS, 128), F32),
                pltpu.VMEM((12, 24, 16, 128), F32),
                pltpu.VMEM((9, 5, 24, 128), F32),
                pltpu.VMEM((9, 5, 24, 128), F32),
                pltpu.VMEM((9, 16, 128), F32),
                pltpu.VMEM((9, 4, 8, 128), F32),
                pltpu.VMEM((9, 8, 128), F32),
                pltpu.VMEM((9, EX, EY, EZ), F32),
                pltpu.VMEM((EX, EY, EZ), jnp.int32),
                pltpu.VMEM((EX, EY, EZ), jnp.int32),
                pltpu.VMEM((9, EX, EY, EZ), F32),
                pltpu.VMEM((12, 16, 128), F32),
                pltpu.VMEM((3, 4, 16, DEEP), F32),
                pltpu.VMEM((3, 24, DEEP), F32),
                pltpu.VMEM((DEEP, DEEP), BF16),
                pltpu.VMEM((EZ, DEEP), BF16),
                pltpu.VMEM((DEEP, EZ), BF16),
                pltpu.VMEM((wide // 2, 8, 128), F32),
                pltpu.VMEM((2 * narrow, 8, 128), F32),
                pltpu.SMEM((18,), F32),
                sems((7,)), sems((13,)),
                sems((8,)), sems((8,)), sems((3,)), sems((3,)), sems((8,)), sems((8,)),
                sems((8,)), sems((8,)), sems((3,)), sems((3,)),
                sems((wide // 2,)), sems((wide // 2,)), sems((2 * narrow,)), sems((2 * narrow,)),
            ],
            compiler_params=pltpu.CompilerParams(
                collective_id=0, has_side_effects=True, vmem_limit_bytes=56 << 20
            ),
        )(design, passive, displacement.reshape(9, EX, EY, EZ), support, loading)
        return residual.reshape(3, 3, EX, EY, EZ), compliance, sensitivity

    in_specs = (
        P("wide", "narrow", None),
        P("wide", "narrow", None),
        P(None, None, "wide", "narrow", None),
        P("wide", "narrow", None),
        P("wide", "narrow", None),
    )
    out_specs = (P(None, None, "wide", "narrow", None), P(), P("wide", "narrow", None))
    return jax.shard_map(local, mesh=mesh, in_specs=in_specs, out_specs=out_specs, check_vma=False)
```

```python
import functools
import math

import jax
import jax.numpy as jnp
import numpy as np
from jax import lax
from jax.experimental import pallas as pl
from jax.experimental.pallas import tpu as pltpu
from jax.sharding import PartitionSpec as P

sharpness = 8.0
thresholds = (0.7, 0.5, 0.3)
stiff_floor = 0.001
load_force = 4.0
poisson = 0.3

F32, BF16 = jnp.float32, jnp.bfloat16
MESH = pl.DeviceIdType.MESH
ROWS, COLS, DEEP = 12, 48, 384
EX, EY, EZ = 4, 16, 128
DIRS = ((1, 0), (-1, 0), (0, 1), (0, -1), (1, 1), (1, -1), (-1, 1), (-1, -1))


def element_matrix():
    inv_root = 1.0 / np.sqrt(3.0)
    elastic = np.full((3, 3), poisson) + np.eye(3) * (1.0 - 2.0 * poisson)
    elastic = np.block(
        [[elastic, np.zeros((3, 3))], [np.zeros((3, 3)), np.eye(3) * (0.5 - poisson)]]
    ) / ((1.0 + poisson) * (1.0 - 2.0 * poisson))
    signs = [(2 * (c // 4) - 1, 2 * (c // 2 % 2) - 1, 2 * (c % 2) - 1) for c in range(8)]
    stiffness = np.zeros((24, 24))
    for ga in (-inv_root, inv_root):
        for gb in (-inv_root, inv_root):
            for gc in (-inv_root, inv_root):
                point = (ga, gb, gc)
                strain = np.zeros((6, 24))
                for c in range(8):
                    d = []
                    for along in range(3):
                        s = signs[c][along] / 4.0
                        for other in range(3):
                            if other != along:
                                s = s * (1.0 + signs[c][other] * point[other])
                        d.append(s)
                    col = 3 * c
                    strain[0, col], strain[1, col + 1], strain[2, col + 2] = d
                    strain[3, col], strain[3, col + 1] = d[1], d[0]
                    strain[4, col + 1], strain[4, col + 2] = d[2], d[1]
                    strain[5, col], strain[5, col + 2] = d[2], d[0]
                stiffness = stiffness + strain.T @ elastic @ strain * 0.125
    return stiffness


def mode_matrix():
    h = np.zeros((8, 8))
    for mode in range(8):
        for c in range(8):
            v = 1.0
            for bit in (4, 2, 1):
                if mode & bit:
                    v *= 1.0 if c & bit else -1.0
            h[mode, c] = v
    full = np.kron(h, np.eye(3))
    k = full @ element_matrix() @ full.T / 64.0
    return [
        [(j, float(k[i, j])) for j in range(24) if abs(k[i, j]) > 1e-9] for i in range(24)
    ]


def tent(values):
    p = [a + b for a, b in zip(values, values[1:])]
    q = [a + b for a, b in zip(p, p[2:])]
    r = [a + b for a, b in zip(q, q[1:])]
    return [a + b for a, b in zip(r, r[2:])]


def inverse_weight(place, extent):
    edge = jnp.minimum(place, extent - 1 - place)
    return jnp.where(
        edge >= 3, 1.0 / 16.0, jnp.where(edge == 2, 1.0 / 15.0, jnp.where(edge == 1, 1.0 / 13.0, 0.1))
    ).astype(F32)


def split(value):
    high = value.astype(BF16)
    return high, (value - high.astype(F32)).astype(BF16)


def times(value, matrix):
    high, low = split(value)
    return jnp.dot(high, matrix, preferred_element_type=F32) + jnp.dot(
        low, matrix, preferred_element_type=F32
    )


def level(bl, eta):
    low = math.tanh(sharpness * eta)
    den = low + math.tanh(sharpness * (1.0 - eta))
    t = jnp.tanh(bl * sharpness - sharpness * eta)
    rho = t * (1.0 / den) + low / den
    return rho, 1.0 - t * t


def slope_scale(eta):
    den = math.tanh(sharpness * eta) + math.tanh(sharpness * (1.0 - eta))
    return sharpness / den * 3.0 * (1.0 - stiff_floor) / 27.0


def banded(high, low, band, g):
    h, l = (part[pl.ds(3 * g, 3)].reshape(144, DEEP) for part in (high, low))
    b = band[...]
    first, second = (
        jnp.dot(h[:, k : k + 256], b, preferred_element_type=F32)
        + jnp.dot(l[:, k : k + 256], b, preferred_element_type=F32)
        for k in (0, 128)
    )
    lane = lax.broadcasted_iota(jnp.int32, (144, 128), 1)
    middle = jnp.where(lane < 64, first[:, 128:256], second[:, 0:128])
    return first[:, 0:128], middle, second[:, 128:256]


def kernel(
    wide, narrow,
    design, passive, disp, support, loading,
    AH, AL, RES, COMP, BAND,
    D, XF, PA, SW, BL, T, EN, ESP, GX, V, M, FS, FXR, FYR, FDR, U, SU, LO, MOD, S3,
    WT, SPREAD, GATHER, AR1, AR2, RX,
    lsem, dss, drs, mss, mrs, bss, brs, ess, ers, fss, frs, sss, srs, a1s, a1r, a2s, a2r,
):
    w = lax.axis_index("wide")
    n = lax.axis_index("narrow")
    zc, xl, core = w // 4, (w // 2) % 2, w % 2
    count1, count2 = wide // 2, 2 * narrow
    i1 = zc * 2 + core
    i2 = xl * narrow + n

    def within(dw, dn):
        ok = None
        for step, at, count in ((dw, w, wide), (dn, n, narrow)):
            if step:
                cond = at < count - 1 if step > 0 else at > 0
                ok = cond if ok is None else ok & cond
        return ok

    def peer1(k):
        j = (i1 + k) % count1
        return j, ((j // 2) * 4 + xl * 2 + j % 2, n)

    def peer2(k):
        j = (i2 + k) % count2
        return j, (zc * 4 + (j // narrow) * 2 + core, j % narrow)

    def around(dw, dn):
        return ((w + dw + wide) % wide, (n + dn + narrow) % narrow)

    barrier = pltpu.get_barrier_semaphore()
    total = count1 - 1 + count2 - 1
    for dw, dn in DIRS:
        total = total + within(dw, dn).astype(jnp.int32)

        @pl.when(within(dw, dn))
        def _(dw=dw, dn=dn):
            pl.semaphore_signal(barrier, 1, device_id=around(dw, dn), device_id_type=MESH)

    for k in range(1, count1):
        pl.semaphore_signal(barrier, 1, device_id=peer1(k)[1], device_id_type=MESH)
    for k in range(1, count2):
        pl.semaphore_signal(barrier, 1, device_id=peer2(k)[1], device_id_type=MESH)

    loads = [
        pltpu.make_async_copy(disp, U.at[:, 0:4, 0:16, :], lsem.at[0]),
        pltpu.make_async_copy(support, SU.at[0:4, 0:16, :], lsem.at[1]),
        pltpu.make_async_copy(design, D.at[3:15, 8:56, :], lsem.at[2]),
        pltpu.make_async_copy(loading, LO, lsem.at[3]),
    ] + [
        pltpu.make_async_copy(passive.at[:, :, 128 * c : 128 * c + 128], PA.at[:, c], lsem.at[4 + c])
        for c in range(3)
    ]
    for copy in loads:
        copy.start()

    class Message:
        def __init__(self, src, dst, ss, rs, dw, dn):
            self.to, self.origin = within(dw, dn), within(-dw, -dn)
            self.copy = pltpu.make_async_remote_copy(
                src_ref=src, dst_ref=dst, send_sem=ss, recv_sem=rs,
                device_id=around(dw, dn), device_id_type=MESH,
            )

        def start(self):
            pl.when(self.to)(self.copy.start)

        def wait_send(self):
            pl.when(self.to)(self.copy.wait_send)

        def wait_recv(self):
            pl.when(self.origin)(self.copy.wait_recv)

    def x_part(dw, low, high, depth):
        if dw == 0:
            return pl.ds(low, high - low), pl.ds(low, high - low)
        if dw > 0:
            return pl.ds(high - depth, depth), pl.ds(low - depth, depth)
        return pl.ds(low, depth), pl.ds(high, depth)

    designs, fields, energies = [], [], []
    for d, (dw, dn) in enumerate(DIRS):
        sx, tx = x_part(dw, 0, ROWS, 3)
        tx = pl.ds(tx.start + 3, tx.size)
        sy, ty = x_part(dn, 0, COLS, 3)
        ty = pl.ds(ty.start + 8, ty.size)
        designs.append(
            Message(design.at[sx, sy, :], D.at[tx, ty, :], dss.at[d], drs.at[d], dw, dn)
        )
        sx, tx = x_part(dw, 3, 15, 3)
        sy, ty = x_part(dn, 8, 24, 1)
        fields.append(
            Message(BL.at[sx, :, sy, :], BL.at[tx, :, ty, :], bss.at[d], brs.at[d], dw, dn)
        )
        sx, tx = x_part(dw, 1, 5, 1)
        energies.append(
            Message(EN.at[:, sx, sy, :], EN.at[:, tx, ty, :], ess.at[d], ers.at[d], dw, dn)
        )
    moves, holds, forces = [], [], []
    for d, (dw, dn) in enumerate(((-1, 0), (0, -1), (-1, -1))):
        sx, tx = x_part(dw, 0, 4, 1)
        sy, ty = x_part(dn, 0, 16, 1)
        moves.append(
            Message(disp.at[:, sx, sy, :], U.at[:, tx, ty, :], mss.at[d], mrs.at[d], dw, dn)
        )
        holds.append(
            Message(support.at[sx, sy, :], SU.at[tx, ty, :], sss.at[d], srs.at[d], dw, dn)
        )
    forces.append(Message(FS.at[:, 4, 0:16, :], FXR, fss.at[0], frs.at[0], 1, 0))
    forces.append(
        Message(FS.at[:, 0:4, 16:17, :], FYR.at[:, :, 0:1, :], fss.at[1], frs.at[1], 0, 1)
    )
    forces.append(Message(FS.at[:, 4, 16:17, :], FDR.at[:, 0:1, :], fss.at[2], frs.at[2], 1, 1))

    pl.semaphore_wait(barrier, total)
    for message in moves + holds + designs:
        message.start()

    def near(shape):
        return lax.broadcasted_iota(jnp.int32, shape, 0), lax.broadcasted_iota(jnp.int32, shape, 1)

    a, b = near((256, 256))
    BAND[...] = jnp.maximum(4 - jnp.abs(a - b), 0).astype(F32).astype(BF16)
    a, b = near((EZ, DEEP))
    gap = b - 3 * a
    SPREAD[...] = jnp.where((gap >= 0) & (gap < 3), 1.0, 0.0).astype(BF16)
    a, b = near((DEEP, EZ))
    gap = a - 3 * b
    GATHER[...] = jnp.where((gap >= 0) & (gap < 3), 1.0, 0.0).astype(BF16)
    a, b = near((24, DEEP))
    a = jnp.where(a == 23, -1, a)
    deep = inverse_weight(b, DEEP)
    for m in range(3):
        WT[m] = inverse_weight(n * COLS + 3 * a + m, narrow * COLS) * deep
    for x in range(18):
        RX[x] = inverse_weight(w * ROWS + x - 3, wide * ROWS)

    zero = functools.partial(jnp.zeros, dtype=F32)

    @pl.when(w == 0)
    def _():
        D[0:3] = zero((3, 64, DEEP))
        BL[0:3] = zero((3, 3, 32, DEEP))
        EN[:, 0] = zero((3, 32, 128))
        FXR[...] = zero((9, 16, 128))

    @pl.when(w == wide - 1)
    def _():
        D[15:18] = zero((3, 64, DEEP))
        BL[15:18] = zero((3, 3, 32, DEEP))
        EN[:, 5] = zero((3, 32, 128))
        U[:, 4] = zero((9, 24, 128))

    @pl.when(n == 0)
    def _():
        D[:, 0:8] = zero((18, 8, DEEP))
        BL[:, :, 0:8] = zero((18, 3, 8, DEEP))
        EN[:, :, 0:8] = zero((3, 6, 8, 128))
        FYR[...] = zero((9, 4, 8, 128))

    @pl.when(n == narrow - 1)
    def _():
        D[:, 56:64] = zero((18, 8, DEEP))
        BL[:, :, 24:32] = zero((18, 3, 8, DEEP))
        EN[:, :, 24:32] = zero((3, 6, 8, 128))
        U[:, :, 16:24] = zero((9, 5, 8, 128))

    @pl.when((n == 0) | (w == 0))
    def _():
        FDR[...] = zero((9, 8, 128))

    FS[...] = zero((9, 5, 24, 128))

    for copy in loads[4:]:
        copy.wait()

    def solid_step(x, _):
        for m in range(3):
            for t in range(2):
                for c in range(3):
                    void = PA[x, c, pl.ds(24 * t + m, 8, stride=3), :]
                    rows, lanes = slice(8 * t, 8 * t + 8), slice(128 * c, 128 * c + 128)
                    SW[x, m, rows, lanes] = (1.0 - void.astype(F32)) * (WT[m, rows, lanes] * RX[x + 3])
        return 0

    lax.fori_loop(0, ROWS, solid_step, 0)

    loads[0].wait()
    loads[1].wait()
    for message in moves + holds:
        message.wait_recv()
    for l in range(5):
        free = 1.0 - SU[l].astype(F32)
        for k in range(9):
            M[k, l] = U[k, l] * free

    modes = mode_matrix()
    lane = lax.broadcasted_iota(jnp.int32, (8, 128), 1)

    def energy_step(i, _):
        r, l = i // 4, i % 4
        for t in range(2):
            hat = [None] * 24
            for comp in range(3):
                k = r * 3 + comp
                corner = {}
                for p in range(2):
                    for q in range(2):
                        v = M[k, l + p, pl.ds(8 * t + q, 8), :]
                        v1 = jnp.where(lane < 127, pltpu.roll(v, 127, axis=1), 0.0)
                        corner[p, q, 0], corner[p, q, 1] = v + v1, v1 - v
                for s in range(2):
                    y = {}
                    for p in range(2):
                        y[p, 0] = corner[p, 0, s] + corner[p, 1, s]
                        y[p, 1] = corner[p, 1, s] - corner[p, 0, s]
                    for q in range(2):
                        hat[3 * (2 * q + s) + comp] = y[0, q] + y[1, q]
                        hat[3 * (4 + 2 * q + s) + comp] = y[1, q] - y[0, q]
            energy = None
            for row in range(24):
                if not modes[row]:
                    continue
                value = None
                for j, factor in modes[row]:
                    term = hat[j] * factor
                    value = term if value is None else value + term
                V[i, row, 8 * t : 8 * t + 8] = value
                term = value * hat[row]
                energy = term if energy is None else energy + term
            EN[r, 1 + l, 8 + 8 * t : 16 + 8 * t] = energy
        return 0

    lax.fori_loop(0, 12, energy_step, 0)
    for message in energies:
        message.start()

    loads[2].wait()
    for message in designs:
        message.wait_recv()

    def x_step(t, _):
        rows = pl.ds(pl.multiple_of(8 * t, 8), 8)
        for c in range(3):
            out = tent([D[x, rows, 128 * c : 128 * c + 128] for x in range(18)])
            for x in range(ROWS):
                XF[x, c, rows, :] = out[x]
        return 0

    lax.fori_loop(0, 8, x_step, 0)

    def keep(x, parts):
        for m in range(3):
            block = jnp.concatenate(
                [jnp.concatenate([parts[m, t, c] for t in range(2)], axis=0) for c in range(3)], axis=1
            )
            high, low = split(block)
            AH[x, 16 * m : 16 * m + 16, :] = high
            AL[x, 16 * m : 16 * m + 16, :] = low

    def y_step(x, _):
        parts = {}
        for t in range(2):
            for c in range(3):
                out = tent([XF[x, c, pl.ds(8 + 24 * t + k, 8, stride=3), :] for k in range(-3, 6)])
                for m in range(3):
                    parts[m, t, c] = out[m]
        keep(x, parts)
        return 0

    lax.fori_loop(0, ROWS, y_step, 0)

    def z_step(g, _):
        z = banded(AH, AL, BAND, g)
        for xr in range(3):
            x = 3 * g + xr
            for m in range(3):
                at = 16 * (3 * xr + m)
                for c in range(3):
                    lanes = slice(128 * c, 128 * c + 128)
                    BL[x + 3, m, 8:24, lanes] = z[c][at : at + 16] * SW[x, m, :, lanes]
        return 0

    lax.fori_loop(0, 4, z_step, 0)
    for message in fields[2:]:
        message.start()

    def own_step(xe, _):
        sums = [None] * 3
        for xr in range(3):
            for m in range(3):
                bl = BL[3 + 3 * xe + xr, m, 8:24, :]
                for r in range(3):
                    rho, slope = level(bl, thresholds[r])
                    square = rho * rho
                    T[r, 3 + 3 * xe + xr, m, 0:16] = square * slope
                    cube = square * rho
                    sums[r] = cube if sums[r] is None else sums[r] + cube
        for r in range(3):
            S3[r, xe] = sums[r]
        return 0

    lax.fori_loop(0, 4, own_step, 0)
    moduli = times(S3[...].reshape(192, DEEP), GATHER[...]) * ((1.0 - stiff_floor) / 27.0) + stiff_floor
    MOD[...] = moduli.reshape(12, 16, 128)
    row8 = lax.broadcasted_iota(jnp.int32, (8, 128), 0)
    tile = zero((8, 128))
    for r in range(3):
        part = zero((8, 128))
        for l in range(4):
            for t in range(2):
                part = part + MOD[4 * r + l, 8 * t : 8 * t + 8] * EN[r, 1 + l, 8 + 8 * t : 16 + 8 * t]
        tile = jnp.where(row8 == r, jnp.sum(part, axis=0, keepdims=True), tile)
    AR1[i1] = tile

    def exchange(buf, ss, rs, me, count, peer):
        out = []
        for k in range(1, count):
            j, device = peer(k)
            send = pltpu.make_async_remote_copy(
                src_ref=buf.at[me], dst_ref=buf.at[me], send_sem=ss.at[k], recv_sem=rs.at[me],
                device_id=device, device_id_type=MESH,
            )
            recv = pltpu.make_async_remote_copy(
                src_ref=buf.at[j], dst_ref=buf.at[j], send_sem=ss.at[k], recv_sem=rs.at[j],
                device_id=device, device_id_type=MESH,
            )
            out.append((send, recv))
        return out

    phase1 = exchange(AR1, a1s, a1r, i1, count1, peer1)
    phase2 = exchange(AR2, a2s, a2r, i2, count2, peer2)
    for send, _ in phase1:
        send.start()
    for message in fields[:2]:
        message.start()

    def force_step(i, _):
        r, l = i // 4, i % 4
        for t in range(2):
            mod = MOD[i, 8 * t : 8 * t + 8]
            for comp in range(3):
                k = r * 3 + comp

                def mode(p, q, s):
                    row = 3 * (4 * p + 2 * q + s) + comp
                    return V[i, row, 8 * t : 8 * t + 8] * mod if modes[row] else None

                def minus(a, b):
                    return b * -1.0 if a is None else a - b

                def plus(a, b):
                    return b if a is None else a + b

                zz = {}
                for p in range(2):
                    for q in range(2):
                        v0, v1 = mode(p, q, 0), mode(p, q, 1)
                        high = jnp.where(lane > 0, pltpu.roll(plus(v0, v1), 1, axis=1), 0.0)
                        zz[p, q] = minus(v0, v1) + high
                for c in range(2):
                    y0, y1 = [
                        (zz[p, 1] + zz[p, 0]) if c else (zz[p, 0] - zz[p, 1]) for p in range(2)
                    ]
                    rows = pl.ds(8 * t + c, 8)
                    FS[k, l, rows, :] = FS[k, l, rows, :] + (y0 - y1)
                    FS[k, l + 1, rows, :] = FS[k, l + 1, rows, :] + (y0 + y1)
        return 0

    lax.fori_loop(0, 12, force_step, 0)
    for message in forces:
        message.start()

    for _, recv in phase1:
        recv.wait_recv()
    total1 = AR1[0]
    for j in range(1, count1):
        total1 = total1 + AR1[j]
    AR2[i2] = total1
    for send, _ in phase2:
        send.start()

    for message in energies:
        message.wait_recv()
    for r in range(3):
        blocks = []
        for l in range(6):
            blocks.append(EN[r, l, 8:24])
            blocks.append(jnp.where(row8 == 7, EN[r, l, 0:8], EN[r, l, 24:32]))
        ESP[r] = times(jnp.concatenate(blocks, axis=0), SPREAD[...]).reshape(6, 24, DEEP)

    def own_terms(xe, _):
        for xr in range(3):
            x = 3 + 3 * xe + xr
            for m in range(3):
                scale = WT[m, 0:16] * RX[x]
                for r in range(3):
                    T[r, x, m, 0:16] = T[r, x, m, 0:16] * (ESP[r, 1 + xe, 0:16] * scale)
        return 0

    lax.fori_loop(0, 4, own_terms, 0)
    for message in fields[2:4]:
        message.wait_recv()

    def terms(x, xe, m, bl, rows):
        scale = WT[m, rows] * RX[x]
        for r in range(3):
            rho, slope = level(bl, thresholds[r])
            T[r, x, m, rows] = rho * rho * slope * (ESP[r, xe, rows] * scale)

    def column_terms(x, _):
        for m in range(3):
            edge = lax.broadcasted_iota(jnp.int32, (8, DEEP), 0) == 7
            bl = jnp.where(edge, BL[x, m, 0:8, :], BL[x, m, 24:32, :])
            terms(x, x // 3, m, bl, slice(16, 24))
        return 0

    lax.fori_loop(3, 15, column_terms, 0)
    for message in fields[4:]:
        message.wait_recv()
    for l in (0, 5):
        lax.fori_loop(3 * l, 3 * l + 3, column_terms, 0)
    for message in fields[:2]:
        message.wait_recv()
    for l in (0, 5):

        def row_terms(xr, _, l=l):
            for m in range(3):
                terms(3 * l + xr, l, m, BL[3 * l + xr, m, 8:24, :], slice(0, 16))
            return 0

        lax.fori_loop(0, 3, row_terms, 0)

    for message in forces:
        message.wait_recv()
    loads[3].wait()
    for k in range(9):
        FS[k, 0, 0:16] = FS[k, 0, 0:16] + FXR[k]
        FS[k, 0:4, 0:8] = FS[k, 0:4, 0:8] + jnp.where(
            lax.broadcasted_iota(jnp.int32, (4, 8, 128), 1) == 0, FYR[k], 0.0
        )
        FS[k, 0, 0:8] = FS[k, 0, 0:8] + jnp.where(row8 == 0, FDR[k], 0.0)
    free = 1.0 - SU[0:4, 0:16].astype(F32)
    load = LO[...].astype(F32) * (-load_force)
    for k in range(9):
        stiff = FS[k, 0:4, 0:16]
        RES[k] = ((load - stiff) if k % 3 == 2 else (0.0 - stiff)) * free

    for _, recv in phase2:
        recv.wait_recv()
    total2 = AR2[0]
    for j in range(1, count2):
        total2 = total2 + AR2[j]
    COMP[...] = total2
    scales = []
    for r in range(3):
        whole = jnp.sum(total2[r : r + 1], axis=1, keepdims=True)
        scales.append(jnp.broadcast_to(-slope_scale(thresholds[r]) / whole, (8, 128)))

    def x_back(m, _):
        for t in range(3):
            for c in range(3):
                lanes = slice(128 * c, 128 * c + 128)
                rows = slice(8 * t, 8 * t + 8)
                values = []
                for x in range(18):
                    v = T[0, x, m, rows, lanes] * scales[0]
                    v = v + T[1, x, m, rows, lanes] * scales[1]
                    values.append(v + T[2, x, m, rows, lanes] * scales[2])
                out = tent(values)
                for x in range(ROWS):
                    GX[x, m, c, 8 + 8 * t : 16 + 8 * t, :] = out[x]
                    if t == 2:
                        GX[x, m, c, 0:8, :] = out[x]
        return 0

    lax.fori_loop(0, 3, x_back, 0)

    def y_back(x, _):
        parts = {}
        for t in range(2):
            for c in range(3):
                out = tent([GX[x, k % 3, c, pl.ds(8 + 8 * t + k // 3, 8), :] for k in range(-3, 6)])
                for m in range(3):
                    parts[m, t, c] = out[m]
        keep(x, parts)
        return 0

    lax.fori_loop(0, ROWS, y_back, 0)

    for message in moves + holds + designs + fields + energies + forces:
        message.wait_send()
    for send, _ in phase1 + phase2:
        send.wait_send()


def finish(AH, AL, RES, COMP, BAND, res_out, comp_out, sens_out, OUT, osem):
    res_copy = pltpu.make_async_copy(RES, res_out, osem.at[12])
    res_copy.start()
    for r in range(3):
        comp_out[r] = jnp.sum(COMP[r : r + 1])

    def out_copy(g, c):
        return pltpu.make_async_copy(
            OUT.at[pl.ds(3 * g, 3), c],
            sens_out.at[pl.ds(3 * g, 3), :, 128 * c : 128 * c + 128],
            osem.at[3 * g + c],
        )

    def z_back(g, _):
        z = banded(AH, AL, BAND, g)
        for xr in range(3):
            for m in range(3):
                for t in range(2):
                    for c in range(3):
                        at = 16 * (3 * xr + m) + 8 * t
                        OUT[3 * g + xr, c, pl.ds(24 * t + m, 8, stride=3), :] = z[c][at : at + 8]
        for c in range(3):
            out_copy(g, c).start()
        return 0

    lax.fori_loop(0, 4, z_back, 0)
    res_copy.wait()
    for g in range(4):
        for c in range(3):
            out_copy(g, c).wait()


def solution(mesh):
    wide, narrow = mesh.shape["wide"], mesh.shape["narrow"]

    def local(design, passive, displacement, support, loading):
        sems = pltpu.SemaphoreType.DMA
        vmem = pl.BlockSpec(memory_space=pltpu.VMEM)
        hbm = pl.BlockSpec(memory_space=pltpu.MemorySpace.HBM)
        passed = (
            jax.ShapeDtypeStruct((ROWS, COLS, DEEP), BF16),
            jax.ShapeDtypeStruct((ROWS, COLS, DEEP), BF16),
            jax.ShapeDtypeStruct((9, EX, EY, EZ), F32),
            jax.ShapeDtypeStruct((8, 128), F32),
            jax.ShapeDtypeStruct((256, 256), BF16),
        )
        parts = pl.pallas_call(
            functools.partial(kernel, wide, narrow),
            out_shape=passed,
            in_specs=[hbm] * 5,
            out_specs=(vmem,) * 5,
            scratch_shapes=[
                pltpu.VMEM((18, 64, DEEP), F32),
                pltpu.VMEM((ROWS, 3, 64, 128), F32),
                pltpu.VMEM((ROWS, 3, COLS, 128), jnp.int32),
                pltpu.VMEM((ROWS, 3, 16, DEEP), F32),
                pltpu.VMEM((18, 3, 32, DEEP), F32),
                pltpu.VMEM((3, 18, 3, 24, DEEP), F32),
                pltpu.VMEM((3, 6, 32, 128), F32),
                pltpu.VMEM((3, 6, 24, DEEP), F32),
                pltpu.VMEM((ROWS, 3, 3, 32, 128), F32),
                pltpu.VMEM((12, 24, 16, 128), F32),
                pltpu.VMEM((9, 5, 24, 128), F32),
                pltpu.VMEM((9, 5, 24, 128), F32),
                pltpu.VMEM((9, 16, 128), F32),
                pltpu.VMEM((9, 4, 8, 128), F32),
                pltpu.VMEM((9, 8, 128), F32),
                pltpu.VMEM((9, 5, 24, 128), F32),
                pltpu.VMEM((5, 24, 128), jnp.int32),
                pltpu.VMEM((EX, EY, EZ), jnp.int32),
                pltpu.VMEM((12, 16, 128), F32),
                pltpu.VMEM((3, 4, 16, DEEP), F32),
                pltpu.VMEM((3, 24, DEEP), F32),
                pltpu.VMEM((EZ, DEEP), BF16),
                pltpu.VMEM((DEEP, EZ), BF16),
                pltpu.VMEM((wide // 2, 8, 128), F32),
                pltpu.VMEM((2 * narrow, 8, 128), F32),
                pltpu.SMEM((18,), F32),
                sems((7,)),
                sems((8,)), sems((8,)), sems((3,)), sems((3,)), sems((8,)), sems((8,)),
                sems((8,)), sems((8,)), sems((3,)), sems((3,)), sems((3,)), sems((3,)),
                sems((wide // 2,)), sems((wide // 2,)), sems((2 * narrow,)), sems((2 * narrow,)),
            ],
            compiler_params=pltpu.CompilerParams(
                collective_id=0, has_side_effects=True, vmem_limit_bytes=40 << 20
            ),
        )(*(
            pltpu.with_memory_space_constraint(a, pltpu.MemorySpace.HBM)
            for a in (design, passive, displacement.reshape(9, EX, EY, EZ), support, loading)
        ))
        residual, compliance, sensitivity = pl.pallas_call(
            finish,
            out_shape=(
                jax.ShapeDtypeStruct((9, EX, EY, EZ), F32),
                jax.ShapeDtypeStruct((3,), F32),
                jax.ShapeDtypeStruct((ROWS, COLS, DEEP), F32),
            ),
            in_specs=[vmem] * 5,
            out_specs=(hbm, pl.BlockSpec(memory_space=pltpu.SMEM), hbm),
            scratch_shapes=[pltpu.VMEM((ROWS, 3, COLS, 128), F32), sems((13,))],
            compiler_params=pltpu.CompilerParams(vmem_limit_bytes=8 << 20),
        )(*parts)
        return residual.reshape(3, 3, EX, EY, EZ), compliance, sensitivity

    in_specs = (
        P("wide", "narrow", None),
        P("wide", "narrow", None),
        P(None, None, "wide", "narrow", None),
        P("wide", "narrow", None),
        P("wide", "narrow", None),
    )
    out_specs = (P(None, None, "wide", "narrow", None), P(), P("wide", "narrow", None))
    return jax.shard_map(local, mesh=mesh, in_specs=in_specs, out_specs=out_specs, check_vma=False)
```

```python
import functools
import math

import jax
import jax.numpy as jnp
import numpy as np
from jax import lax
from jax.experimental import pallas as pl
from jax.experimental.pallas import tpu as pltpu
from jax.sharding import PartitionSpec as P

sharpness = 8.0
thresholds = (0.7, 0.5, 0.3)
stiff_floor = 0.001
load_force = 4.0
poisson = 0.3

F32, BF16 = jnp.float32, jnp.bfloat16
MESH = pl.DeviceIdType.MESH
ROWS, COLS, DEEP = 12, 48, 384
EX, EY, EZ = 4, 16, 128
DIRS = ((1, 0), (-1, 0), (0, 1), (0, -1), (1, 1), (1, -1), (-1, 1), (-1, -1))


def element_matrix():
    inv_root = 1.0 / np.sqrt(3.0)
    elastic = np.full((3, 3), poisson) + np.eye(3) * (1.0 - 2.0 * poisson)
    elastic = np.block(
        [[elastic, np.zeros((3, 3))], [np.zeros((3, 3)), np.eye(3) * (0.5 - poisson)]]
    ) / ((1.0 + poisson) * (1.0 - 2.0 * poisson))
    signs = [(2 * (c // 4) - 1, 2 * (c // 2 % 2) - 1, 2 * (c % 2) - 1) for c in range(8)]
    stiffness = np.zeros((24, 24))
    for ga in (-inv_root, inv_root):
        for gb in (-inv_root, inv_root):
            for gc in (-inv_root, inv_root):
                point = (ga, gb, gc)
                strain = np.zeros((6, 24))
                for c in range(8):
                    d = []
                    for along in range(3):
                        s = signs[c][along] / 4.0
                        for other in range(3):
                            if other != along:
                                s = s * (1.0 + signs[c][other] * point[other])
                        d.append(s)
                    col = 3 * c
                    strain[0, col], strain[1, col + 1], strain[2, col + 2] = d
                    strain[3, col], strain[3, col + 1] = d[1], d[0]
                    strain[4, col + 1], strain[4, col + 2] = d[2], d[1]
                    strain[5, col], strain[5, col + 2] = d[2], d[0]
                stiffness = stiffness + strain.T @ elastic @ strain * 0.125
    return stiffness


def mode_matrix():
    h = np.zeros((8, 8))
    for mode in range(8):
        for c in range(8):
            v = 1.0
            for bit in (4, 2, 1):
                if mode & bit:
                    v *= 1.0 if c & bit else -1.0
            h[mode, c] = v
    full = np.kron(h, np.eye(3))
    k = full @ element_matrix() @ full.T / 64.0
    return [
        [(j, float(k[i, j])) for j in range(24) if abs(k[i, j]) > 1e-9] for i in range(24)
    ]


def tent(values):
    p = [a + b for a, b in zip(values, values[1:])]
    q = [a + b for a, b in zip(p, p[2:])]
    r = [a + b for a, b in zip(q, q[1:])]
    return [a + b for a, b in zip(r, r[2:])]


def inverse_weight(place, extent):
    edge = jnp.minimum(place, extent - 1 - place)
    return jnp.where(
        edge >= 3, 1.0 / 16.0, jnp.where(edge == 2, 1.0 / 15.0, jnp.where(edge == 1, 1.0 / 13.0, 0.1))
    ).astype(F32)


def split(value):
    high = value.astype(BF16)
    return high, (value - high.astype(F32)).astype(BF16)


def times(value, matrix):
    high, low = split(value)
    return jnp.dot(high, matrix, preferred_element_type=F32) + jnp.dot(
        low, matrix, preferred_element_type=F32
    )


def level(bl, eta):
    low = math.tanh(sharpness * eta)
    t = jnp.tanh(bl * sharpness - sharpness * eta)
    return t + low, 1.0 - t * t


def denominator(eta):
    return math.tanh(sharpness * eta) + math.tanh(sharpness * (1.0 - eta))


def slope_scale(eta):
    return sharpness / denominator(eta) ** 3 * 3.0 * (1.0 - stiff_floor) / 27.0


def banded(high, low, band, groups):
    h, l = (
        jnp.concatenate([part[3 * g : 3 * g + 3].reshape(144, DEEP) for g in groups], axis=0)
        for part in (high, low)
    )
    b = band[...]
    first, second = (
        jnp.dot(h[:, k : k + 256], b, preferred_element_type=F32)
        + jnp.dot(l[:, k : k + 256], b, preferred_element_type=F32)
        for k in (0, 128)
    )
    lane = lax.broadcasted_iota(jnp.int32, (144 * len(groups), 128), 1)
    middle = jnp.where(lane < 64, first[:, 128:256], second[:, 0:128])
    return first[:, 0:128], middle, second[:, 128:256]


def keep(AH, AL, x, parts):
    for m in range(3):
        block = jnp.concatenate(
            [jnp.concatenate([parts[m, t, c] for t in range(2)], axis=0) for c in range(3)], axis=1
        )
        high, low = split(block)
        AH[x, 16 * m : 16 * m + 16, :] = high
        AL[x, 16 * m : 16 * m + 16, :] = low


def kernel(
    wide, narrow,
    design, passive, disp, support, loading,
    GX, RES, COMP, BAND,
    AH, AL, D, XF, PA, SW, BL, T, EN, ESP, V, M, FS, FXR, FYR, FDR, U, SU, LO, MOD, S3,
    WT, SPREAD, GATHER, AR1, AR2, RX,
    lsem, dss, drs, mss, mrs, bss, brs, ess, ers, fss, frs, sss, srs, a1s, a1r, a2s, a2r,
):
    w = lax.axis_index("wide")
    n = lax.axis_index("narrow")
    zc, xl, core = w // 4, (w // 2) % 2, w % 2
    count1, count2 = wide // 2, 2 * narrow
    i1 = zc * 2 + core
    i2 = xl * narrow + n

    def within(dw, dn):
        ok = None
        for step, at, count in ((dw, w, wide), (dn, n, narrow)):
            if step:
                cond = at < count - 1 if step > 0 else at > 0
                ok = cond if ok is None else ok & cond
        return ok

    def peer1(k):
        j = (i1 + k) % count1
        return (j // 2) * 4 + xl * 2 + j % 2, n

    def peer2(k):
        j = (i2 + k) % count2
        return zc * 4 + (j // narrow) * 2 + core, j % narrow

    def around(dw, dn):
        return ((w + dw + wide) % wide, (n + dn + narrow) % narrow)

    barrier = pltpu.get_barrier_semaphore()
    total = count1 - 1 + count2 - 1
    for dw, dn in DIRS:
        total = total + within(dw, dn).astype(jnp.int32)

        @pl.when(within(dw, dn))
        def _(dw=dw, dn=dn):
            pl.semaphore_signal(barrier, 1, device_id=around(dw, dn), device_id_type=MESH)

    for k in range(1, count1):
        pl.semaphore_signal(barrier, 1, device_id=peer1(k), device_id_type=MESH)
    for k in range(1, count2):
        pl.semaphore_signal(barrier, 1, device_id=peer2(k), device_id_type=MESH)

    loads = [
        pltpu.make_async_copy(disp, U.at[:, 0:4, 0:16, :], lsem.at[0]),
        pltpu.make_async_copy(support, SU.at[0:4, 0:16, :], lsem.at[1]),
        pltpu.make_async_copy(design, D.at[3:15, 8:56, :], lsem.at[2]),
        pltpu.make_async_copy(loading, LO, lsem.at[3]),
    ] + [
        pltpu.make_async_copy(passive.at[:, :, 128 * c : 128 * c + 128], PA.at[:, c], lsem.at[4 + c])
        for c in range(3)
    ]
    for copy in loads:
        copy.start()

    class Message:
        def __init__(self, src, dst, ss, rs, dw, dn):
            self.to, self.origin = within(dw, dn), within(-dw, -dn)
            self.copy = pltpu.make_async_remote_copy(
                src_ref=src, dst_ref=dst, send_sem=ss, recv_sem=rs,
                device_id=around(dw, dn), device_id_type=MESH,
            )

        def start(self):
            pl.when(self.to)(self.copy.start)

        def wait_send(self):
            pl.when(self.to)(self.copy.wait_send)

        def wait_recv(self):
            pl.when(self.origin)(self.copy.wait_recv)

    def x_part(dw, low, high, depth):
        if dw == 0:
            return pl.ds(low, high - low), pl.ds(low, high - low)
        if dw > 0:
            return pl.ds(high - depth, depth), pl.ds(low - depth, depth)
        return pl.ds(low, depth), pl.ds(high, depth)

    designs, fields, energies = [], [], []
    for d, (dw, dn) in enumerate(DIRS):
        sx, tx = x_part(dw, 0, ROWS, 3)
        tx = pl.ds(tx.start + 3, tx.size)
        sy, ty = x_part(dn, 0, COLS, 3)
        ty = pl.ds(ty.start + 8, ty.size)
        designs.append(
            Message(design.at[sx, sy, :], D.at[tx, ty, :], dss.at[d], drs.at[d], dw, dn)
        )
        sx, tx = x_part(dw, 3, 15, 3)
        sy, ty = x_part(dn, 8, 24, 1)
        fields.append(
            Message(BL.at[sx, :, sy, :], BL.at[tx, :, ty, :], bss.at[d], brs.at[d], dw, dn)
        )
        sx, tx = x_part(dw, 1, 5, 1)
        energies.append(
            Message(EN.at[:, sx, sy, :], EN.at[:, tx, ty, :], ess.at[d], ers.at[d], dw, dn)
        )
    moves, holds, forces = [], [], []
    for d, (dw, dn) in enumerate(((-1, 0), (0, -1), (-1, -1))):
        sx, tx = x_part(dw, 0, 4, 1)
        sy, ty = x_part(dn, 0, 16, 1)
        moves.append(
            Message(disp.at[:, sx, sy, :], U.at[:, tx, ty, :], mss.at[d], mrs.at[d], dw, dn)
        )
        holds.append(
            Message(support.at[sx, sy, :], SU.at[tx, ty, :], sss.at[d], srs.at[d], dw, dn)
        )
    forces.append(Message(FS.at[:, 4, 0:16, :], FXR, fss.at[0], frs.at[0], 1, 0))
    forces.append(
        Message(FS.at[:, 0:4, 16:17, :], FYR.at[:, :, 0:1, :], fss.at[1], frs.at[1], 0, 1)
    )
    forces.append(Message(FS.at[:, 4, 16:17, :], FDR.at[:, 0:1, :], fss.at[2], frs.at[2], 1, 1))

    pl.semaphore_wait(barrier, total)
    for message in moves[1:] + holds[1:] + designs + moves[:1] + holds[:1]:
        message.start()

    def near(shape):
        return lax.broadcasted_iota(jnp.int32, shape, 0), lax.broadcasted_iota(jnp.int32, shape, 1)

    a, b = near((256, 256))
    BAND[...] = jnp.maximum(4 - jnp.abs(a - b), 0).astype(F32).astype(BF16)
    a, b = near((EZ, DEEP))
    gap = b - 3 * a
    SPREAD[...] = jnp.where((gap >= 0) & (gap < 3), 1.0, 0.0).astype(BF16)
    a, b = near((DEEP, EZ))
    gap = a - 3 * b
    GATHER[...] = jnp.where((gap >= 0) & (gap < 3), 1.0, 0.0).astype(BF16)
    a, b = near((24, DEEP))
    a = jnp.where(a == 23, -1, a)
    deep = inverse_weight(b, DEEP)
    for m in range(3):
        WT[m] = inverse_weight(n * COLS + 3 * a + m, narrow * COLS) * deep
    for x in range(18):
        RX[x] = inverse_weight(w * ROWS + x - 3, wide * ROWS)

    zero = functools.partial(jnp.zeros, dtype=F32)

    @pl.when(w == 0)
    def _():
        D[0:3] = zero((3, 64, DEEP))
        BL[0:3] = zero((3, 3, 32, DEEP))
        EN[:, 0] = zero((3, 32, 128))
        FXR[...] = zero((9, 16, 128))

    @pl.when(w == wide - 1)
    def _():
        D[15:18] = zero((3, 64, DEEP))
        BL[15:18] = zero((3, 3, 32, DEEP))
        EN[:, 5] = zero((3, 32, 128))
        U[:, 4] = zero((9, 24, 128))

    @pl.when(n == 0)
    def _():
        D[:, 0:8] = zero((18, 8, DEEP))
        BL[:, :, 0:8] = zero((18, 3, 8, DEEP))
        EN[:, :, 0:8] = zero((3, 6, 8, 128))
        FYR[...] = zero((9, 4, 8, 128))

    @pl.when(n == narrow - 1)
    def _():
        D[:, 56:64] = zero((18, 8, DEEP))
        BL[:, :, 24:32] = zero((18, 3, 8, DEEP))
        EN[:, :, 24:32] = zero((3, 6, 8, 128))
        U[:, :, 16:24] = zero((9, 5, 8, 128))

    @pl.when((n == 0) | (w == 0))
    def _():
        FDR[...] = zero((9, 8, 128))

    FS[...] = zero((9, 5, 24, 128))

    for copy in loads[4:]:
        copy.wait()

    def solid_step(x, _):
        for m in range(3):
            for t in range(2):
                for c in range(3):
                    void = PA[x, c, pl.ds(24 * t + m, 8, stride=3), :]
                    rows, lanes = slice(8 * t, 8 * t + 8), slice(128 * c, 128 * c + 128)
                    SW[x, m, rows, lanes] = (1.0 - void.astype(F32)) * (WT[m, rows, lanes] * RX[x + 3])
        return 0

    lax.fori_loop(0, ROWS, solid_step, 0)

    loads[0].wait()
    loads[1].wait()

    def moved(l):
        free = 1.0 - SU[l].astype(F32)
        for k in range(9):
            M[k, l] = U[k, l] * free

    for message in (moves[1], holds[1]):
        message.wait_recv()
    for l in range(4):
        moved(l)

    modes = mode_matrix()
    lane = lax.broadcasted_iota(jnp.int32, (8, 128), 1)

    def energy_step(r, l):
        i = r * 4 + l
        for t in range(2):
            hat = [None] * 24
            for comp in range(3):
                k = r * 3 + comp
                corner = {}
                for p in range(2):
                    for q in range(2):
                        v = M[k, l + p, pl.ds(8 * t + q, 8), :]
                        v1 = jnp.where(lane < 127, pltpu.roll(v, 127, axis=1), 0.0)
                        corner[p, q, 0], corner[p, q, 1] = v + v1, v1 - v
                for s in range(2):
                    y = {}
                    for p in range(2):
                        y[p, 0] = corner[p, 0, s] + corner[p, 1, s]
                        y[p, 1] = corner[p, 1, s] - corner[p, 0, s]
                    for q in range(2):
                        hat[3 * (2 * q + s) + comp] = y[0, q] + y[1, q]
                        hat[3 * (4 + 2 * q + s) + comp] = y[1, q] - y[0, q]
            energy = None
            for row in range(24):
                if not modes[row]:
                    continue
                value = None
                for j, factor in modes[row]:
                    term = hat[j] * factor
                    value = term if value is None else value + term
                V[i, row, 8 * t : 8 * t + 8] = value
                term = value * hat[row]
                energy = term if energy is None else energy + term
            EN[r, 1 + l, 8 + 8 * t : 16 + 8 * t] = energy

    def inner_energies(j, _):
        energy_step(j // 3, j % 3)
        return 0

    def last_energies(r, _):
        energy_step(r, 3)
        return 0

    lax.fori_loop(0, 9, inner_energies, 0)

    loads[2].wait()
    for message in designs:
        message.wait_recv()

    def x_step(t, _):
        rows = pl.ds(pl.multiple_of(8 * t, 8), 8)
        for c in range(3):
            out = tent([D[x, rows, 128 * c : 128 * c + 128] for x in range(18)])
            for x in range(ROWS):
                XF[x, c, rows, :] = out[x]
        return 0

    lax.fori_loop(0, 8, x_step, 0)

    def y_step(x, _):
        parts = {}
        for t in range(2):
            for c in range(3):
                out = tent([XF[x, c, pl.ds(8 + 24 * t + k, 8, stride=3), :] for k in range(-3, 6)])
                for m in range(3):
                    parts[m, t, c] = out[m]
        keep(AH, AL, x, parts)
        return 0

    lax.fori_loop(0, ROWS, y_step, 0)

    def z_step(groups):
        z = banded(AH, AL, BAND, groups)
        for i, g in enumerate(groups):
            for xr in range(3):
                x = 3 * g + xr
                for m in range(3):
                    at = 144 * i + 16 * (3 * xr + m)
                    for c in range(3):
                        lanes = slice(128 * c, 128 * c + 128)
                        BL[x + 3, m, 8:24, lanes] = z[c][at : at + 16] * SW[x, m, :, lanes]

    z_step((0, 3))
    for message in fields[:2]:
        message.start()
    for message in (moves[0], holds[0], moves[2], holds[2]):
        message.wait_recv()
    moved(4)
    lax.fori_loop(0, 3, last_energies, 0)
    for message in energies:
        message.start()
    z_step((1, 2))
    for message in fields[2:]:
        message.start()

    def own_step(xe, _):
        sums = [None] * 3
        for xr in range(3):
            for m in range(3):
                bl = BL[3 + 3 * xe + xr, m, 8:24, :]
                for r in range(3):
                    rho, _ = level(bl, thresholds[r])
                    cube = rho * rho * rho
                    sums[r] = cube if sums[r] is None else sums[r] + cube
        for r in range(3):
            S3[r, xe] = sums[r]
        return 0

    lax.fori_loop(0, 4, own_step, 0)
    moduli = times(S3[...].reshape(192, DEEP), GATHER[...]).reshape(12, 16, 128)
    for r in range(3):
        scale = (1.0 - stiff_floor) / 27.0 / denominator(thresholds[r]) ** 3
        MOD[4 * r : 4 * r + 4] = moduli[4 * r : 4 * r + 4] * scale + stiff_floor
    row8 = lax.broadcasted_iota(jnp.int32, (8, 128), 0)
    tile = zero((8, 128))
    for r in range(3):
        part = zero((8, 128))
        for l in range(4):
            for t in range(2):
                part = part + MOD[4 * r + l, 8 * t : 8 * t + 8] * EN[r, 1 + l, 8 + 8 * t : 16 + 8 * t]
        tile = jnp.where(row8 == r, jnp.sum(part, axis=0, keepdims=True), tile)
    AR1[i1] = tile

    def exchange(buf, ss, rs, me, count, peer):
        def remote(part, device):
            return pltpu.make_async_remote_copy(
                src_ref=part, dst_ref=part, send_sem=ss, recv_sem=rs, device_id=device, device_id_type=MESH
            )

        whole = remote(buf.at[pl.ds(0, count - 1)], peer(1))
        return [remote(buf.at[me], peer(k)) for k in range(1, count)], whole

    sends1, whole1 = exchange(AR1, a1s, a1r, i1, count1, peer1)
    sends2, whole2 = exchange(AR2, a2s, a2r, i2, count2, peer2)
    for send in sends1:
        send.start()

    def force_step(i, _):
        r, l = i // 4, i % 4
        for t in range(2):
            mod = MOD[i, 8 * t : 8 * t + 8]
            for comp in range(3):
                k = r * 3 + comp

                def mode(p, q, s):
                    row = 3 * (4 * p + 2 * q + s) + comp
                    return V[i, row, 8 * t : 8 * t + 8] * mod if modes[row] else None

                def minus(a, b):
                    return b * -1.0 if a is None else a - b

                def plus(a, b):
                    return b if a is None else a + b

                zz = {}
                for p in range(2):
                    for q in range(2):
                        v0, v1 = mode(p, q, 0), mode(p, q, 1)
                        high = jnp.where(lane > 0, pltpu.roll(plus(v0, v1), 1, axis=1), 0.0)
                        zz[p, q] = minus(v0, v1) + high
                for c in range(2):
                    y0, y1 = [
                        (zz[p, 1] + zz[p, 0]) if c else (zz[p, 0] - zz[p, 1]) for p in range(2)
                    ]
                    rows = pl.ds(8 * t + c, 8)
                    FS[k, l, rows, :] = FS[k, l, rows, :] + (y0 - y1)
                    FS[k, l + 1, rows, :] = FS[k, l + 1, rows, :] + (y0 + y1)
        return 0

    lax.fori_loop(0, 12, force_step, 0)

    block = jnp.concatenate([EN[r, l, 8:24] for r in range(3) for l in range(1, 5)], axis=0)
    ESP[:, 1:5, 0:16] = times(block, SPREAD[...]).reshape(3, 4, 16, DEEP)

    def terms(x, xe, m, bl, rows):
        scale = WT[m, rows] * RX[x]
        for r in range(3):
            rho, slope = level(bl, thresholds[r])
            T[r, x, m, rows] = rho * rho * slope * (ESP[r, xe, rows] * scale)

    def row_terms(x, _):
        for m in range(3):
            terms(x, x // 3, m, BL[x, m, 8:24, :], slice(0, 16))
        return 0

    def column_terms(x, _):
        for m in range(3):
            edge = lax.broadcasted_iota(jnp.int32, (8, DEEP), 0) == 7
            bl = jnp.where(edge, BL[x, m, 0:8, :], BL[x, m, 24:32, :])
            terms(x, x // 3, m, bl, slice(16, 24))
        return 0

    lax.fori_loop(3, 15, row_terms, 0)

    whole1.wait_recv()
    total1 = AR1[0]
    for j in range(1, count1):
        total1 = total1 + AR1[j]
    AR2[i2] = total1
    for send in sends2:
        send.start()
    for message in forces:
        message.start()

    for message in energies:
        message.wait_recv()
    blocks = []
    for r in range(3):
        blocks += [EN[r, 0, 8:24], EN[r, 5, 8:24]]
        for l in range(6):
            blocks.append(jnp.where(row8 == 7, EN[r, l, 0:8], EN[r, l, 24:32]))
    block = times(jnp.concatenate(blocks, axis=0), SPREAD[...])
    for r in range(3):
        ESP[r, 0, 0:16] = block[80 * r : 80 * r + 16]
        ESP[r, 5, 0:16] = block[80 * r + 16 : 80 * r + 32]
        for l in range(6):
            ESP[r, l, 16:24] = block[80 * r + 32 + 8 * l : 80 * r + 40 + 8 * l]
    for message in fields[:2]:
        message.wait_recv()
    for l in (0, 15):
        lax.fori_loop(l, l + 3, row_terms, 0)
    for message in fields[2:4]:
        message.wait_recv()
    lax.fori_loop(3, 15, column_terms, 0)
    for message in fields[4:]:
        message.wait_recv()
    for l in (0, 15):
        lax.fori_loop(l, l + 3, column_terms, 0)

    for message in forces:
        message.wait_recv()
    loads[3].wait()
    for k in range(9):
        FS[k, 0, 0:16] = FS[k, 0, 0:16] + FXR[k]
        FS[k, 0:4, 0:8] = FS[k, 0:4, 0:8] + jnp.where(
            lax.broadcasted_iota(jnp.int32, (4, 8, 128), 1) == 0, FYR[k], 0.0
        )
        FS[k, 0, 0:8] = FS[k, 0, 0:8] + jnp.where(row8 == 0, FDR[k], 0.0)
    free = 1.0 - SU[0:4, 0:16].astype(F32)
    load = LO[...].astype(F32) * (-load_force)
    for k in range(9):
        stiff = FS[k, 0:4, 0:16]
        RES[k] = ((load - stiff) if k % 3 == 2 else (0.0 - stiff)) * free

    whole2.wait_recv()
    total2 = AR2[0]
    for j in range(1, count2):
        total2 = total2 + AR2[j]
    COMP[...] = total2
    scales = []
    for r in range(3):
        whole = jnp.sum(total2[r : r + 1], axis=1, keepdims=True)
        scales.append(jnp.broadcast_to(-slope_scale(thresholds[r]) / whole, (8, 128)))

    def x_back(m, _):
        for t in range(3):
            for c in range(3):
                lanes = slice(128 * c, 128 * c + 128)
                rows = slice(8 * t, 8 * t + 8)
                values = []
                for x in range(18):
                    v = T[0, x, m, rows, lanes] * scales[0]
                    v = v + T[1, x, m, rows, lanes] * scales[1]
                    values.append(v + T[2, x, m, rows, lanes] * scales[2])
                out = tent(values)
                for x in range(ROWS):
                    GX[x, m, c, 8 + 8 * t : 16 + 8 * t, :] = out[x]
                    if t == 2:
                        GX[x, m, c, 0:8, :] = out[x]
        return 0

    lax.fori_loop(0, 3, x_back, 0)

    for message in moves + holds + designs + fields + energies + forces:
        message.wait_send()
    whole1.wait_send()
    whole2.wait_send()


def finish(GX, RES, COMP, BAND, res_out, comp_out, sens_out, AH, AL, OUT, osem):
    res_copy = pltpu.make_async_copy(RES, res_out, osem.at[6])
    res_copy.start()
    for r in range(3):
        comp_out[r] = jnp.sum(COMP[r : r + 1])

    def out_copy(g, c):
        return pltpu.make_async_copy(
            OUT.at[pl.ds(6 * g, 6), c],
            sens_out.at[pl.ds(6 * g, 6), :, 128 * c : 128 * c + 128],
            osem.at[3 * g + c],
        )

    def y_back(x, _):
        parts = {}
        for t in range(2):
            for c in range(3):
                out = tent([GX[x, k % 3, c, pl.ds(8 + 8 * t + k // 3, 8), :] for k in range(-3, 6)])
                for m in range(3):
                    parts[m, t, c] = out[m]
        keep(AH, AL, x, parts)
        return 0

    for g in range(2):
        lax.fori_loop(6 * g, 6 * g + 6, y_back, 0)
        z = banded(AH, AL, BAND, (2 * g, 2 * g + 1))
        for c in range(3):
            for xr in range(6):
                for m in range(3):
                    for t in range(2):
                        at = 16 * (3 * xr + m) + 8 * t
                        OUT[6 * g + xr, c, pl.ds(24 * t + m, 8, stride=3), :] = z[c][at : at + 8]
            out_copy(g, c).start()
    res_copy.wait()
    for g in range(2):
        for c in range(3):
            out_copy(g, c).wait()


def solution(mesh):
    wide, narrow = mesh.shape["wide"], mesh.shape["narrow"]

    def local(design, passive, displacement, support, loading):
        sems = pltpu.SemaphoreType.DMA
        vmem = pl.BlockSpec(memory_space=pltpu.VMEM)
        hbm = pl.BlockSpec(memory_space=pltpu.MemorySpace.HBM)
        passed = (
            jax.ShapeDtypeStruct((ROWS, 3, 3, 32, 128), F32),
            jax.ShapeDtypeStruct((9, EX, EY, EZ), F32),
            jax.ShapeDtypeStruct((8, 128), F32),
            jax.ShapeDtypeStruct((256, 256), BF16),
        )
        parts = pl.pallas_call(
            functools.partial(kernel, wide, narrow),
            out_shape=passed,
            in_specs=[hbm] * 5,
            out_specs=(vmem,) * 4,
            scratch_shapes=[
                pltpu.VMEM((ROWS, COLS, DEEP), BF16),
                pltpu.VMEM((ROWS, COLS, DEEP), BF16),
                pltpu.VMEM((18, 64, DEEP), F32),
                pltpu.VMEM((ROWS, 3, 64, 128), F32),
                pltpu.VMEM((ROWS, 3, COLS, 128), jnp.int32),
                pltpu.VMEM((ROWS, 3, 16, DEEP), F32),
                pltpu.VMEM((18, 3, 32, DEEP), F32),
                pltpu.VMEM((3, 18, 3, 24, DEEP), F32),
                pltpu.VMEM((3, 6, 32, 128), F32),
                pltpu.VMEM((3, 6, 24, DEEP), F32),
                pltpu.VMEM((12, 24, 16, 128), F32),
                pltpu.VMEM((9, 5, 24, 128), F32),
                pltpu.VMEM((9, 5, 24, 128), F32),
                pltpu.VMEM((9, 16, 128), F32),
                pltpu.VMEM((9, 4, 8, 128), F32),
                pltpu.VMEM((9, 8, 128), F32),
                pltpu.VMEM((9, 5, 24, 128), F32),
                pltpu.VMEM((5, 24, 128), jnp.int32),
                pltpu.VMEM((EX, EY, EZ), jnp.int32),
                pltpu.VMEM((12, 16, 128), F32),
                pltpu.VMEM((3, 4, 16, DEEP), F32),
                pltpu.VMEM((3, 24, DEEP), F32),
                pltpu.VMEM((EZ, DEEP), BF16),
                pltpu.VMEM((DEEP, EZ), BF16),
                pltpu.VMEM((wide // 2, 8, 128), F32),
                pltpu.VMEM((2 * narrow, 8, 128), F32),
                pltpu.SMEM((18,), F32),
                sems((7,)),
                sems((8,)), sems((8,)), sems((3,)), sems((3,)), sems((8,)), sems((8,)),
                sems((8,)), sems((8,)), sems((3,)), sems((3,)), sems((3,)), sems((3,)),
                sems, sems, sems, sems,
            ],
            compiler_params=pltpu.CompilerParams(
                collective_id=0, has_side_effects=True, vmem_limit_bytes=40 << 20
            ),
        )(*(
            pltpu.with_memory_space_constraint(a, pltpu.MemorySpace.HBM)
            for a in (design, passive, displacement.reshape(9, EX, EY, EZ), support, loading)
        ))
        residual, compliance, sensitivity = pl.pallas_call(
            finish,
            out_shape=(
                jax.ShapeDtypeStruct((9, EX, EY, EZ), F32),
                jax.ShapeDtypeStruct((3,), F32),
                jax.ShapeDtypeStruct((ROWS, COLS, DEEP), F32),
            ),
            in_specs=[vmem] * 4,
            out_specs=(hbm, pl.BlockSpec(memory_space=pltpu.SMEM), hbm),
            scratch_shapes=[
                pltpu.VMEM((ROWS, COLS, DEEP), BF16),
                pltpu.VMEM((ROWS, COLS, DEEP), BF16),
                pltpu.VMEM((ROWS, 3, COLS, 128), F32),
                sems((7,)),
            ],
            compiler_params=pltpu.CompilerParams(vmem_limit_bytes=8 << 20),
        )(*parts)
        return residual.reshape(3, 3, EX, EY, EZ), compliance, sensitivity

    in_specs = (
        P("wide", "narrow", None),
        P("wide", "narrow", None),
        P(None, None, "wide", "narrow", None),
        P("wide", "narrow", None),
        P("wide", "narrow", None),
    )
    out_specs = (P(None, None, "wide", "narrow", None), P(), P("wide", "narrow", None))
    return jax.shard_map(local, mesh=mesh, in_specs=in_specs, out_specs=out_specs, check_vma=False)
```

```python
import functools
import math

import jax
import jax.numpy as jnp
import numpy as np
from jax import lax
from jax.experimental import pallas as pl
from jax.experimental.pallas import tpu as pltpu
from jax.sharding import PartitionSpec as P

sharpness = 8.0
thresholds = (0.7, 0.5, 0.3)
stiff_floor = 0.001
load_force = 4.0
poisson = 0.3

F32, BF16 = jnp.float32, jnp.bfloat16
MESH = pl.DeviceIdType.MESH
ROWS, COLS, DEEP = 12, 48, 384
EX, EY, EZ = 4, 16, 128
DIRS = ((1, 0), (-1, 0), (0, 1), (0, -1), (1, 1), (1, -1), (-1, 1), (-1, -1))


def element_matrix():
    inv_root = 1.0 / np.sqrt(3.0)
    elastic = np.full((3, 3), poisson) + np.eye(3) * (1.0 - 2.0 * poisson)
    elastic = np.block(
        [[elastic, np.zeros((3, 3))], [np.zeros((3, 3)), np.eye(3) * (0.5 - poisson)]]
    ) / ((1.0 + poisson) * (1.0 - 2.0 * poisson))
    signs = [(2 * (c // 4) - 1, 2 * (c // 2 % 2) - 1, 2 * (c % 2) - 1) for c in range(8)]
    stiffness = np.zeros((24, 24))
    for ga in (-inv_root, inv_root):
        for gb in (-inv_root, inv_root):
            for gc in (-inv_root, inv_root):
                point = (ga, gb, gc)
                strain = np.zeros((6, 24))
                for c in range(8):
                    d = []
                    for along in range(3):
                        s = signs[c][along] / 4.0
                        for other in range(3):
                            if other != along:
                                s = s * (1.0 + signs[c][other] * point[other])
                        d.append(s)
                    col = 3 * c
                    strain[0, col], strain[1, col + 1], strain[2, col + 2] = d
                    strain[3, col], strain[3, col + 1] = d[1], d[0]
                    strain[4, col + 1], strain[4, col + 2] = d[2], d[1]
                    strain[5, col], strain[5, col + 2] = d[2], d[0]
                stiffness = stiffness + strain.T @ elastic @ strain * 0.125
    return stiffness


def mode_matrix():
    h = np.zeros((8, 8))
    for mode in range(8):
        for c in range(8):
            v = 1.0
            for bit in (4, 2, 1):
                if mode & bit:
                    v *= 1.0 if c & bit else -1.0
            h[mode, c] = v
    full = np.kron(h, np.eye(3))
    k = full @ element_matrix() @ full.T / 64.0
    return [
        [(j, float(k[i, j])) for j in range(24) if abs(k[i, j]) > 1e-9] for i in range(24)
    ]


def tent(values):
    p = [a + b for a, b in zip(values, values[1:])]
    q = [a + b for a, b in zip(p, p[2:])]
    r = [a + b for a, b in zip(q, q[1:])]
    return [a + b for a, b in zip(r, r[2:])]


def inverse_weight(place, extent):
    edge = jnp.minimum(place, extent - 1 - place)
    return jnp.where(
        edge >= 3, 1.0 / 16.0, jnp.where(edge == 2, 1.0 / 15.0, jnp.where(edge == 1, 1.0 / 13.0, 0.1))
    ).astype(F32)


def split(value):
    high = value.astype(BF16)
    return high, (value - high.astype(F32)).astype(BF16)


def times(value, matrix):
    high, low = split(value)
    return jnp.dot(high, matrix, preferred_element_type=F32) + jnp.dot(
        low, matrix, preferred_element_type=F32
    )


def level(bl, eta):
    low = math.tanh(sharpness * eta)
    t = jnp.tanh(bl * sharpness - sharpness * eta)
    return t + low, 1.0 - t * t


def denominator(eta):
    return math.tanh(sharpness * eta) + math.tanh(sharpness * (1.0 - eta))


def slope_scale(eta):
    return sharpness / denominator(eta) ** 3 * 3.0 * (1.0 - stiff_floor) / 27.0


def banded(high, low, band, groups):
    h, l = (
        jnp.concatenate([part[3 * g : 3 * g + 3].reshape(144, DEEP) for g in groups], axis=0)
        for part in (high, low)
    )
    b = band[...]
    first, second = (
        jnp.dot(h[:, k : k + 256], b, preferred_element_type=F32)
        + jnp.dot(l[:, k : k + 256], b, preferred_element_type=F32)
        for k in (0, 128)
    )
    lane = lax.broadcasted_iota(jnp.int32, (144 * len(groups), 128), 1)
    middle = jnp.where(lane < 64, first[:, 128:256], second[:, 0:128])
    return first[:, 0:128], middle, second[:, 128:256]


def keep(AH, AL, x, parts):
    for m in range(3):
        block = jnp.concatenate(
            [jnp.concatenate([parts[m, t, c] for t in range(2)], axis=0) for c in range(3)], axis=1
        )
        high, low = split(block)
        AH[x, 16 * m : 16 * m + 16, :] = high
        AL[x, 16 * m : 16 * m + 16, :] = low


def kernel(
    wide, narrow,
    design, passive, disp, support, loading,
    GX, RES, COMP, BAND,
    AH, AL, D, XF, PA, SW, BL, T, EN, ESP, V, M, FS, FXR, FYR, FDR, U, SU, LO, MOD, S3,
    WT, SPREAD, GATHER, AR1, AR2, RX,
    lsem, dss, drs, mss, mrs, bss, brs, ess, ers, fss, frs, sss, srs, a1s, a1r, a2s, a2r,
):
    w = lax.axis_index("wide")
    n = lax.axis_index("narrow")
    zc, xl, core = w // 4, (w // 2) % 2, w % 2
    count1, count2 = wide // 2, 2 * narrow
    i1 = zc * 2 + core
    i2 = xl * narrow + n

    def within(dw, dn):
        ok = None
        for step, at, count in ((dw, w, wide), (dn, n, narrow)):
            if step:
                cond = at < count - 1 if step > 0 else at > 0
                ok = cond if ok is None else ok & cond
        return ok

    def peer1(k):
        j = (i1 + k) % count1
        return (j // 2) * 4 + xl * 2 + j % 2, n

    def peer2(k):
        j = (i2 + k) % count2
        return zc * 4 + (j // narrow) * 2 + core, j % narrow

    def around(dw, dn):
        return ((w + dw + wide) % wide, (n + dn + narrow) % narrow)

    barrier = pltpu.get_barrier_semaphore()
    total = count1 - 1 + count2 - 1
    for dw, dn in DIRS:
        total = total + within(dw, dn).astype(jnp.int32)

        @pl.when(within(dw, dn))
        def _(dw=dw, dn=dn):
            pl.semaphore_signal(barrier, 1, device_id=around(dw, dn), device_id_type=MESH)

    for k in range(1, count1):
        pl.semaphore_signal(barrier, 1, device_id=peer1(k), device_id_type=MESH)
    for k in range(1, count2):
        pl.semaphore_signal(barrier, 1, device_id=peer2(k), device_id_type=MESH)

    loads = [
        pltpu.make_async_copy(disp, U.at[:, 0:4, 0:16, :], lsem.at[0]),
        pltpu.make_async_copy(support, SU.at[0:4, 0:16, :], lsem.at[1]),
        pltpu.make_async_copy(design, D.at[3:15, 8:56, :], lsem.at[2]),
        pltpu.make_async_copy(loading, LO, lsem.at[3]),
    ] + [
        pltpu.make_async_copy(passive.at[:, :, 128 * c : 128 * c + 128], PA.at[:, c], lsem.at[4 + c])
        for c in range(3)
    ]
    for copy in loads:
        copy.start()

    class Message:
        def __init__(self, src, dst, ss, rs, dw, dn):
            self.to, self.origin = within(dw, dn), within(-dw, -dn)
            self.copy = pltpu.make_async_remote_copy(
                src_ref=src, dst_ref=dst, send_sem=ss, recv_sem=rs,
                device_id=around(dw, dn), device_id_type=MESH,
            )

        def start(self):
            pl.when(self.to)(self.copy.start)

        def wait_send(self):
            pl.when(self.to)(self.copy.wait_send)

        def wait_recv(self):
            pl.when(self.origin)(self.copy.wait_recv)

    def x_part(dw, low, high, depth):
        if dw == 0:
            return pl.ds(low, high - low), pl.ds(low, high - low)
        if dw > 0:
            return pl.ds(high - depth, depth), pl.ds(low - depth, depth)
        return pl.ds(low, depth), pl.ds(high, depth)

    designs, fields, energies = [], [], []
    for d, (dw, dn) in enumerate(DIRS):
        sx, tx = x_part(dw, 0, ROWS, 3)
        tx = pl.ds(tx.start + 3, tx.size)
        sy, ty = x_part(dn, 0, COLS, 3)
        ty = pl.ds(ty.start + 8, ty.size)
        designs.append(
            Message(design.at[sx, sy, :], D.at[tx, ty, :], dss.at[d], drs.at[d], dw, dn)
        )
        sx, tx = x_part(dw, 3, 15, 3)
        sy, ty = x_part(dn, 8, 24, 1)
        fields.append(
            Message(BL.at[sx, :, sy, :], BL.at[tx, :, ty, :], bss.at[d], brs.at[d], dw, dn)
        )
        sx, tx = x_part(dw, 1, 5, 1)
        energies.append(
            Message(EN.at[:, sx, sy, :], EN.at[:, tx, ty, :], ess.at[d], ers.at[d], dw, dn)
        )
    moves, holds, forces = [], [], []
    for d, (dw, dn) in enumerate(((-1, 0), (0, -1), (-1, -1))):
        sx, tx = x_part(dw, 0, 4, 1)
        sy, ty = x_part(dn, 0, 16, 1)
        moves.append(
            Message(disp.at[:, sx, sy, :], U.at[:, tx, ty, :], mss.at[d], mrs.at[d], dw, dn)
        )
        holds.append(
            Message(support.at[sx, sy, :], SU.at[tx, ty, :], sss.at[d], srs.at[d], dw, dn)
        )
    forces.append(Message(FS.at[:, 4, 0:16, :], FXR, fss.at[0], frs.at[0], 1, 0))
    forces.append(
        Message(FS.at[:, 0:4, 16:17, :], FYR.at[:, :, 0:1, :], fss.at[1], frs.at[1], 0, 1)
    )
    forces.append(Message(FS.at[:, 4, 16:17, :], FDR.at[:, 0:1, :], fss.at[2], frs.at[2], 1, 1))

    pl.semaphore_wait(barrier, total)
    for message in moves[1:] + holds[1:] + designs[2:] + designs[:2] + moves[:1] + holds[:1]:
        message.start()

    def near(shape):
        return lax.broadcasted_iota(jnp.int32, shape, 0), lax.broadcasted_iota(jnp.int32, shape, 1)

    a, b = near((256, 256))
    BAND[...] = jnp.maximum(4 - jnp.abs(a - b), 0).astype(F32).astype(BF16)
    a, b = near((EZ, DEEP))
    gap = b - 3 * a
    SPREAD[...] = jnp.where((gap >= 0) & (gap < 3), 1.0, 0.0).astype(BF16)
    a, b = near((DEEP, EZ))
    gap = a - 3 * b
    GATHER[...] = jnp.where((gap >= 0) & (gap < 3), 1.0, 0.0).astype(BF16)
    a, b = near((24, DEEP))
    a = jnp.where(a == 23, -1, a)
    deep = inverse_weight(b, DEEP)
    for m in range(3):
        WT[m] = inverse_weight(n * COLS + 3 * a + m, narrow * COLS) * deep
    for x in range(18):
        RX[x] = inverse_weight(w * ROWS + x - 3, wide * ROWS)

    zero = functools.partial(jnp.zeros, dtype=F32)

    @pl.when(w == 0)
    def _():
        D[0:3] = zero((3, 64, DEEP))
        BL[0:3] = zero((3, 3, 32, DEEP))
        EN[:, 0] = zero((3, 32, 128))
        FXR[...] = zero((9, 16, 128))

    @pl.when(w == wide - 1)
    def _():
        D[15:18] = zero((3, 64, DEEP))
        BL[15:18] = zero((3, 3, 32, DEEP))
        EN[:, 5] = zero((3, 32, 128))
        U[:, 4] = zero((9, 24, 128))

    @pl.when(n == 0)
    def _():
        D[:, 0:8] = zero((18, 8, DEEP))
        BL[:, :, 0:8] = zero((18, 3, 8, DEEP))
        EN[:, :, 0:8] = zero((3, 6, 8, 128))
        FYR[...] = zero((9, 4, 8, 128))

    @pl.when(n == narrow - 1)
    def _():
        D[:, 56:64] = zero((18, 8, DEEP))
        BL[:, :, 24:32] = zero((18, 3, 8, DEEP))
        EN[:, :, 24:32] = zero((3, 6, 8, 128))
        U[:, :, 16:24] = zero((9, 5, 8, 128))

    @pl.when((n == 0) | (w == 0))
    def _():
        FDR[...] = zero((9, 8, 128))

    FS[...] = zero((9, 5, 24, 128))

    for copy in loads[4:]:
        copy.wait()

    def solid_step(x, _):
        for m in range(3):
            for t in range(2):
                for c in range(3):
                    void = PA[x, c, pl.ds(24 * t + m, 8, stride=3), :]
                    rows, lanes = slice(8 * t, 8 * t + 8), slice(128 * c, 128 * c + 128)
                    SW[x, m, rows, lanes] = (1.0 - void.astype(F32)) * (WT[m, rows, lanes] * RX[x + 3])
        return 0

    lax.fori_loop(0, ROWS, solid_step, 0)

    loads[0].wait()
    loads[1].wait()

    def moved(l):
        free = 1.0 - SU[l].astype(F32)
        for k in range(9):
            M[k, l] = U[k, l] * free

    for message in (moves[1], holds[1]):
        message.wait_recv()
    for l in range(4):
        moved(l)

    modes = mode_matrix()
    lane = lax.broadcasted_iota(jnp.int32, (8, 128), 1)

    def energy_step(r, l):
        i = r * 4 + l
        for t in range(2):
            hat = [None] * 24
            for comp in range(3):
                k = r * 3 + comp
                corner = {}
                for p in range(2):
                    for q in range(2):
                        v = M[k, l + p, pl.ds(8 * t + q, 8), :]
                        v1 = jnp.where(lane < 127, pltpu.roll(v, 127, axis=1), 0.0)
                        corner[p, q, 0], corner[p, q, 1] = v + v1, v1 - v
                for s in range(2):
                    y = {}
                    for p in range(2):
                        y[p, 0] = corner[p, 0, s] + corner[p, 1, s]
                        y[p, 1] = corner[p, 1, s] - corner[p, 0, s]
                    for q in range(2):
                        hat[3 * (2 * q + s) + comp] = y[0, q] + y[1, q]
                        hat[3 * (4 + 2 * q + s) + comp] = y[1, q] - y[0, q]
            energy = None
            for row in range(24):
                if not modes[row]:
                    continue
                value = None
                for j, factor in modes[row]:
                    term = hat[j] * factor
                    value = term if value is None else value + term
                V[i, row, 8 * t : 8 * t + 8] = value
                term = value * hat[row]
                energy = term if energy is None else energy + term
            EN[r, 1 + l, 8 + 8 * t : 16 + 8 * t] = energy

    def inner_energies(j, _):
        energy_step(j // 3, j % 3)
        return 0

    def last_energies(r, _):
        energy_step(r, 3)
        return 0

    lax.fori_loop(0, 9, inner_energies, 0)
    early = [message for message, d in zip(energies, DIRS) if d[0] < 0]
    late = [message for message, d in zip(energies, DIRS) if d[0] >= 0]
    for message in early:
        message.start()

    loads[2].wait()
    for message in designs:
        message.wait_recv()

    def x_step(t, _):
        rows = pl.ds(pl.multiple_of(8 * t, 8), 8)
        for c in range(3):
            out = tent([D[x, rows, 128 * c : 128 * c + 128] for x in range(18)])
            for x in range(ROWS):
                XF[x, c, rows, :] = out[x]
        return 0

    lax.fori_loop(0, 8, x_step, 0)

    def y_step(x, _):
        parts = {}
        for t in range(2):
            for c in range(3):
                out = tent([XF[x, c, pl.ds(8 + 24 * t + k, 8, stride=3), :] for k in range(-3, 6)])
                for m in range(3):
                    parts[m, t, c] = out[m]
        keep(AH, AL, x, parts)
        return 0

    lax.fori_loop(0, ROWS, y_step, 0)

    def z_step(groups):
        z = banded(AH, AL, BAND, groups)
        for i, g in enumerate(groups):
            for xr in range(3):
                x = 3 * g + xr
                for m in range(3):
                    at = 144 * i + 16 * (3 * xr + m)
                    for c in range(3):
                        lanes = slice(128 * c, 128 * c + 128)
                        BL[x + 3, m, 8:24, lanes] = z[c][at : at + 16] * SW[x, m, :, lanes]

    z_step((0, 3))
    z_step((1, 2))
    for message in fields[2:]:
        message.start()
    fields[1].start()
    for message in (moves[0], holds[0], moves[2], holds[2]):
        message.wait_recv()
    moved(4)
    lax.fori_loop(0, 3, last_energies, 0)
    for message in late:
        message.start()
    fields[0].start()

    def own_step(xe, _):
        sums = [None] * 3
        for xr in range(3):
            for m in range(3):
                bl = BL[3 + 3 * xe + xr, m, 8:24, :]
                for r in range(3):
                    rho, _ = level(bl, thresholds[r])
                    cube = rho * rho * rho
                    sums[r] = cube if sums[r] is None else sums[r] + cube
        for r in range(3):
            S3[r, xe] = sums[r]
        return 0

    lax.fori_loop(0, 4, own_step, 0)
    moduli = times(S3[...].reshape(192, DEEP), GATHER[...]).reshape(12, 16, 128)
    for r in range(3):
        scale = (1.0 - stiff_floor) / 27.0 / denominator(thresholds[r]) ** 3
        MOD[4 * r : 4 * r + 4] = moduli[4 * r : 4 * r + 4] * scale + stiff_floor
    row8 = lax.broadcasted_iota(jnp.int32, (8, 128), 0)
    spot = lax.broadcasted_iota(jnp.int32, (1, 128), 1)
    line = zero((1, 128))
    for r in range(3):
        part = zero((8, 128))
        for l in range(4):
            for t in range(2):
                part = part + MOD[4 * r + l, 8 * t : 8 * t + 8] * EN[r, 1 + l, 8 + 8 * t : 16 + 8 * t]
        part = jnp.sum(jnp.sum(part, axis=0, keepdims=True), axis=1, keepdims=True)
        line = jnp.where(spot == r, part, line)
    AR1[pl.ds(i1, 1), :] = line

    def exchange(buf, ss, rs, me, count, peer):
        def remote(part, device):
            return pltpu.make_async_remote_copy(
                src_ref=part, dst_ref=part, send_sem=ss, recv_sem=rs, device_id=device, device_id_type=MESH
            )

        whole = remote(buf.at[pl.ds(0, count - 1)], peer(1))
        return [remote(buf.at[pl.ds(me, 1)], peer(k)) for k in range(1, count)], whole

    sends1, whole1 = exchange(AR1, a1s, a1r, i1, count1, peer1)
    sends2, whole2 = exchange(AR2, a2s, a2r, i2, count2, peer2)
    for send in sends1:
        send.start()

    def force_step(i, _):
        r, l = i // 4, i % 4
        for t in range(2):
            mod = MOD[i, 8 * t : 8 * t + 8]
            for comp in range(3):
                k = r * 3 + comp

                def mode(p, q, s):
                    row = 3 * (4 * p + 2 * q + s) + comp
                    return V[i, row, 8 * t : 8 * t + 8] * mod if modes[row] else None

                def minus(a, b):
                    return b * -1.0 if a is None else a - b

                def plus(a, b):
                    return b if a is None else a + b

                zz = {}
                for p in range(2):
                    for q in range(2):
                        v0, v1 = mode(p, q, 0), mode(p, q, 1)
                        high = jnp.where(lane > 0, pltpu.roll(plus(v0, v1), 1, axis=1), 0.0)
                        zz[p, q] = minus(v0, v1) + high
                for c in range(2):
                    y0, y1 = [
                        (zz[p, 1] + zz[p, 0]) if c else (zz[p, 0] - zz[p, 1]) for p in range(2)
                    ]
                    rows = pl.ds(8 * t + c, 8)
                    FS[k, l, rows, :] = FS[k, l, rows, :] + (y0 - y1)
                    FS[k, l + 1, rows, :] = FS[k, l + 1, rows, :] + (y0 + y1)
        return 0

    lax.fori_loop(0, 12, force_step, 0)

    block = jnp.concatenate([EN[r, l, 8:24] for r in range(3) for l in range(1, 5)], axis=0)
    ESP[:, 1:5, 0:16] = times(block, SPREAD[...]).reshape(3, 4, 16, DEEP)

    def terms(x, xe, m, bl, rows):
        scale = WT[m, rows] * RX[x]
        for r in range(3):
            rho, slope = level(bl, thresholds[r])
            T[r, x, m, rows] = rho * rho * slope * (ESP[r, xe, rows] * scale)

    def row_terms(x, _):
        for m in range(3):
            terms(x, x // 3, m, BL[x, m, 8:24, :], slice(0, 16))
        return 0

    def column_terms(x, _):
        for m in range(3):
            edge = lax.broadcasted_iota(jnp.int32, (8, DEEP), 0) == 7
            bl = jnp.where(edge, BL[x, m, 0:8, :], BL[x, m, 24:32, :])
            terms(x, x // 3, m, bl, slice(16, 24))
        return 0

    lax.fori_loop(3, 15, row_terms, 0)

    whole1.wait_recv()
    AR2[pl.ds(i2, 1), :] = jnp.sum(AR1[...], axis=0, keepdims=True)
    for send in sends2:
        send.start()
    for message in forces:
        message.start()

    for message in energies:
        message.wait_recv()
    blocks = []
    for r in range(3):
        blocks += [EN[r, 0, 8:24], EN[r, 5, 8:24]]
        for l in range(6):
            blocks.append(jnp.where(row8 == 7, EN[r, l, 0:8], EN[r, l, 24:32]))
    block = times(jnp.concatenate(blocks, axis=0), SPREAD[...])
    for r in range(3):
        ESP[r, 0, 0:16] = block[80 * r : 80 * r + 16]
        ESP[r, 5, 0:16] = block[80 * r + 16 : 80 * r + 32]
        for l in range(6):
            ESP[r, l, 16:24] = block[80 * r + 32 + 8 * l : 80 * r + 40 + 8 * l]
    for message in fields[:2]:
        message.wait_recv()
    for l in (0, 15):
        lax.fori_loop(l, l + 3, row_terms, 0)
    for message in fields[2:4]:
        message.wait_recv()
    lax.fori_loop(3, 15, column_terms, 0)
    for message in fields[4:]:
        message.wait_recv()
    for l in (0, 15):
        lax.fori_loop(l, l + 3, column_terms, 0)

    for message in forces:
        message.wait_recv()
    loads[3].wait()
    for k in range(9):
        FS[k, 0, 0:16] = FS[k, 0, 0:16] + FXR[k]
        FS[k, 0:4, 0:8] = FS[k, 0:4, 0:8] + jnp.where(
            lax.broadcasted_iota(jnp.int32, (4, 8, 128), 1) == 0, FYR[k], 0.0
        )
        FS[k, 0, 0:8] = FS[k, 0, 0:8] + jnp.where(row8 == 0, FDR[k], 0.0)
    free = 1.0 - SU[0:4, 0:16].astype(F32)
    load = LO[...].astype(F32) * (-load_force)
    for k in range(9):
        stiff = FS[k, 0:4, 0:16]
        RES[k] = ((load - stiff) if k % 3 == 2 else (0.0 - stiff)) * free

    whole2.wait_recv()
    whole = jnp.sum(AR2[...], axis=0, keepdims=True)
    COMP[...] = jnp.broadcast_to(whole, (8, 128))
    scales = [
        jnp.broadcast_to(-slope_scale(thresholds[r]) / whole[:, r : r + 1], (8, 128)) for r in range(3)
    ]

    def x_back(m, _):
        for t in range(3):
            for c in range(3):
                lanes = slice(128 * c, 128 * c + 128)
                rows = slice(8 * t, 8 * t + 8)
                values = []
                for x in range(18):
                    v = T[0, x, m, rows, lanes] * scales[0]
                    v = v + T[1, x, m, rows, lanes] * scales[1]
                    values.append(v + T[2, x, m, rows, lanes] * scales[2])
                out = tent(values)
                for x in range(ROWS):
                    GX[x, m, c, 8 + 8 * t : 16 + 8 * t, :] = out[x]
                    if t == 2:
                        GX[x, m, c, 0:8, :] = out[x]
        return 0

    lax.fori_loop(0, 3, x_back, 0)

    for message in moves + holds + designs + fields + energies + forces:
        message.wait_send()
    whole1.wait_send()
    whole2.wait_send()


def finish(GX, RES, COMP, BAND, res_out, comp_out, sens_out, AH, AL, OUT, osem):
    res_copy = pltpu.make_async_copy(RES, res_out, osem.at[6])
    res_copy.start()
    spot = lax.broadcasted_iota(jnp.int32, (1, 128), 1)
    for r in range(3):
        comp_out[r] = jnp.sum(jnp.where(spot == r, COMP[0:1], 0.0))

    def out_copy(g, c):
        return pltpu.make_async_copy(
            OUT.at[pl.ds(6 * g, 6), c],
            sens_out.at[pl.ds(6 * g, 6), :, 128 * c : 128 * c + 128],
            osem.at[3 * g + c],
        )

    def y_back(x, _):
        parts = {}
        for t in range(2):
            for c in range(3):
                out = tent([GX[x, k % 3, c, pl.ds(8 + 8 * t + k // 3, 8), :] for k in range(-3, 6)])
                for m in range(3):
                    parts[m, t, c] = out[m]
        keep(AH, AL, x, parts)
        return 0

    for g in range(2):
        lax.fori_loop(6 * g, 6 * g + 6, y_back, 0)
        z = banded(AH, AL, BAND, (2 * g, 2 * g + 1))
        for c in range(3):
            for xr in range(6):
                for m in range(3):
                    for t in range(2):
                        at = 16 * (3 * xr + m) + 8 * t
                        OUT[6 * g + xr, c, pl.ds(24 * t + m, 8, stride=3), :] = z[c][at : at + 8]
            out_copy(g, c).start()
    res_copy.wait()
    for g in range(2):
        for c in range(3):
            out_copy(g, c).wait()


def solution(mesh):
    wide, narrow = mesh.shape["wide"], mesh.shape["narrow"]

    def local(design, passive, displacement, support, loading):
        sems = pltpu.SemaphoreType.DMA
        vmem = pl.BlockSpec(memory_space=pltpu.VMEM)
        hbm = pl.BlockSpec(memory_space=pltpu.MemorySpace.HBM)
        passed = (
            jax.ShapeDtypeStruct((ROWS, 3, 3, 32, 128), F32),
            jax.ShapeDtypeStruct((9, EX, EY, EZ), F32),
            jax.ShapeDtypeStruct((8, 128), F32),
            jax.ShapeDtypeStruct((256, 256), BF16),
        )
        parts = pl.pallas_call(
            functools.partial(kernel, wide, narrow),
            out_shape=passed,
            in_specs=[hbm] * 5,
            out_specs=(vmem,) * 4,
            scratch_shapes=[
                pltpu.VMEM((ROWS, COLS, DEEP), BF16),
                pltpu.VMEM((ROWS, COLS, DEEP), BF16),
                pltpu.VMEM((18, 64, DEEP), F32),
                pltpu.VMEM((ROWS, 3, 64, 128), F32),
                pltpu.VMEM((ROWS, 3, COLS, 128), jnp.int32),
                pltpu.VMEM((ROWS, 3, 16, DEEP), F32),
                pltpu.VMEM((18, 3, 32, DEEP), F32),
                pltpu.VMEM((3, 18, 3, 24, DEEP), F32),
                pltpu.VMEM((3, 6, 32, 128), F32),
                pltpu.VMEM((3, 6, 24, DEEP), F32),
                pltpu.VMEM((12, 24, 16, 128), F32),
                pltpu.VMEM((9, 5, 24, 128), F32),
                pltpu.VMEM((9, 5, 24, 128), F32),
                pltpu.VMEM((9, 16, 128), F32),
                pltpu.VMEM((9, 4, 8, 128), F32),
                pltpu.VMEM((9, 8, 128), F32),
                pltpu.VMEM((9, 5, 24, 128), F32),
                pltpu.VMEM((5, 24, 128), jnp.int32),
                pltpu.VMEM((EX, EY, EZ), jnp.int32),
                pltpu.VMEM((12, 16, 128), F32),
                pltpu.VMEM((3, 4, 16, DEEP), F32),
                pltpu.VMEM((3, 24, DEEP), F32),
                pltpu.VMEM((EZ, DEEP), BF16),
                pltpu.VMEM((DEEP, EZ), BF16),
                pltpu.VMEM((wide // 2, 128), F32),
                pltpu.VMEM((2 * narrow, 128), F32),
                pltpu.SMEM((18,), F32),
                sems((7,)),
                sems((8,)), sems((8,)), sems((3,)), sems((3,)), sems((8,)), sems((8,)),
                sems((8,)), sems((8,)), sems((3,)), sems((3,)), sems((3,)), sems((3,)),
                sems, sems, sems, sems,
            ],
            compiler_params=pltpu.CompilerParams(
                collective_id=0, has_side_effects=True, vmem_limit_bytes=40 << 20
            ),
        )(*(
            pltpu.with_memory_space_constraint(a, pltpu.MemorySpace.HBM)
            for a in (design, passive, displacement.reshape(9, EX, EY, EZ), support, loading)
        ))
        residual, compliance, sensitivity = pl.pallas_call(
            finish,
            out_shape=(
                jax.ShapeDtypeStruct((9, EX, EY, EZ), F32),
                jax.ShapeDtypeStruct((3,), F32),
                jax.ShapeDtypeStruct((ROWS, COLS, DEEP), F32),
            ),
            in_specs=[vmem] * 4,
            out_specs=(hbm, pl.BlockSpec(memory_space=pltpu.SMEM), hbm),
            scratch_shapes=[
                pltpu.VMEM((ROWS, COLS, DEEP), BF16),
                pltpu.VMEM((ROWS, COLS, DEEP), BF16),
                pltpu.VMEM((ROWS, 3, COLS, 128), F32),
                sems((7,)),
            ],
            compiler_params=pltpu.CompilerParams(vmem_limit_bytes=8 << 20),
        )(*parts)
        return residual.reshape(3, 3, EX, EY, EZ), compliance, sensitivity

    in_specs = (
        P("wide", "narrow", None),
        P("wide", "narrow", None),
        P(None, None, "wide", "narrow", None),
        P("wide", "narrow", None),
        P("wide", "narrow", None),
    )
    out_specs = (P(None, None, "wide", "narrow", None), P(), P("wide", "narrow", None))
    return jax.shard_map(local, mesh=mesh, in_specs=in_specs, out_specs=out_specs, check_vma=False)
```

```python
import functools
import math

import jax
import jax.numpy as jnp
import numpy as np
from jax import lax
from jax.experimental import pallas as pl
from jax.experimental.pallas import tpu as pltpu
from jax.sharding import PartitionSpec as P

sharpness = 8.0
thresholds = (0.7, 0.5, 0.3)
stiff_floor = 0.001
load_force = 4.0
poisson = 0.3

F32, BF16 = jnp.float32, jnp.bfloat16
MESH = pl.DeviceIdType.MESH
ROWS, COLS, DEEP = 12, 48, 384
EX, EY, EZ = 4, 16, 128
DIRS = ((1, 0), (-1, 0), (0, 1), (0, -1), (1, 1), (1, -1), (-1, 1), (-1, -1))


def element_matrix():
    inv_root = 1.0 / np.sqrt(3.0)
    elastic = np.full((3, 3), poisson) + np.eye(3) * (1.0 - 2.0 * poisson)
    elastic = np.block(
        [[elastic, np.zeros((3, 3))], [np.zeros((3, 3)), np.eye(3) * (0.5 - poisson)]]
    ) / ((1.0 + poisson) * (1.0 - 2.0 * poisson))
    signs = [(2 * (c // 4) - 1, 2 * (c // 2 % 2) - 1, 2 * (c % 2) - 1) for c in range(8)]
    stiffness = np.zeros((24, 24))
    for ga in (-inv_root, inv_root):
        for gb in (-inv_root, inv_root):
            for gc in (-inv_root, inv_root):
                point = (ga, gb, gc)
                strain = np.zeros((6, 24))
                for c in range(8):
                    d = []
                    for along in range(3):
                        s = signs[c][along] / 4.0
                        for other in range(3):
                            if other != along:
                                s = s * (1.0 + signs[c][other] * point[other])
                        d.append(s)
                    col = 3 * c
                    strain[0, col], strain[1, col + 1], strain[2, col + 2] = d
                    strain[3, col], strain[3, col + 1] = d[1], d[0]
                    strain[4, col + 1], strain[4, col + 2] = d[2], d[1]
                    strain[5, col], strain[5, col + 2] = d[2], d[0]
                stiffness = stiffness + strain.T @ elastic @ strain * 0.125
    return stiffness


def mode_matrix():
    h = np.zeros((8, 8))
    for mode in range(8):
        for c in range(8):
            v = 1.0
            for bit in (4, 2, 1):
                if mode & bit:
                    v *= 1.0 if c & bit else -1.0
            h[mode, c] = v
    full = np.kron(h, np.eye(3))
    k = full @ element_matrix() @ full.T / 64.0
    return [
        [(j, float(k[i, j])) for j in range(24) if abs(k[i, j]) > 1e-9] for i in range(24)
    ]


def tent(values):
    p = [a + b for a, b in zip(values, values[1:])]
    q = [a + b for a, b in zip(p, p[2:])]
    r = [a + b for a, b in zip(q, q[1:])]
    return [a + b for a, b in zip(r, r[2:])]


def inverse_weight(place, extent):
    edge = jnp.minimum(place, extent - 1 - place)
    return jnp.where(
        edge >= 3, 1.0 / 16.0, jnp.where(edge == 2, 1.0 / 15.0, jnp.where(edge == 1, 1.0 / 13.0, 0.1))
    ).astype(F32)


def split(value):
    high = value.astype(BF16)
    return high, (value - high.astype(F32)).astype(BF16)


def times(value, matrix):
    high, low = split(value)
    return jnp.dot(high, matrix, preferred_element_type=F32) + jnp.dot(
        low, matrix, preferred_element_type=F32
    )


def level(bl, eta):
    low = math.tanh(sharpness * eta)
    t = jnp.tanh(bl * sharpness - sharpness * eta)
    return t + low, 1.0 - t * t


def denominator(eta):
    return math.tanh(sharpness * eta) + math.tanh(sharpness * (1.0 - eta))


def slope_scale(eta):
    return sharpness / denominator(eta) ** 3 * 3.0 * (1.0 - stiff_floor) / 27.0


def banded(high, low, band, groups):
    h, l = (
        jnp.concatenate([part[3 * g : 3 * g + 3].reshape(144, DEEP) for g in groups], axis=0)
        for part in (high, low)
    )
    b = band[...]
    first, second = (
        jnp.dot(h[:, k : k + 256], b, preferred_element_type=F32)
        + jnp.dot(l[:, k : k + 256], b, preferred_element_type=F32)
        for k in (0, 128)
    )
    lane = lax.broadcasted_iota(jnp.int32, (144 * len(groups), 128), 1)
    middle = jnp.where(lane < 64, first[:, 128:256], second[:, 0:128])
    return first[:, 0:128], middle, second[:, 128:256]


def keep(AH, AL, x, parts):
    for m in range(3):
        block = jnp.concatenate(
            [jnp.concatenate([parts[m, t, c] for t in range(2)], axis=0) for c in range(3)], axis=1
        )
        high, low = split(block)
        AH[x, 16 * m : 16 * m + 16, :] = high
        AL[x, 16 * m : 16 * m + 16, :] = low


def kernel(
    wide, narrow,
    design, passive, disp, support, loading,
    Y, RES, COMP, BAND,
    AH, AL, D, XF, PA, SW, BL, T, EN, ESP, GX, V, M, FS, FXR, FYR, FDR, U, SU, LO, MOD, S3,
    WT, SPREAD, GATHER, AR1, AR2, RX,
    lsem, dss, drs, mss, mrs, bss, brs, ess, ers, fss, frs, sss, srs, a1s, a1r, a2s, a2r,
):
    w = lax.axis_index("wide")
    n = lax.axis_index("narrow")
    zc, xl, core = w // 4, (w // 2) % 2, w % 2
    count1, count2 = wide // 2, 2 * narrow
    i1 = zc * 2 + core
    i2 = xl * narrow + n

    def within(dw, dn):
        ok = None
        for step, at, count in ((dw, w, wide), (dn, n, narrow)):
            if step:
                cond = at < count - 1 if step > 0 else at > 0
                ok = cond if ok is None else ok & cond
        return ok

    def peer1(k):
        j = (i1 + k) % count1
        return (j // 2) * 4 + xl * 2 + j % 2, n

    def peer2(k):
        j = (i2 + k) % count2
        return zc * 4 + (j // narrow) * 2 + core, j % narrow

    def around(dw, dn):
        return ((w + dw + wide) % wide, (n + dn + narrow) % narrow)

    barrier = pltpu.get_barrier_semaphore()
    total = count1 - 1 + count2 - 1
    for dw, dn in DIRS:
        total = total + within(dw, dn).astype(jnp.int32)

        @pl.when(within(dw, dn))
        def _(dw=dw, dn=dn):
            pl.semaphore_signal(barrier, 1, device_id=around(dw, dn), device_id_type=MESH)

    for k in range(1, count1):
        pl.semaphore_signal(barrier, 1, device_id=peer1(k), device_id_type=MESH)
    for k in range(1, count2):
        pl.semaphore_signal(barrier, 1, device_id=peer2(k), device_id_type=MESH)

    loads = [
        pltpu.make_async_copy(disp, U.at[:, 0:4, 0:16, :], lsem.at[0]),
        pltpu.make_async_copy(support, SU.at[0:4, 0:16, :], lsem.at[1]),
        pltpu.make_async_copy(design, D.at[3:15, 8:56, :], lsem.at[2]),
        pltpu.make_async_copy(loading, LO, lsem.at[3]),
    ] + [
        pltpu.make_async_copy(passive.at[:, :, 128 * c : 128 * c + 128], PA.at[:, c], lsem.at[4 + c])
        for c in range(3)
    ]
    for copy in loads:
        copy.start()

    class Message:
        def __init__(self, src, dst, ss, rs, dw, dn):
            self.to, self.origin = within(dw, dn), within(-dw, -dn)
            self.copy = pltpu.make_async_remote_copy(
                src_ref=src, dst_ref=dst, send_sem=ss, recv_sem=rs,
                device_id=around(dw, dn), device_id_type=MESH,
            )

        def start(self):
            pl.when(self.to)(self.copy.start)

        def wait_send(self):
            pl.when(self.to)(self.copy.wait_send)

        def wait_recv(self):
            pl.when(self.origin)(self.copy.wait_recv)

    def x_part(dw, low, high, depth):
        if dw == 0:
            return pl.ds(low, high - low), pl.ds(low, high - low)
        if dw > 0:
            return pl.ds(high - depth, depth), pl.ds(low - depth, depth)
        return pl.ds(low, depth), pl.ds(high, depth)

    designs, fields, energies = [], [], []
    for d, (dw, dn) in enumerate(DIRS):
        sx, tx = x_part(dw, 0, ROWS, 3)
        tx = pl.ds(tx.start + 3, tx.size)
        sy, ty = x_part(dn, 0, COLS, 3)
        ty = pl.ds(ty.start + 8, ty.size)
        designs.append(
            Message(design.at[sx, sy, :], D.at[tx, ty, :], dss.at[d], drs.at[d], dw, dn)
        )
        sx, tx = x_part(dw, 3, 15, 3)
        sy, ty = x_part(dn, 8, 24, 1)
        fields.append(
            Message(BL.at[sx, :, sy, :], BL.at[tx, :, ty, :], bss.at[d], brs.at[d], dw, dn)
        )
        sx, tx = x_part(dw, 1, 5, 1)
        energies.append(
            Message(EN.at[:, sx, sy, :], EN.at[:, tx, ty, :], ess.at[d], ers.at[d], dw, dn)
        )
    moves, holds, forces = [], [], []
    for d, (dw, dn) in enumerate(((-1, 0), (0, -1), (-1, -1))):
        sx, tx = x_part(dw, 0, 4, 1)
        sy, ty = x_part(dn, 0, 16, 1)
        moves.append(
            Message(disp.at[:, sx, sy, :], U.at[:, tx, ty, :], mss.at[d], mrs.at[d], dw, dn)
        )
        holds.append(
            Message(support.at[sx, sy, :], SU.at[tx, ty, :], sss.at[d], srs.at[d], dw, dn)
        )
    forces.append(Message(FS.at[:, 4, 0:16, :], FXR, fss.at[0], frs.at[0], 1, 0))
    forces.append(
        Message(FS.at[:, 0:4, 16:17, :], FYR.at[:, :, 0:1, :], fss.at[1], frs.at[1], 0, 1)
    )
    forces.append(Message(FS.at[:, 4, 16:17, :], FDR.at[:, 0:1, :], fss.at[2], frs.at[2], 1, 1))

    pl.semaphore_wait(barrier, total)
    for message in moves[1:] + holds[1:] + designs[2:] + designs[:2] + moves[:1] + holds[:1]:
        message.start()

    def near(shape):
        return lax.broadcasted_iota(jnp.int32, shape, 0), lax.broadcasted_iota(jnp.int32, shape, 1)

    a, b = near((256, 256))
    BAND[...] = jnp.maximum(4 - jnp.abs(a - b), 0).astype(F32).astype(BF16)
    a, b = near((EZ, DEEP))
    gap = b - 3 * a
    SPREAD[...] = jnp.where((gap >= 0) & (gap < 3), 1.0, 0.0).astype(BF16)
    a, b = near((DEEP, EZ))
    gap = a - 3 * b
    GATHER[...] = jnp.where((gap >= 0) & (gap < 3), 1.0, 0.0).astype(BF16)
    a, b = near((24, DEEP))
    a = jnp.where(a == 23, -1, a)
    deep = inverse_weight(b, DEEP)
    for m in range(3):
        WT[m] = inverse_weight(n * COLS + 3 * a + m, narrow * COLS) * deep
    for x in range(18):
        RX[x] = inverse_weight(w * ROWS + x - 3, wide * ROWS)

    zero = functools.partial(jnp.zeros, dtype=F32)

    @pl.when(w == 0)
    def _():
        D[0:3] = zero((3, 64, DEEP))
        BL[0:3] = zero((3, 3, 32, DEEP))
        EN[:, 0] = zero((3, 32, 128))
        FXR[...] = zero((9, 16, 128))

    @pl.when(w == wide - 1)
    def _():
        D[15:18] = zero((3, 64, DEEP))
        BL[15:18] = zero((3, 3, 32, DEEP))
        EN[:, 5] = zero((3, 32, 128))
        U[:, 4] = zero((9, 24, 128))

    @pl.when(n == 0)
    def _():
        D[:, 0:8] = zero((18, 8, DEEP))
        BL[:, :, 0:8] = zero((18, 3, 8, DEEP))
        EN[:, :, 0:8] = zero((3, 6, 8, 128))
        FYR[...] = zero((9, 4, 8, 128))

    @pl.when(n == narrow - 1)
    def _():
        D[:, 56:64] = zero((18, 8, DEEP))
        BL[:, :, 24:32] = zero((18, 3, 8, DEEP))
        EN[:, :, 24:32] = zero((3, 6, 8, 128))
        U[:, :, 16:24] = zero((9, 5, 8, 128))

    @pl.when((n == 0) | (w == 0))
    def _():
        FDR[...] = zero((9, 8, 128))

    FS[...] = zero((9, 5, 24, 128))

    for copy in loads[4:]:
        copy.wait()

    def solid_step(x, _):
        for m in range(3):
            for t in range(2):
                for c in range(3):
                    void = PA[x, c, pl.ds(24 * t + m, 8, stride=3), :]
                    rows, lanes = slice(8 * t, 8 * t + 8), slice(128 * c, 128 * c + 128)
                    SW[x, m, rows, lanes] = (1.0 - void.astype(F32)) * (WT[m, rows, lanes] * RX[x + 3])
        return 0

    lax.fori_loop(0, ROWS, solid_step, 0)

    loads[0].wait()
    loads[1].wait()

    def moved(l):
        free = 1.0 - SU[l].astype(F32)
        for k in range(9):
            M[k, l] = U[k, l] * free

    for message in (moves[1], holds[1]):
        message.wait_recv()
    for l in range(4):
        moved(l)

    modes = mode_matrix()
    lane = lax.broadcasted_iota(jnp.int32, (8, 128), 1)

    def energy_step(r, l):
        i = r * 4 + l
        for t in range(2):
            hat = [None] * 24
            for comp in range(3):
                k = r * 3 + comp
                corner = {}
                for p in range(2):
                    for q in range(2):
                        v = M[k, l + p, pl.ds(8 * t + q, 8), :]
                        v1 = jnp.where(lane < 127, pltpu.roll(v, 127, axis=1), 0.0)
                        corner[p, q, 0], corner[p, q, 1] = v + v1, v1 - v
                for s in range(2):
                    y = {}
                    for p in range(2):
                        y[p, 0] = corner[p, 0, s] + corner[p, 1, s]
                        y[p, 1] = corner[p, 1, s] - corner[p, 0, s]
                    for q in range(2):
                        hat[3 * (2 * q + s) + comp] = y[0, q] + y[1, q]
                        hat[3 * (4 + 2 * q + s) + comp] = y[1, q] - y[0, q]
            energy = None
            for row in range(24):
                if not modes[row]:
                    continue
                value = None
                for j, factor in modes[row]:
                    term = hat[j] * factor
                    value = term if value is None else value + term
                V[i, row, 8 * t : 8 * t + 8] = value
                term = value * hat[row]
                energy = term if energy is None else energy + term
            EN[r, 1 + l, 8 + 8 * t : 16 + 8 * t] = energy

    def inner_energies(j, _):
        energy_step(j // 3, j % 3)
        return 0

    def last_energies(r, _):
        energy_step(r, 3)
        return 0

    lax.fori_loop(0, 9, inner_energies, 0)
    early = [message for message, d in zip(energies, DIRS) if d[0] < 0]
    late = [message for message, d in zip(energies, DIRS) if d[0] >= 0]
    for message in early:
        message.start()

    loads[2].wait()
    for message in designs:
        message.wait_recv()

    def x_step(t, _):
        rows = pl.ds(pl.multiple_of(8 * t, 8), 8)
        for c in range(3):
            out = tent([D[x, rows, 128 * c : 128 * c + 128] for x in range(18)])
            for x in range(ROWS):
                XF[x, c, rows, :] = out[x]
        return 0

    lax.fori_loop(0, 8, x_step, 0)

    def y_step(x, _):
        parts = {}
        for t in range(2):
            for c in range(3):
                out = tent([XF[x, c, pl.ds(8 + 24 * t + k, 8, stride=3), :] for k in range(-3, 6)])
                for m in range(3):
                    parts[m, t, c] = out[m]
        keep(AH, AL, x, parts)
        return 0

    lax.fori_loop(0, ROWS, y_step, 0)

    def z_step(groups):
        z = banded(AH, AL, BAND, groups)
        for i, g in enumerate(groups):
            for xr in range(3):
                x = 3 * g + xr
                for m in range(3):
                    at = 144 * i + 16 * (3 * xr + m)
                    for c in range(3):
                        lanes = slice(128 * c, 128 * c + 128)
                        BL[x + 3, m, 8:24, lanes] = z[c][at : at + 16] * SW[x, m, :, lanes]

    z_step((0, 3))
    z_step((1, 2))
    for message in fields[2:]:
        message.start()
    for message in (moves[0], holds[0], moves[2], holds[2]):
        message.wait_recv()
    moved(4)
    lax.fori_loop(0, 3, last_energies, 0)
    for message in late + fields[:2]:
        message.start()

    def own_step(xe, _):
        sums = [None] * 3
        for xr in range(3):
            for m in range(3):
                bl = BL[3 + 3 * xe + xr, m, 8:24, :]
                for r in range(3):
                    rho, _ = level(bl, thresholds[r])
                    cube = rho * rho * rho
                    sums[r] = cube if sums[r] is None else sums[r] + cube
        for r in range(3):
            S3[r, xe] = sums[r]
        return 0

    lax.fori_loop(0, 4, own_step, 0)
    moduli = times(S3[...].reshape(192, DEEP), GATHER[...]).reshape(12, 16, 128)
    for r in range(3):
        scale = (1.0 - stiff_floor) / 27.0 / denominator(thresholds[r]) ** 3
        MOD[4 * r : 4 * r + 4] = moduli[4 * r : 4 * r + 4] * scale + stiff_floor
    row8 = lax.broadcasted_iota(jnp.int32, (8, 128), 0)
    spot = lax.broadcasted_iota(jnp.int32, (1, 128), 1)
    line = zero((1, 128))
    for r in range(3):
        part = zero((8, 128))
        for l in range(4):
            for t in range(2):
                part = part + MOD[4 * r + l, 8 * t : 8 * t + 8] * EN[r, 1 + l, 8 + 8 * t : 16 + 8 * t]
        part = jnp.sum(jnp.sum(part, axis=0, keepdims=True), axis=1, keepdims=True)
        line = jnp.where(spot == r, part, line)
    AR1[pl.ds(i1, 1), :] = line

    def exchange(buf, ss, rs, me, count, peer):
        def remote(part, device):
            return pltpu.make_async_remote_copy(
                src_ref=part, dst_ref=part, send_sem=ss, recv_sem=rs, device_id=device, device_id_type=MESH
            )

        whole = remote(buf.at[pl.ds(0, count - 1)], peer(1))
        return [remote(buf.at[pl.ds(me, 1)], peer(k)) for k in range(1, count)], whole

    sends1, whole1 = exchange(AR1, a1s, a1r, i1, count1, peer1)
    sends2, whole2 = exchange(AR2, a2s, a2r, i2, count2, peer2)
    for send in sends1:
        send.start()

    def force_step(i, _):
        r, l = i // 4, i % 4
        for t in range(2):
            mod = MOD[i, 8 * t : 8 * t + 8]
            for comp in range(3):
                k = r * 3 + comp

                def mode(p, q, s):
                    row = 3 * (4 * p + 2 * q + s) + comp
                    return V[i, row, 8 * t : 8 * t + 8] * mod if modes[row] else None

                def minus(a, b):
                    return b * -1.0 if a is None else a - b

                def plus(a, b):
                    return b if a is None else a + b

                zz = {}
                for p in range(2):
                    for q in range(2):
                        v0, v1 = mode(p, q, 0), mode(p, q, 1)
                        high = jnp.where(lane > 0, pltpu.roll(plus(v0, v1), 1, axis=1), 0.0)
                        zz[p, q] = minus(v0, v1) + high
                for c in range(2):
                    y0, y1 = [
                        (zz[p, 1] + zz[p, 0]) if c else (zz[p, 0] - zz[p, 1]) for p in range(2)
                    ]
                    rows = pl.ds(8 * t + c, 8)
                    FS[k, l, rows, :] = FS[k, l, rows, :] + (y0 - y1)
                    FS[k, l + 1, rows, :] = FS[k, l + 1, rows, :] + (y0 + y1)
        return 0

    lax.fori_loop(0, 12, force_step, 0)

    block = jnp.concatenate([EN[r, l, 8:24] for r in range(3) for l in range(1, 5)], axis=0)
    ESP[:, 1:5, 0:16] = times(block, SPREAD[...]).reshape(3, 4, 16, DEEP)

    def terms(x, xe, m, bl, rows):
        scale = WT[m, rows] * RX[x]
        for r in range(3):
            rho, slope = level(bl, thresholds[r])
            T[r, x, m, rows] = rho * rho * slope * (ESP[r, xe, rows] * scale)

    def row_terms(x, _):
        for m in range(3):
            terms(x, x // 3, m, BL[x, m, 8:24, :], slice(0, 16))
        return 0

    def column_terms(x, _):
        for m in range(3):
            edge = lax.broadcasted_iota(jnp.int32, (8, DEEP), 0) == 7
            bl = jnp.where(edge, BL[x, m, 0:8, :], BL[x, m, 24:32, :])
            terms(x, x // 3, m, bl, slice(16, 24))
        return 0

    lax.fori_loop(3, 15, row_terms, 0)

    whole1.wait_recv()
    AR2[pl.ds(i2, 1), :] = jnp.sum(AR1[...], axis=0, keepdims=True)
    for send in sends2:
        send.start()
    for message in forces:
        message.start()

    for message in energies:
        message.wait_recv()
    blocks = []
    for r in range(3):
        blocks += [EN[r, 0, 8:24], EN[r, 5, 8:24]]
        for l in range(6):
            blocks.append(jnp.where(row8 == 7, EN[r, l, 0:8], EN[r, l, 24:32]))
    block = times(jnp.concatenate(blocks, axis=0), SPREAD[...])
    for r in range(3):
        ESP[r, 0, 0:16] = block[80 * r : 80 * r + 16]
        ESP[r, 5, 0:16] = block[80 * r + 16 : 80 * r + 32]
        for l in range(6):
            ESP[r, l, 16:24] = block[80 * r + 32 + 8 * l : 80 * r + 40 + 8 * l]
    for message in fields[2:4]:
        message.wait_recv()
    lax.fori_loop(3, 15, column_terms, 0)
    for message in fields[4:]:
        message.wait_recv()
    for l in (0, 15):
        lax.fori_loop(l, l + 3, column_terms, 0)
    for message in fields[:2]:
        message.wait_recv()
    for l in (0, 15):
        lax.fori_loop(l, l + 3, row_terms, 0)

    def back_step(r, _):
        def x_back(m, _):
            for t in range(3):
                for c in range(3):
                    lanes = slice(128 * c, 128 * c + 128)
                    rows = slice(8 * t, 8 * t + 8)
                    out = tent([T[r, x, m, rows, lanes] for x in range(18)])
                    for x in range(ROWS):
                        GX[x, m, c, 8 + 8 * t : 16 + 8 * t, :] = out[x]
                        if t == 2:
                            GX[x, m, c, 0:8, :] = out[x]
            return 0

        def y_back(x, _):
            for t in range(2):
                for c in range(3):
                    out = tent(
                        [GX[x, k % 3, c, pl.ds(8 + 8 * t + k // 3, 8), :] for k in range(-3, 6)]
                    )
                    for m in range(3):
                        at = 16 * m + 8 * t
                        Y[r, x, at : at + 8, 128 * c : 128 * c + 128] = out[m]
            return 0

        lax.fori_loop(0, 3, x_back, 0)
        lax.fori_loop(0, ROWS, y_back, 0)
        return 0

    lax.fori_loop(0, 3, back_step, 0)

    for message in forces:
        message.wait_recv()
    loads[3].wait()
    for k in range(9):
        FS[k, 0, 0:16] = FS[k, 0, 0:16] + FXR[k]
        FS[k, 0:4, 0:8] = FS[k, 0:4, 0:8] + jnp.where(
            lax.broadcasted_iota(jnp.int32, (4, 8, 128), 1) == 0, FYR[k], 0.0
        )
        FS[k, 0, 0:8] = FS[k, 0, 0:8] + jnp.where(row8 == 0, FDR[k], 0.0)
    free = 1.0 - SU[0:4, 0:16].astype(F32)
    load = LO[...].astype(F32) * (-load_force)
    for k in range(9):
        stiff = FS[k, 0:4, 0:16]
        RES[k] = ((load - stiff) if k % 3 == 2 else (0.0 - stiff)) * free

    whole2.wait_recv()
    COMP[...] = jnp.broadcast_to(jnp.sum(AR2[...], axis=0, keepdims=True), (8, 128))

    for message in moves + holds + designs + fields + energies + forces:
        message.wait_send()
    whole1.wait_send()
    whole2.wait_send()


def finish(Y, RES, COMP, BAND, res_out, comp_out, sens_out, AH, AL, OUT, osem):
    res_copy = pltpu.make_async_copy(RES, res_out, osem.at[6])
    res_copy.start()
    spot = lax.broadcasted_iota(jnp.int32, (1, 128), 1)
    for r in range(3):
        comp_out[r] = jnp.sum(jnp.where(spot == r, COMP[0:1], 0.0))

    def out_copy(g, c):
        return pltpu.make_async_copy(
            OUT.at[pl.ds(6 * g, 6), c],
            sens_out.at[pl.ds(6 * g, 6), :, 128 * c : 128 * c + 128],
            osem.at[3 * g + c],
        )

    scales = [
        jnp.broadcast_to(-slope_scale(thresholds[r]) / COMP[0:1, r : r + 1], (8, 128)) for r in range(3)
    ]

    def combine(x, _):
        parts = {}
        for m in range(3):
            for t in range(2):
                at = 16 * m + 8 * t
                for c in range(3):
                    lanes = slice(128 * c, 128 * c + 128)
                    value = Y[0, x, at : at + 8, lanes] * scales[0]
                    value = value + Y[1, x, at : at + 8, lanes] * scales[1]
                    parts[m, t, c] = value + Y[2, x, at : at + 8, lanes] * scales[2]
        keep(AH, AL, x, parts)
        return 0

    for g in range(2):
        lax.fori_loop(6 * g, 6 * g + 6, combine, 0)
        z = banded(AH, AL, BAND, (2 * g, 2 * g + 1))
        for c in range(3):
            for xr in range(6):
                for m in range(3):
                    for t in range(2):
                        at = 16 * (3 * xr + m) + 8 * t
                        OUT[6 * g + xr, c, pl.ds(24 * t + m, 8, stride=3), :] = z[c][at : at + 8]
            out_copy(g, c).start()
    res_copy.wait()
    for g in range(2):
        for c in range(3):
            out_copy(g, c).wait()


def solution(mesh):
    wide, narrow = mesh.shape["wide"], mesh.shape["narrow"]

    def local(design, passive, displacement, support, loading):
        sems = pltpu.SemaphoreType.DMA
        vmem = pl.BlockSpec(memory_space=pltpu.VMEM)
        hbm = pl.BlockSpec(memory_space=pltpu.MemorySpace.HBM)
        passed = (
            jax.ShapeDtypeStruct((3, ROWS, COLS, DEEP), F32),
            jax.ShapeDtypeStruct((9, EX, EY, EZ), F32),
            jax.ShapeDtypeStruct((8, 128), F32),
            jax.ShapeDtypeStruct((256, 256), BF16),
        )
        parts = pl.pallas_call(
            functools.partial(kernel, wide, narrow),
            out_shape=passed,
            in_specs=[hbm] * 5,
            out_specs=(vmem,) * 4,
            scratch_shapes=[
                pltpu.VMEM((ROWS, COLS, DEEP), BF16),
                pltpu.VMEM((ROWS, COLS, DEEP), BF16),
                pltpu.VMEM((18, 64, DEEP), F32),
                pltpu.VMEM((ROWS, 3, 64, 128), F32),
                pltpu.VMEM((ROWS, 3, COLS, 128), jnp.int32),
                pltpu.VMEM((ROWS, 3, 16, DEEP), F32),
                pltpu.VMEM((18, 3, 32, DEEP), F32),
                pltpu.VMEM((3, 18, 3, 24, DEEP), F32),
                pltpu.VMEM((3, 6, 32, 128), F32),
                pltpu.VMEM((3, 6, 24, DEEP), F32),
                pltpu.VMEM((ROWS, 3, 3, 32, 128), F32),
                pltpu.VMEM((12, 24, 16, 128), F32),
                pltpu.VMEM((9, 5, 24, 128), F32),
                pltpu.VMEM((9, 5, 24, 128), F32),
                pltpu.VMEM((9, 16, 128), F32),
                pltpu.VMEM((9, 4, 8, 128), F32),
                pltpu.VMEM((9, 8, 128), F32),
                pltpu.VMEM((9, 5, 24, 128), F32),
                pltpu.VMEM((5, 24, 128), jnp.int32),
                pltpu.VMEM((EX, EY, EZ), jnp.int32),
                pltpu.VMEM((12, 16, 128), F32),
                pltpu.VMEM((3, 4, 16, DEEP), F32),
                pltpu.VMEM((3, 24, DEEP), F32),
                pltpu.VMEM((EZ, DEEP), BF16),
                pltpu.VMEM((DEEP, EZ), BF16),
                pltpu.VMEM((wide // 2, 128), F32),
                pltpu.VMEM((2 * narrow, 128), F32),
                pltpu.SMEM((18,), F32),
                sems((7,)),
                sems((8,)), sems((8,)), sems((3,)), sems((3,)), sems((8,)), sems((8,)),
                sems((8,)), sems((8,)), sems((3,)), sems((3,)), sems((3,)), sems((3,)),
                sems, sems, sems, sems,
            ],
            compiler_params=pltpu.CompilerParams(
                collective_id=0, has_side_effects=True, vmem_limit_bytes=40 << 20
            ),
        )(*(
            pltpu.with_memory_space_constraint(a, pltpu.MemorySpace.HBM)
            for a in (design, passive, displacement.reshape(9, EX, EY, EZ), support, loading)
        ))
        residual, compliance, sensitivity = pl.pallas_call(
            finish,
            out_shape=(
                jax.ShapeDtypeStruct((9, EX, EY, EZ), F32),
                jax.ShapeDtypeStruct((3,), F32),
                jax.ShapeDtypeStruct((ROWS, COLS, DEEP), F32),
            ),
            in_specs=[vmem] * 4,
            out_specs=(hbm, pl.BlockSpec(memory_space=pltpu.SMEM), hbm),
            scratch_shapes=[
                pltpu.VMEM((ROWS, COLS, DEEP), BF16),
                pltpu.VMEM((ROWS, COLS, DEEP), BF16),
                pltpu.VMEM((ROWS, 3, COLS, 128), F32),
                sems((7,)),
            ],
            compiler_params=pltpu.CompilerParams(vmem_limit_bytes=8 << 20),
        )(*parts)
        return residual.reshape(3, 3, EX, EY, EZ), compliance, sensitivity

    in_specs = (
        P("wide", "narrow", None),
        P("wide", "narrow", None),
        P(None, None, "wide", "narrow", None),
        P("wide", "narrow", None),
        P("wide", "narrow", None),
    )
    out_specs = (P(None, None, "wide", "narrow", None), P(), P("wide", "narrow", None))
    return jax.shard_map(local, mesh=mesh, in_specs=in_specs, out_specs=out_specs, check_vma=False)
```

```python
import functools
import math

import jax
import jax.numpy as jnp
import numpy as np
from jax import lax
from jax.experimental import pallas as pl
from jax.experimental.pallas import tpu as pltpu
from jax.sharding import PartitionSpec as P

sharpness = 8.0
thresholds = (0.7, 0.5, 0.3)
stiff_floor = 0.001
load_force = 4.0
poisson = 0.3

F32, BF16 = jnp.float32, jnp.bfloat16
MESH = pl.DeviceIdType.MESH
ROWS, COLS, DEEP = 12, 48, 384
EX, EY, EZ = 4, 16, 128
DIRS = ((1, 0), (-1, 0), (0, 1), (0, -1), (1, 1), (1, -1), (-1, 1), (-1, -1))


def element_matrix():
    inv_root = 1.0 / np.sqrt(3.0)
    elastic = np.full((3, 3), poisson) + np.eye(3) * (1.0 - 2.0 * poisson)
    elastic = np.block(
        [[elastic, np.zeros((3, 3))], [np.zeros((3, 3)), np.eye(3) * (0.5 - poisson)]]
    ) / ((1.0 + poisson) * (1.0 - 2.0 * poisson))
    signs = [(2 * (c // 4) - 1, 2 * (c // 2 % 2) - 1, 2 * (c % 2) - 1) for c in range(8)]
    stiffness = np.zeros((24, 24))
    for ga in (-inv_root, inv_root):
        for gb in (-inv_root, inv_root):
            for gc in (-inv_root, inv_root):
                point = (ga, gb, gc)
                strain = np.zeros((6, 24))
                for c in range(8):
                    d = []
                    for along in range(3):
                        s = signs[c][along] / 4.0
                        for other in range(3):
                            if other != along:
                                s = s * (1.0 + signs[c][other] * point[other])
                        d.append(s)
                    col = 3 * c
                    strain[0, col], strain[1, col + 1], strain[2, col + 2] = d
                    strain[3, col], strain[3, col + 1] = d[1], d[0]
                    strain[4, col + 1], strain[4, col + 2] = d[2], d[1]
                    strain[5, col], strain[5, col + 2] = d[2], d[0]
                stiffness = stiffness + strain.T @ elastic @ strain * 0.125
    return stiffness


def mode_matrix():
    h = np.zeros((8, 8))
    for mode in range(8):
        for c in range(8):
            v = 1.0
            for bit in (4, 2, 1):
                if mode & bit:
                    v *= 1.0 if c & bit else -1.0
            h[mode, c] = v
    full = np.kron(h, np.eye(3))
    k = full @ element_matrix() @ full.T / 64.0
    return [
        [(j, float(k[i, j])) for j in range(24) if abs(k[i, j]) > 1e-9] for i in range(24)
    ]


def tent(values):
    p = [a + b for a, b in zip(values, values[1:])]
    q = [a + b for a, b in zip(p, p[2:])]
    r = [a + b for a, b in zip(q, q[1:])]
    return [a + b for a, b in zip(r, r[2:])]


def inverse_weight(place, extent):
    edge = jnp.minimum(place, extent - 1 - place)
    return jnp.where(
        edge >= 3, 1.0 / 16.0, jnp.where(edge == 2, 1.0 / 15.0, jnp.where(edge == 1, 1.0 / 13.0, 0.1))
    ).astype(F32)


def split(value):
    high = value.astype(BF16)
    return high, (value - high.astype(F32)).astype(BF16)


def times(value, matrix):
    high, low = split(value)
    return jnp.dot(high, matrix, preferred_element_type=F32) + jnp.dot(
        low, matrix, preferred_element_type=F32
    )


def level(bl, eta):
    low = math.tanh(sharpness * eta)
    t = jnp.tanh(bl * sharpness - sharpness * eta)
    return t + low, 1.0 - t * t


def denominator(eta):
    return math.tanh(sharpness * eta) + math.tanh(sharpness * (1.0 - eta))


def slope_scale(eta):
    return sharpness / denominator(eta) ** 3 * 3.0 * (1.0 - stiff_floor) / 27.0


def banded(high, low, band, groups):
    h, l = (
        jnp.concatenate([part[3 * g : 3 * g + 3].reshape(144, DEEP) for g in groups], axis=0)
        for part in (high, low)
    )
    b = band[...]
    first, second = (
        jnp.dot(h[:, k : k + 256], b, preferred_element_type=F32)
        + jnp.dot(l[:, k : k + 256], b, preferred_element_type=F32)
        for k in (0, 128)
    )
    lane = lax.broadcasted_iota(jnp.int32, (144 * len(groups), 128), 1)
    middle = jnp.where(lane < 64, first[:, 128:256], second[:, 0:128])
    return first[:, 0:128], middle, second[:, 128:256]


def keep(AH, AL, x, parts):
    for m in range(3):
        block = jnp.concatenate(
            [jnp.concatenate([parts[m, t, c] for t in range(2)], axis=0) for c in range(3)], axis=1
        )
        high, low = split(block)
        AH[x, 16 * m : 16 * m + 16, :] = high
        AL[x, 16 * m : 16 * m + 16, :] = low


def kernel(
    wide, narrow,
    design, passive, disp, support, loading,
    Y, RES, COMP, BAND,
    AH, AL, D, XF, PA, SW, BL, T, EN, ESP, GX, V, M, FS, FXR, FYR, FDR, U, SU, LO, MOD, S3,
    WT, SPREAD, GATHER, AR1, AR2, RX,
    lsem, dss, drs, mss, mrs, bss, brs, ess, ers, fss, frs, sss, srs, a1s, a1r, a2s, a2r,
):
    w = lax.axis_index("wide")
    n = lax.axis_index("narrow")
    zc, xl, core = w // 4, (w // 2) % 2, w % 2
    count1, count2 = wide // 2, 2 * narrow
    i1 = zc * 2 + core
    i2 = xl * narrow + n

    def within(dw, dn):
        ok = None
        for step, at, count in ((dw, w, wide), (dn, n, narrow)):
            if step:
                cond = at < count - 1 if step > 0 else at > 0
                ok = cond if ok is None else ok & cond
        return ok

    def peer1(k):
        j = (i1 + k) % count1
        return (j // 2) * 4 + xl * 2 + j % 2, n

    def peer2(k):
        j = (i2 + k) % count2
        return zc * 4 + (j // narrow) * 2 + core, j % narrow

    def around(dw, dn):
        return ((w + dw + wide) % wide, (n + dn + narrow) % narrow)

    barrier = pltpu.get_barrier_semaphore()
    total = count1 - 1 + count2 - 1
    for dw, dn in DIRS:
        total = total + within(dw, dn).astype(jnp.int32)

        @pl.when(within(dw, dn))
        def _(dw=dw, dn=dn):
            pl.semaphore_signal(barrier, 1, device_id=around(dw, dn), device_id_type=MESH)

    for k in range(1, count1):
        pl.semaphore_signal(barrier, 1, device_id=peer1(k), device_id_type=MESH)
    for k in range(1, count2):
        pl.semaphore_signal(barrier, 1, device_id=peer2(k), device_id_type=MESH)

    loads = [
        pltpu.make_async_copy(disp, U.at[:, 0:4, 0:16, :], lsem.at[0]),
        pltpu.make_async_copy(support, SU.at[0:4, 0:16, :], lsem.at[1]),
        pltpu.make_async_copy(design, D.at[3:15, 8:56, :], lsem.at[2]),
        pltpu.make_async_copy(loading, LO, lsem.at[3]),
    ] + [
        pltpu.make_async_copy(passive.at[:, :, 128 * c : 128 * c + 128], PA.at[:, c], lsem.at[4 + c])
        for c in range(3)
    ]
    for copy in loads:
        copy.start()

    class Message:
        def __init__(self, src, dst, ss, rs, dw, dn):
            self.to, self.origin = within(dw, dn), within(-dw, -dn)
            self.copy = pltpu.make_async_remote_copy(
                src_ref=src, dst_ref=dst, send_sem=ss, recv_sem=rs,
                device_id=around(dw, dn), device_id_type=MESH,
            )

        def start(self):
            pl.when(self.to)(self.copy.start)

        def wait_send(self):
            pl.when(self.to)(self.copy.wait_send)

        def wait_recv(self):
            pl.when(self.origin)(self.copy.wait_recv)

    def x_part(dw, low, high, depth):
        if dw == 0:
            return pl.ds(low, high - low), pl.ds(low, high - low)
        if dw > 0:
            return pl.ds(high - depth, depth), pl.ds(low - depth, depth)
        return pl.ds(low, depth), pl.ds(high, depth)

    designs, fields, energies = [], [], []
    for d, (dw, dn) in enumerate(DIRS):
        sx, tx = x_part(dw, 0, ROWS, 3)
        tx = pl.ds(tx.start + 3, tx.size)
        sy, ty = x_part(dn, 0, COLS, 3)
        ty = pl.ds(ty.start + 8, ty.size)
        designs.append(
            Message(design.at[sx, sy, :], D.at[tx, ty, :], dss.at[d], drs.at[d], dw, dn)
        )
        sx, tx = x_part(dw, 3, 15, 3)
        sy, ty = x_part(dn, 8, 24, 1)
        fields.append(
            Message(BL.at[sx, :, sy, :], BL.at[tx, :, ty, :], bss.at[d], brs.at[d], dw, dn)
        )
        sx, tx = x_part(dw, 1, 5, 1)
        energies.append(
            Message(EN.at[:, sx, sy, :], EN.at[:, tx, ty, :], ess.at[d], ers.at[d], dw, dn)
        )
    moves, holds, forces = [], [], []
    for d, (dw, dn) in enumerate(((-1, 0), (0, -1), (-1, -1))):
        sx, tx = x_part(dw, 0, 4, 1)
        sy, ty = x_part(dn, 0, 16, 1)
        moves.append(
            Message(disp.at[:, sx, sy, :], U.at[:, tx, ty, :], mss.at[d], mrs.at[d], dw, dn)
        )
        holds.append(
            Message(support.at[sx, sy, :], SU.at[tx, ty, :], sss.at[d], srs.at[d], dw, dn)
        )
    forces.append(Message(FS.at[:, 4, 0:16, :], FXR, fss.at[0], frs.at[0], 1, 0))
    forces.append(
        Message(FS.at[:, 0:4, 16:17, :], FYR.at[:, :, 0:1, :], fss.at[1], frs.at[1], 0, 1)
    )
    forces.append(Message(FS.at[:, 4, 16:17, :], FDR.at[:, 0:1, :], fss.at[2], frs.at[2], 1, 1))

    pl.semaphore_wait(barrier, total)
    for message in moves + holds + designs[2:] + designs[:2]:
        message.start()

    def near(shape):
        return lax.broadcasted_iota(jnp.int32, shape, 0), lax.broadcasted_iota(jnp.int32, shape, 1)

    a, b = near((256, 256))
    BAND[...] = jnp.maximum(4 - jnp.abs(a - b), 0).astype(F32).astype(BF16)
    a, b = near((EZ, DEEP))
    gap = b - 3 * a
    SPREAD[...] = jnp.where((gap >= 0) & (gap < 3), 1.0, 0.0).astype(BF16)
    a, b = near((DEEP, EZ))
    gap = a - 3 * b
    GATHER[...] = jnp.where((gap >= 0) & (gap < 3), 1.0, 0.0).astype(BF16)
    a, b = near((24, DEEP))
    a = jnp.where(a == 23, -1, a)
    deep = inverse_weight(b, DEEP)
    for m in range(3):
        WT[m] = inverse_weight(n * COLS + 3 * a + m, narrow * COLS) * deep
    for x in range(18):
        RX[x] = inverse_weight(w * ROWS + x - 3, wide * ROWS)

    zero = functools.partial(jnp.zeros, dtype=F32)

    @pl.when(w == 0)
    def _():
        D[0:3] = zero((3, 64, DEEP))
        BL[0:3] = zero((3, 3, 32, DEEP))
        EN[:, 0] = zero((3, 32, 128))
        FXR[...] = zero((9, 16, 128))

    @pl.when(w == wide - 1)
    def _():
        D[15:18] = zero((3, 64, DEEP))
        BL[15:18] = zero((3, 3, 32, DEEP))
        EN[:, 5] = zero((3, 32, 128))
        U[:, 4] = zero((9, 24, 128))

    @pl.when(n == 0)
    def _():
        D[:, 0:8] = zero((18, 8, DEEP))
        BL[:, :, 0:8] = zero((18, 3, 8, DEEP))
        EN[:, :, 0:8] = zero((3, 6, 8, 128))
        FYR[...] = zero((9, 4, 8, 128))

    @pl.when(n == narrow - 1)
    def _():
        D[:, 56:64] = zero((18, 8, DEEP))
        BL[:, :, 24:32] = zero((18, 3, 8, DEEP))
        EN[:, :, 24:32] = zero((3, 6, 8, 128))
        U[:, :, 16:24] = zero((9, 5, 8, 128))

    @pl.when((n == 0) | (w == 0))
    def _():
        FDR[...] = zero((9, 8, 128))

    FS[...] = zero((9, 5, 24, 128))

    for copy in loads[4:]:
        copy.wait()

    def solid_step(x, _):
        for m in range(3):
            for t in range(2):
                for c in range(3):
                    void = PA[x, c, pl.ds(24 * t + m, 8, stride=3), :]
                    rows, lanes = slice(8 * t, 8 * t + 8), slice(128 * c, 128 * c + 128)
                    SW[x, m, rows, lanes] = (1.0 - void.astype(F32)) * (WT[m, rows, lanes] * RX[x + 3])
        return 0

    lax.fori_loop(0, ROWS, solid_step, 0)

    loads[0].wait()
    loads[1].wait()

    def moved(l):
        free = 1.0 - SU[l].astype(F32)
        for k in range(9):
            M[k, l] = U[k, l] * free

    for message in (moves[1], holds[1]):
        message.wait_recv()
    for l in range(4):
        moved(l)

    modes = mode_matrix()
    lane = lax.broadcasted_iota(jnp.int32, (8, 128), 1)

    def energy_step(r, l):
        i = r * 4 + l
        for t in range(2):
            hat = [None] * 24
            for comp in range(3):
                k = r * 3 + comp
                corner = {}
                for p in range(2):
                    for q in range(2):
                        v = M[k, l + p, pl.ds(8 * t + q, 8), :]
                        v1 = jnp.where(lane < 127, pltpu.roll(v, 127, axis=1), 0.0)
                        corner[p, q, 0], corner[p, q, 1] = v + v1, v1 - v
                for s in range(2):
                    y = {}
                    for p in range(2):
                        y[p, 0] = corner[p, 0, s] + corner[p, 1, s]
                        y[p, 1] = corner[p, 1, s] - corner[p, 0, s]
                    for q in range(2):
                        hat[3 * (2 * q + s) + comp] = y[0, q] + y[1, q]
                        hat[3 * (4 + 2 * q + s) + comp] = y[1, q] - y[0, q]
            energy = None
            for row in range(24):
                if not modes[row]:
                    continue
                value = None
                for j, factor in modes[row]:
                    term = hat[j] * factor
                    value = term if value is None else value + term
                V[i, row, 8 * t : 8 * t + 8] = value
                term = value * hat[row]
                energy = term if energy is None else energy + term
            EN[r, 1 + l, 8 + 8 * t : 16 + 8 * t] = energy

    def inner_energies(j, _):
        energy_step(j // 3, j % 3)
        return 0

    def last_energies(r, _):
        energy_step(r, 3)
        return 0

    lax.fori_loop(0, 9, inner_energies, 0)
    for message in (moves[0], holds[0], moves[2], holds[2]):
        message.wait_recv()
    moved(4)
    lax.fori_loop(0, 3, last_energies, 0)
    for message in energies:
        message.start()

    loads[2].wait()
    for message in designs:
        message.wait_recv()

    def x_step(t, _):
        rows = pl.ds(pl.multiple_of(8 * t, 8), 8)
        for c in range(3):
            out = tent([D[x, rows, 128 * c : 128 * c + 128] for x in range(18)])
            for x in range(ROWS):
                XF[x, c, rows, :] = out[x]
        return 0

    lax.fori_loop(0, 8, x_step, 0)

    def y_step(x, _):
        parts = {}
        for t in range(2):
            for c in range(3):
                out = tent([XF[x, c, pl.ds(8 + 24 * t + k, 8, stride=3), :] for k in range(-3, 6)])
                for m in range(3):
                    parts[m, t, c] = out[m]
        keep(AH, AL, x, parts)
        return 0

    lax.fori_loop(0, ROWS, y_step, 0)

    def z_step(groups):
        z = banded(AH, AL, BAND, groups)
        for i, g in enumerate(groups):
            for xr in range(3):
                x = 3 * g + xr
                for m in range(3):
                    at = 144 * i + 16 * (3 * xr + m)
                    for c in range(3):
                        lanes = slice(128 * c, 128 * c + 128)
                        BL[x + 3, m, 8:24, lanes] = z[c][at : at + 16] * SW[x, m, :, lanes]

    z_step((0, 3))
    z_step((1, 2))
    for message in fields[2:] + fields[:2]:
        message.start()

    def own_step(xe, _):
        sums = [None] * 3
        for xr in range(3):
            for m in range(3):
                bl = BL[3 + 3 * xe + xr, m, 8:24, :]
                for r in range(3):
                    rho, _ = level(bl, thresholds[r])
                    cube = rho * rho * rho
                    sums[r] = cube if sums[r] is None else sums[r] + cube
        for r in range(3):
            S3[r, xe] = sums[r]
        return 0

    lax.fori_loop(0, 4, own_step, 0)
    moduli = times(S3[...].reshape(192, DEEP), GATHER[...]).reshape(12, 16, 128)
    for r in range(3):
        scale = (1.0 - stiff_floor) / 27.0 / denominator(thresholds[r]) ** 3
        MOD[4 * r : 4 * r + 4] = moduli[4 * r : 4 * r + 4] * scale + stiff_floor
    row8 = lax.broadcasted_iota(jnp.int32, (8, 128), 0)
    spot = lax.broadcasted_iota(jnp.int32, (1, 128), 1)
    line = zero((1, 128))
    for r in range(3):
        part = zero((8, 128))
        for l in range(4):
            for t in range(2):
                part = part + MOD[4 * r + l, 8 * t : 8 * t + 8] * EN[r, 1 + l, 8 + 8 * t : 16 + 8 * t]
        part = jnp.sum(jnp.sum(part, axis=0, keepdims=True), axis=1, keepdims=True)
        line = jnp.where(spot == r, part, line)
    AR1[pl.ds(i1, 1), :] = line

    def exchange(buf, ss, rs, me, count, peer):
        def remote(part, device):
            return pltpu.make_async_remote_copy(
                src_ref=part, dst_ref=part, send_sem=ss, recv_sem=rs, device_id=device, device_id_type=MESH
            )

        whole = remote(buf.at[pl.ds(0, count - 1)], peer(1))
        return [remote(buf.at[pl.ds(me, 1)], peer(k)) for k in range(1, count)], whole

    sends1, whole1 = exchange(AR1, a1s, a1r, i1, count1, peer1)
    sends2, whole2 = exchange(AR2, a2s, a2r, i2, count2, peer2)
    for send in sends1:
        send.start()

    def force_step(i, _):
        r, l = i // 4, i % 4
        for t in range(2):
            mod = MOD[i, 8 * t : 8 * t + 8]
            for comp in range(3):
                k = r * 3 + comp

                def mode(p, q, s):
                    row = 3 * (4 * p + 2 * q + s) + comp
                    return V[i, row, 8 * t : 8 * t + 8] * mod if modes[row] else None

                def minus(a, b):
                    return b * -1.0 if a is None else a - b

                def plus(a, b):
                    return b if a is None else a + b

                zz = {}
                for p in range(2):
                    for q in range(2):
                        v0, v1 = mode(p, q, 0), mode(p, q, 1)
                        high = jnp.where(lane > 0, pltpu.roll(plus(v0, v1), 1, axis=1), 0.0)
                        zz[p, q] = minus(v0, v1) + high
                for c in range(2):
                    y0, y1 = [
                        (zz[p, 1] + zz[p, 0]) if c else (zz[p, 0] - zz[p, 1]) for p in range(2)
                    ]
                    rows = pl.ds(8 * t + c, 8)
                    FS[k, l, rows, :] = FS[k, l, rows, :] + (y0 - y1)
                    FS[k, l + 1, rows, :] = FS[k, l + 1, rows, :] + (y0 + y1)
        return 0

    lax.fori_loop(0, 12, force_step, 0)

    block = jnp.concatenate([EN[r, l, 8:24] for r in range(3) for l in range(1, 5)], axis=0)
    ESP[:, 1:5, 0:16] = times(block, SPREAD[...]).reshape(3, 4, 16, DEEP)

    def terms(x, xe, m, bl, rows):
        scale = WT[m, rows] * RX[x]
        for r in range(3):
            rho, slope = level(bl, thresholds[r])
            T[r, x, m, rows] = rho * rho * slope * (ESP[r, xe, rows] * scale)

    def row_terms(x, _):
        for m in range(3):
            terms(x, x // 3, m, BL[x, m, 8:24, :], slice(0, 16))
        return 0

    def column_terms(x, _):
        for m in range(3):
            edge = lax.broadcasted_iota(jnp.int32, (8, DEEP), 0) == 7
            bl = jnp.where(edge, BL[x, m, 0:8, :], BL[x, m, 24:32, :])
            terms(x, x // 3, m, bl, slice(16, 24))
        return 0

    lax.fori_loop(3, 15, row_terms, 0)

    whole1.wait_recv()
    AR2[pl.ds(i2, 1), :] = jnp.sum(AR1[...], axis=0, keepdims=True)
    for send in sends2:
        send.start()
    for message in forces:
        message.start()

    for message in energies:
        message.wait_recv()
    blocks = []
    for r in range(3):
        blocks += [EN[r, 0, 8:24], EN[r, 5, 8:24]]
        for l in range(6):
            blocks.append(jnp.where(row8 == 7, EN[r, l, 0:8], EN[r, l, 24:32]))
    block = times(jnp.concatenate(blocks, axis=0), SPREAD[...])
    for r in range(3):
        ESP[r, 0, 0:16] = block[80 * r : 80 * r + 16]
        ESP[r, 5, 0:16] = block[80 * r + 16 : 80 * r + 32]
        for l in range(6):
            ESP[r, l, 16:24] = block[80 * r + 32 + 8 * l : 80 * r + 40 + 8 * l]
    for message in fields[2:4]:
        message.wait_recv()
    lax.fori_loop(3, 15, column_terms, 0)
    for message in fields[4:]:
        message.wait_recv()
    for l in (0, 15):
        lax.fori_loop(l, l + 3, column_terms, 0)
    for message in fields[:2]:
        message.wait_recv()
    for l in (0, 15):
        lax.fori_loop(l, l + 3, row_terms, 0)

    def back_step(r, _):
        def x_back(m, _):
            for t in range(3):
                for c in range(3):
                    lanes = slice(128 * c, 128 * c + 128)
                    rows = slice(8 * t, 8 * t + 8)
                    out = tent([T[r, x, m, rows, lanes] for x in range(18)])
                    for x in range(ROWS):
                        GX[x, m, c, 8 + 8 * t : 16 + 8 * t, :] = out[x]
                        if t == 2:
                            GX[x, m, c, 0:8, :] = out[x]
            return 0

        def y_back(x, _):
            for t in range(2):
                for c in range(3):
                    out = tent(
                        [GX[x, k % 3, c, pl.ds(8 + 8 * t + k // 3, 8), :] for k in range(-3, 6)]
                    )
                    for m in range(3):
                        at = 16 * m + 8 * t
                        Y[r, x, at : at + 8, 128 * c : 128 * c + 128] = out[m]
            return 0

        lax.fori_loop(0, 3, x_back, 0)
        lax.fori_loop(0, ROWS, y_back, 0)
        return 0

    lax.fori_loop(0, 3, back_step, 0)

    for message in forces:
        message.wait_recv()
    loads[3].wait()
    for k in range(9):
        FS[k, 0, 0:16] = FS[k, 0, 0:16] + FXR[k]
        FS[k, 0:4, 0:8] = FS[k, 0:4, 0:8] + jnp.where(
            lax.broadcasted_iota(jnp.int32, (4, 8, 128), 1) == 0, FYR[k], 0.0
        )
        FS[k, 0, 0:8] = FS[k, 0, 0:8] + jnp.where(row8 == 0, FDR[k], 0.0)
    free = 1.0 - SU[0:4, 0:16].astype(F32)
    load = LO[...].astype(F32) * (-load_force)
    for k in range(9):
        stiff = FS[k, 0:4, 0:16]
        RES[k] = ((load - stiff) if k % 3 == 2 else (0.0 - stiff)) * free

    whole2.wait_recv()
    COMP[...] = jnp.broadcast_to(jnp.sum(AR2[...], axis=0, keepdims=True), (8, 128))

    for message in moves + holds + designs + fields + energies + forces:
        message.wait_send()
    whole1.wait_send()
    whole2.wait_send()


def finish(Y, RES, COMP, BAND, res_out, comp_out, sens_out, AH, AL, OUT, osem):
    res_copy = pltpu.make_async_copy(RES, res_out, osem.at[6])
    res_copy.start()
    spot = lax.broadcasted_iota(jnp.int32, (1, 128), 1)
    for r in range(3):
        comp_out[r] = jnp.sum(jnp.where(spot == r, COMP[0:1], 0.0))

    def out_copy(g, c):
        return pltpu.make_async_copy(
            OUT.at[pl.ds(6 * g, 6), c],
            sens_out.at[pl.ds(6 * g, 6), :, 128 * c : 128 * c + 128],
            osem.at[3 * g + c],
        )

    scales = [
        jnp.broadcast_to(-slope_scale(thresholds[r]) / COMP[0:1, r : r + 1], (8, 128)) for r in range(3)
    ]

    def combine(x, _):
        parts = {}
        for m in range(3):
            for t in range(2):
                at = 16 * m + 8 * t
                for c in range(3):
                    lanes = slice(128 * c, 128 * c + 128)
                    value = Y[0, x, at : at + 8, lanes] * scales[0]
                    value = value + Y[1, x, at : at + 8, lanes] * scales[1]
                    parts[m, t, c] = value + Y[2, x, at : at + 8, lanes] * scales[2]
        keep(AH, AL, x, parts)
        return 0

    for g in range(2):
        lax.fori_loop(6 * g, 6 * g + 6, combine, 0)
        z = banded(AH, AL, BAND, (2 * g, 2 * g + 1))
        for c in range(3):
            for xr in range(6):
                for m in range(3):
                    for t in range(2):
                        at = 16 * (3 * xr + m) + 8 * t
                        OUT[6 * g + xr, c, pl.ds(24 * t + m, 8, stride=3), :] = z[c][at : at + 8]
            out_copy(g, c).start()
    res_copy.wait()
    for g in range(2):
        for c in range(3):
            out_copy(g, c).wait()


def solution(mesh):
    wide, narrow = mesh.shape["wide"], mesh.shape["narrow"]

    def local(design, passive, displacement, support, loading):
        sems = pltpu.SemaphoreType.DMA
        vmem = pl.BlockSpec(memory_space=pltpu.VMEM)
        hbm = pl.BlockSpec(memory_space=pltpu.MemorySpace.HBM)
        passed = (
            jax.ShapeDtypeStruct((3, ROWS, COLS, DEEP), F32),
            jax.ShapeDtypeStruct((9, EX, EY, EZ), F32),
            jax.ShapeDtypeStruct((8, 128), F32),
            jax.ShapeDtypeStruct((256, 256), BF16),
        )
        parts = pl.pallas_call(
            functools.partial(kernel, wide, narrow),
            out_shape=passed,
            in_specs=[hbm] * 5,
            out_specs=(vmem,) * 4,
            scratch_shapes=[
                pltpu.VMEM((ROWS, COLS, DEEP), BF16),
                pltpu.VMEM((ROWS, COLS, DEEP), BF16),
                pltpu.VMEM((18, 64, DEEP), F32),
                pltpu.VMEM((ROWS, 3, 64, 128), F32),
                pltpu.VMEM((ROWS, 3, COLS, 128), jnp.int32),
                pltpu.VMEM((ROWS, 3, 16, DEEP), F32),
                pltpu.VMEM((18, 3, 32, DEEP), F32),
                pltpu.VMEM((3, 18, 3, 24, DEEP), F32),
                pltpu.VMEM((3, 6, 32, 128), F32),
                pltpu.VMEM((3, 6, 24, DEEP), F32),
                pltpu.VMEM((ROWS, 3, 3, 32, 128), F32),
                pltpu.VMEM((12, 24, 16, 128), F32),
                pltpu.VMEM((9, 5, 24, 128), F32),
                pltpu.VMEM((9, 5, 24, 128), F32),
                pltpu.VMEM((9, 16, 128), F32),
                pltpu.VMEM((9, 4, 8, 128), F32),
                pltpu.VMEM((9, 8, 128), F32),
                pltpu.VMEM((9, 5, 24, 128), F32),
                pltpu.VMEM((5, 24, 128), jnp.int32),
                pltpu.VMEM((EX, EY, EZ), jnp.int32),
                pltpu.VMEM((12, 16, 128), F32),
                pltpu.VMEM((3, 4, 16, DEEP), F32),
                pltpu.VMEM((3, 24, DEEP), F32),
                pltpu.VMEM((EZ, DEEP), BF16),
                pltpu.VMEM((DEEP, EZ), BF16),
                pltpu.VMEM((wide // 2, 128), F32),
                pltpu.VMEM((2 * narrow, 128), F32),
                pltpu.SMEM((18,), F32),
                sems((7,)),
                sems((8,)), sems((8,)), sems((3,)), sems((3,)), sems((8,)), sems((8,)),
                sems((8,)), sems((8,)), sems((3,)), sems((3,)), sems((3,)), sems((3,)),
                sems, sems, sems, sems,
            ],
            compiler_params=pltpu.CompilerParams(
                collective_id=0, has_side_effects=True, vmem_limit_bytes=40 << 20
            ),
        )(*(
            pltpu.with_memory_space_constraint(a, pltpu.MemorySpace.HBM)
            for a in (design, passive, displacement.reshape(9, EX, EY, EZ), support, loading)
        ))
        residual, compliance, sensitivity = pl.pallas_call(
            finish,
            out_shape=(
                jax.ShapeDtypeStruct((9, EX, EY, EZ), F32),
                jax.ShapeDtypeStruct((3,), F32),
                jax.ShapeDtypeStruct((ROWS, COLS, DEEP), F32),
            ),
            in_specs=[vmem] * 4,
            out_specs=(hbm, pl.BlockSpec(memory_space=pltpu.SMEM), hbm),
            scratch_shapes=[
                pltpu.VMEM((ROWS, COLS, DEEP), BF16),
                pltpu.VMEM((ROWS, COLS, DEEP), BF16),
                pltpu.VMEM((ROWS, 3, COLS, 128), F32),
                sems((7,)),
            ],
            compiler_params=pltpu.CompilerParams(vmem_limit_bytes=8 << 20),
        )(*parts)
        return residual.reshape(3, 3, EX, EY, EZ), compliance, sensitivity

    in_specs = (
        P("wide", "narrow", None),
        P("wide", "narrow", None),
        P(None, None, "wide", "narrow", None),
        P("wide", "narrow", None),
        P("wide", "narrow", None),
    )
    out_specs = (P(None, None, "wide", "narrow", None), P(), P("wide", "narrow", None))
    return jax.shard_map(local, mesh=mesh, in_specs=in_specs, out_specs=out_specs, check_vma=False)
```

```python
import functools
import math

import jax
import jax.numpy as jnp
import numpy as np
from jax import lax
from jax.experimental import pallas as pl
from jax.experimental.pallas import tpu as pltpu
from jax.sharding import PartitionSpec as P

sharpness = 8.0
thresholds = (0.7, 0.5, 0.3)
stiff_floor = 0.001
load_force = 4.0
poisson = 0.3

F32, BF16 = jnp.float32, jnp.bfloat16
MESH = pl.DeviceIdType.MESH
ROWS, COLS, DEEP = 12, 48, 384
EX, EY, EZ = 4, 16, 128
DIRS = ((1, 0), (-1, 0), (0, 1), (0, -1), (1, 1), (1, -1), (-1, 1), (-1, -1))


def element_matrix():
    inv_root = 1.0 / np.sqrt(3.0)
    elastic = np.full((3, 3), poisson) + np.eye(3) * (1.0 - 2.0 * poisson)
    elastic = np.block(
        [[elastic, np.zeros((3, 3))], [np.zeros((3, 3)), np.eye(3) * (0.5 - poisson)]]
    ) / ((1.0 + poisson) * (1.0 - 2.0 * poisson))
    signs = [(2 * (c // 4) - 1, 2 * (c // 2 % 2) - 1, 2 * (c % 2) - 1) for c in range(8)]
    stiffness = np.zeros((24, 24))
    for ga in (-inv_root, inv_root):
        for gb in (-inv_root, inv_root):
            for gc in (-inv_root, inv_root):
                point = (ga, gb, gc)
                strain = np.zeros((6, 24))
                for c in range(8):
                    d = []
                    for along in range(3):
                        s = signs[c][along] / 4.0
                        for other in range(3):
                            if other != along:
                                s = s * (1.0 + signs[c][other] * point[other])
                        d.append(s)
                    col = 3 * c
                    strain[0, col], strain[1, col + 1], strain[2, col + 2] = d
                    strain[3, col], strain[3, col + 1] = d[1], d[0]
                    strain[4, col + 1], strain[4, col + 2] = d[2], d[1]
                    strain[5, col], strain[5, col + 2] = d[2], d[0]
                stiffness = stiffness + strain.T @ elastic @ strain * 0.125
    return stiffness


def mode_matrix():
    h = np.zeros((8, 8))
    for mode in range(8):
        for c in range(8):
            v = 1.0
            for bit in (4, 2, 1):
                if mode & bit:
                    v *= 1.0 if c & bit else -1.0
            h[mode, c] = v
    full = np.kron(h, np.eye(3))
    k = full @ element_matrix() @ full.T / 64.0
    return [
        [(j, float(k[i, j])) for j in range(24) if abs(k[i, j]) > 1e-9] for i in range(24)
    ]


def tent(values):
    p = [a + b for a, b in zip(values, values[1:])]
    q = [a + b for a, b in zip(p, p[2:])]
    r = [a + b for a, b in zip(q, q[1:])]
    return [a + b for a, b in zip(r, r[2:])]


def inverse_weight(place, extent):
    edge = jnp.minimum(place, extent - 1 - place)
    return jnp.where(
        edge >= 3, 1.0 / 16.0, jnp.where(edge == 2, 1.0 / 15.0, jnp.where(edge == 1, 1.0 / 13.0, 0.1))
    ).astype(F32)


def split(value):
    high = value.astype(BF16)
    return high, (value - high.astype(F32)).astype(BF16)


def times(value, matrix):
    high, low = split(value)
    return jnp.dot(high, matrix, preferred_element_type=F32) + jnp.dot(
        low, matrix, preferred_element_type=F32
    )


def level(bl, eta):
    low = math.tanh(sharpness * eta)
    t = jnp.tanh(bl * sharpness - sharpness * eta)
    return t + low, 1.0 - t * t


def denominator(eta):
    return math.tanh(sharpness * eta) + math.tanh(sharpness * (1.0 - eta))


def slope_scale(eta):
    return sharpness / denominator(eta) ** 3 * 3.0 * (1.0 - stiff_floor) / 27.0


def banded(high, low, band, groups):
    h, l = (
        jnp.concatenate([part[3 * g : 3 * g + 3].reshape(144, DEEP) for g in groups], axis=0)
        for part in (high, low)
    )
    b = band[...]
    first, second = (
        jnp.dot(h[:, k : k + 256], b, preferred_element_type=F32)
        + jnp.dot(l[:, k : k + 256], b, preferred_element_type=F32)
        for k in (0, 128)
    )
    lane = lax.broadcasted_iota(jnp.int32, (144 * len(groups), 128), 1)
    middle = jnp.where(lane < 64, first[:, 128:256], second[:, 0:128])
    return first[:, 0:128], middle, second[:, 128:256]


def keep(AH, AL, x, parts):
    for m in range(3):
        block = jnp.concatenate(
            [jnp.concatenate([parts[m, t, c] for t in range(2)], axis=0) for c in range(3)], axis=1
        )
        high, low = split(block)
        AH[x, 16 * m : 16 * m + 16, :] = high
        AL[x, 16 * m : 16 * m + 16, :] = low


def kernel(
    wide, narrow,
    design, passive, disp, support, loading,
    Y, RES, COMP, BAND,
    AH, AL, D, XF, PA, SW, BL, T, EN, ESP, GX, V, M, FS, FXR, FYR, FDR, U, SU, LO, MOD, S3,
    WT, SPREAD, GATHER, AR1, AR2, RX,
    lsem, dss, drs, mss, mrs, bss, brs, ess, ers, fss, frs, sss, srs, a1s, a1r, a2s, a2r,
):
    w = lax.axis_index("wide")
    n = lax.axis_index("narrow")
    zc, xl, core = w // 4, (w // 2) % 2, w % 2
    count1, count2 = wide // 2, 2 * narrow
    i1 = zc * 2 + core
    i2 = xl * narrow + n

    def within(dw, dn):
        ok = None
        for step, at, count in ((dw, w, wide), (dn, n, narrow)):
            if step:
                cond = at < count - 1 if step > 0 else at > 0
                ok = cond if ok is None else ok & cond
        return ok

    def peer1(k):
        j = (i1 + k) % count1
        return (j // 2) * 4 + xl * 2 + j % 2, n

    def peer2(k):
        j = (i2 + k) % count2
        return zc * 4 + (j // narrow) * 2 + core, j % narrow

    def around(dw, dn):
        return ((w + dw + wide) % wide, (n + dn + narrow) % narrow)

    barrier = pltpu.get_barrier_semaphore()
    total = count1 - 1 + count2 - 1
    for dw, dn in DIRS:
        total = total + within(dw, dn).astype(jnp.int32)

        @pl.when(within(dw, dn))
        def _(dw=dw, dn=dn):
            pl.semaphore_signal(barrier, 1, device_id=around(dw, dn), device_id_type=MESH)

    for k in range(1, count1):
        pl.semaphore_signal(barrier, 1, device_id=peer1(k), device_id_type=MESH)
    for k in range(1, count2):
        pl.semaphore_signal(barrier, 1, device_id=peer2(k), device_id_type=MESH)

    loads = [
        pltpu.make_async_copy(disp, U.at[:, 0:4, 0:16, :], lsem.at[0]),
        pltpu.make_async_copy(support, SU.at[0:4, 0:16, :], lsem.at[1]),
        pltpu.make_async_copy(design, D.at[3:15, 8:56, :], lsem.at[2]),
        pltpu.make_async_copy(loading, LO, lsem.at[3]),
    ] + [
        pltpu.make_async_copy(passive.at[:, :, 128 * c : 128 * c + 128], PA.at[:, c], lsem.at[4 + c])
        for c in range(3)
    ]
    for copy in loads:
        copy.start()

    class Message:
        def __init__(self, src, dst, ss, rs, dw, dn):
            self.to, self.origin = within(dw, dn), within(-dw, -dn)
            self.copy = pltpu.make_async_remote_copy(
                src_ref=src, dst_ref=dst, send_sem=ss, recv_sem=rs,
                device_id=around(dw, dn), device_id_type=MESH,
            )

        def start(self):
            pl.when(self.to)(self.copy.start)

        def wait_send(self):
            pl.when(self.to)(self.copy.wait_send)

        def wait_recv(self):
            pl.when(self.origin)(self.copy.wait_recv)

    def x_part(dw, low, high, depth):
        if dw == 0:
            return pl.ds(low, high - low), pl.ds(low, high - low)
        if dw > 0:
            return pl.ds(high - depth, depth), pl.ds(low - depth, depth)
        return pl.ds(low, depth), pl.ds(high, depth)

    designs, fields, energies = [], [], []
    for d, (dw, dn) in enumerate(DIRS):
        sx, tx = x_part(dw, 0, ROWS, 3)
        tx = pl.ds(tx.start + 3, tx.size)
        sy, ty = x_part(dn, 0, COLS, 3)
        ty = pl.ds(ty.start + 8, ty.size)
        designs.append(
            Message(design.at[sx, sy, :], D.at[tx, ty, :], dss.at[d], drs.at[d], dw, dn)
        )
        sx, tx = x_part(dw, 3, 15, 3)
        sy, ty = x_part(dn, 8, 24, 1)
        fields.append(
            Message(BL.at[sx, :, sy, :], BL.at[tx, :, ty, :], bss.at[d], brs.at[d], dw, dn)
        )
        sx, tx = x_part(dw, 1, 5, 1)
        energies.append(
            Message(EN.at[:, sx, sy, :], EN.at[:, tx, ty, :], ess.at[d], ers.at[d], dw, dn)
        )
    moves, holds, forces = [], [], []
    for d, (dw, dn) in enumerate(((-1, 0), (0, -1), (-1, -1))):
        sx, tx = x_part(dw, 0, 4, 1)
        sy, ty = x_part(dn, 0, 16, 1)
        moves.append(
            Message(disp.at[:, sx, sy, :], U.at[:, tx, ty, :], mss.at[d], mrs.at[d], dw, dn)
        )
        holds.append(
            Message(support.at[sx, sy, :], SU.at[tx, ty, :], sss.at[d], srs.at[d], dw, dn)
        )
    forces.append(Message(FS.at[:, 4, 0:16, :], FXR, fss.at[0], frs.at[0], 1, 0))
    forces.append(
        Message(FS.at[:, 0:4, 16:17, :], FYR.at[:, :, 0:1, :], fss.at[1], frs.at[1], 0, 1)
    )
    forces.append(Message(FS.at[:, 4, 16:17, :], FDR.at[:, 0:1, :], fss.at[2], frs.at[2], 1, 1))

    pl.semaphore_wait(barrier, total)
    for message in moves + holds + designs[2:] + designs[:2]:
        message.start()

    def near(shape):
        return lax.broadcasted_iota(jnp.int32, shape, 0), lax.broadcasted_iota(jnp.int32, shape, 1)

    a, b = near((256, 256))
    BAND[...] = jnp.maximum(4 - jnp.abs(a - b), 0).astype(F32).astype(BF16)
    a, b = near((EZ, DEEP))
    gap = b - 3 * a
    SPREAD[...] = jnp.where((gap >= 0) & (gap < 3), 1.0, 0.0).astype(BF16)
    a, b = near((DEEP, EZ))
    gap = a - 3 * b
    GATHER[...] = jnp.where((gap >= 0) & (gap < 3), 1.0, 0.0).astype(BF16)
    a, b = near((24, DEEP))
    a = jnp.where(a == 23, -1, a)
    deep = inverse_weight(b, DEEP)
    for m in range(3):
        WT[m] = inverse_weight(n * COLS + 3 * a + m, narrow * COLS) * deep
    for x in range(18):
        RX[x] = inverse_weight(w * ROWS + x - 3, wide * ROWS)

    zero = functools.partial(jnp.zeros, dtype=F32)

    @pl.when(w == 0)
    def _():
        D[0:3] = zero((3, 64, DEEP))
        BL[0:3] = zero((3, 3, 32, DEEP))
        EN[:, 0] = zero((3, 32, 128))
        FXR[...] = zero((9, 16, 128))

    @pl.when(w == wide - 1)
    def _():
        D[15:18] = zero((3, 64, DEEP))
        BL[15:18] = zero((3, 3, 32, DEEP))
        EN[:, 5] = zero((3, 32, 128))
        U[:, 4] = zero((9, 24, 128))

    @pl.when(n == 0)
    def _():
        D[:, 0:8] = zero((18, 8, DEEP))
        BL[:, :, 0:8] = zero((18, 3, 8, DEEP))
        EN[:, :, 0:8] = zero((3, 6, 8, 128))
        FYR[...] = zero((9, 4, 8, 128))

    @pl.when(n == narrow - 1)
    def _():
        D[:, 56:64] = zero((18, 8, DEEP))
        BL[:, :, 24:32] = zero((18, 3, 8, DEEP))
        EN[:, :, 24:32] = zero((3, 6, 8, 128))
        U[:, :, 16:24] = zero((9, 5, 8, 128))

    @pl.when((n == 0) | (w == 0))
    def _():
        FDR[...] = zero((9, 8, 128))

    FS[...] = zero((9, 5, 24, 128))

    for copy in loads[4:]:
        copy.wait()

    def solid_step(x, _):
        for m in range(3):
            for t in range(2):
                for c in range(3):
                    void = PA[x, c, pl.ds(24 * t + m, 8, stride=3), :]
                    rows, lanes = slice(8 * t, 8 * t + 8), slice(128 * c, 128 * c + 128)
                    SW[x, m, rows, lanes] = (1.0 - void.astype(F32)) * (WT[m, rows, lanes] * RX[x + 3])
        return 0

    lax.fori_loop(0, ROWS, solid_step, 0)

    loads[0].wait()
    loads[1].wait()

    def moved(l):
        free = 1.0 - SU[l].astype(F32)
        for k in range(9):
            M[k, l] = U[k, l] * free

    for message in (moves[1], holds[1]):
        message.wait_recv()
    for l in range(4):
        moved(l)

    modes = mode_matrix()
    lane = lax.broadcasted_iota(jnp.int32, (8, 128), 1)

    def energy_step(r, l):
        i = r * 4 + l
        for t in range(2):
            hat = [None] * 24
            for comp in range(3):
                k = r * 3 + comp
                corner = {}
                for p in range(2):
                    for q in range(2):
                        v = M[k, l + p, pl.ds(8 * t + q, 8), :]
                        v1 = jnp.where(lane < 127, pltpu.roll(v, 127, axis=1), 0.0)
                        corner[p, q, 0], corner[p, q, 1] = v + v1, v1 - v
                for s in range(2):
                    y = {}
                    for p in range(2):
                        y[p, 0] = corner[p, 0, s] + corner[p, 1, s]
                        y[p, 1] = corner[p, 1, s] - corner[p, 0, s]
                    for q in range(2):
                        hat[3 * (2 * q + s) + comp] = y[0, q] + y[1, q]
                        hat[3 * (4 + 2 * q + s) + comp] = y[1, q] - y[0, q]
            energy = None
            for row in range(24):
                if not modes[row]:
                    continue
                value = None
                for j, factor in modes[row]:
                    term = hat[j] * factor
                    value = term if value is None else value + term
                V[i, row, 8 * t : 8 * t + 8] = value
                term = value * hat[row]
                energy = term if energy is None else energy + term
            EN[r, 1 + l, 8 + 8 * t : 16 + 8 * t] = energy

    def inner_energies(j, _):
        energy_step(j // 3, j % 3)
        return 0

    def last_energies(r, _):
        energy_step(r, 3)
        return 0

    lax.fori_loop(0, 9, inner_energies, 0)
    for message in (moves[0], holds[0], moves[2], holds[2]):
        message.wait_recv()
    moved(4)
    lax.fori_loop(0, 3, last_energies, 0)
    for message in energies:
        message.start()

    loads[2].wait()
    for message in designs:
        message.wait_recv()

    def x_step(t, _):
        rows = pl.ds(pl.multiple_of(8 * t, 8), 8)
        for c in range(3):
            out = tent([D[x, rows, 128 * c : 128 * c + 128] for x in range(18)])
            for x in range(ROWS):
                XF[x, c, rows, :] = out[x]
        return 0

    lax.fori_loop(0, 8, x_step, 0)

    def y_step(x, _):
        parts = {}
        for t in range(2):
            for c in range(3):
                out = tent([XF[x, c, pl.ds(8 + 24 * t + k, 8, stride=3), :] for k in range(-3, 6)])
                for m in range(3):
                    parts[m, t, c] = out[m]
        keep(AH, AL, x, parts)
        return 0

    lax.fori_loop(0, ROWS, y_step, 0)

    def z_step(groups):
        z = banded(AH, AL, BAND, groups)
        for i, g in enumerate(groups):
            for xr in range(3):
                x = 3 * g + xr
                for m in range(3):
                    at = 144 * i + 16 * (3 * xr + m)
                    for c in range(3):
                        lanes = slice(128 * c, 128 * c + 128)
                        BL[x + 3, m, 8:24, lanes] = z[c][at : at + 16] * SW[x, m, :, lanes]

    z_step((0, 1, 2, 3))
    for message in fields[2:] + fields[:2]:
        message.start()

    def own_step(xe, _):
        sums = [None] * 3
        for xr in range(3):
            for m in range(3):
                bl = BL[3 + 3 * xe + xr, m, 8:24, :]
                for r in range(3):
                    rho, _ = level(bl, thresholds[r])
                    cube = rho * rho * rho
                    sums[r] = cube if sums[r] is None else sums[r] + cube
        for r in range(3):
            S3[r, xe] = sums[r]
        return 0

    lax.fori_loop(0, 4, own_step, 0)
    moduli = times(S3[...].reshape(192, DEEP), GATHER[...]).reshape(12, 16, 128)
    for r in range(3):
        scale = (1.0 - stiff_floor) / 27.0 / denominator(thresholds[r]) ** 3
        MOD[4 * r : 4 * r + 4] = moduli[4 * r : 4 * r + 4] * scale + stiff_floor
    row8 = lax.broadcasted_iota(jnp.int32, (8, 128), 0)
    spot = lax.broadcasted_iota(jnp.int32, (1, 128), 1)
    line = zero((1, 128))
    for r in range(3):
        part = zero((8, 128))
        for l in range(4):
            for t in range(2):
                part = part + MOD[4 * r + l, 8 * t : 8 * t + 8] * EN[r, 1 + l, 8 + 8 * t : 16 + 8 * t]
        part = jnp.sum(jnp.sum(part, axis=0, keepdims=True), axis=1, keepdims=True)
        line = jnp.where(spot == r, part, line)
    AR1[pl.ds(i1, 1), :] = line

    def exchange(buf, ss, rs, me, count, peer):
        def remote(part, device):
            return pltpu.make_async_remote_copy(
                src_ref=part, dst_ref=part, send_sem=ss, recv_sem=rs, device_id=device, device_id_type=MESH
            )

        whole = remote(buf.at[pl.ds(0, count - 1)], peer(1))
        return [remote(buf.at[pl.ds(me, 1)], peer(k)) for k in range(1, count)], whole

    sends1, whole1 = exchange(AR1, a1s, a1r, i1, count1, peer1)
    sends2, whole2 = exchange(AR2, a2s, a2r, i2, count2, peer2)
    for send in sends1:
        send.start()

    def force_step(i, _):
        r, l = i // 4, i % 4
        for t in range(2):
            mod = MOD[i, 8 * t : 8 * t + 8]
            for comp in range(3):
                k = r * 3 + comp

                def mode(p, q, s):
                    row = 3 * (4 * p + 2 * q + s) + comp
                    return V[i, row, 8 * t : 8 * t + 8] * mod if modes[row] else None

                def minus(a, b):
                    return b * -1.0 if a is None else a - b

                def plus(a, b):
                    return b if a is None else a + b

                zz = {}
                for p in range(2):
                    for q in range(2):
                        v0, v1 = mode(p, q, 0), mode(p, q, 1)
                        high = jnp.where(lane > 0, pltpu.roll(plus(v0, v1), 1, axis=1), 0.0)
                        zz[p, q] = minus(v0, v1) + high
                for c in range(2):
                    y0, y1 = [
                        (zz[p, 1] + zz[p, 0]) if c else (zz[p, 0] - zz[p, 1]) for p in range(2)
                    ]
                    rows = pl.ds(8 * t + c, 8)
                    FS[k, l, rows, :] = FS[k, l, rows, :] + (y0 - y1)
                    FS[k, l + 1, rows, :] = FS[k, l + 1, rows, :] + (y0 + y1)
        return 0

    lax.fori_loop(0, 12, force_step, 0)

    block = jnp.concatenate([EN[r, l, 8:24] for r in range(3) for l in range(1, 5)], axis=0)
    ESP[:, 1:5, 0:16] = times(block, SPREAD[...]).reshape(3, 4, 16, DEEP)

    def terms(x, xe, m, bl, rows):
        scale = WT[m, rows] * RX[x]
        for r in range(3):
            rho, slope = level(bl, thresholds[r])
            T[r, x, m, rows] = rho * rho * slope * (ESP[r, xe, rows] * scale)

    def row_terms(x, _):
        for m in range(3):
            terms(x, x // 3, m, BL[x, m, 8:24, :], slice(0, 16))
        return 0

    def column_terms(x, _):
        for m in range(3):
            edge = lax.broadcasted_iota(jnp.int32, (8, DEEP), 0) == 7
            bl = jnp.where(edge, BL[x, m, 0:8, :], BL[x, m, 24:32, :])
            terms(x, x // 3, m, bl, slice(16, 24))
        return 0

    lax.fori_loop(3, 15, row_terms, 0)

    whole1.wait_recv()
    AR2[pl.ds(i2, 1), :] = jnp.sum(AR1[...], axis=0, keepdims=True)
    for send in sends2:
        send.start()
    for message in forces:
        message.start()

    for message in energies:
        message.wait_recv()
    blocks = []
    for r in range(3):
        blocks += [EN[r, 0, 8:24], EN[r, 5, 8:24]]
        for l in range(6):
            blocks.append(jnp.where(row8 == 7, EN[r, l, 0:8], EN[r, l, 24:32]))
    block = times(jnp.concatenate(blocks, axis=0), SPREAD[...])
    for r in range(3):
        ESP[r, 0, 0:16] = block[80 * r : 80 * r + 16]
        ESP[r, 5, 0:16] = block[80 * r + 16 : 80 * r + 32]
        for l in range(6):
            ESP[r, l, 16:24] = block[80 * r + 32 + 8 * l : 80 * r + 40 + 8 * l]
    for message in fields[2:4]:
        message.wait_recv()
    lax.fori_loop(3, 15, column_terms, 0)
    for message in fields[4:]:
        message.wait_recv()
    for l in (0, 15):
        lax.fori_loop(l, l + 3, column_terms, 0)
    for message in fields[:2]:
        message.wait_recv()
    for l in (0, 15):
        lax.fori_loop(l, l + 3, row_terms, 0)

    def back_step(r, _):
        def x_back(m, _):
            for t in range(3):
                for c in range(3):
                    lanes = slice(128 * c, 128 * c + 128)
                    rows = slice(8 * t, 8 * t + 8)
                    out = tent([T[r, x, m, rows, lanes] for x in range(18)])
                    for x in range(ROWS):
                        GX[x, m, c, 8 + 8 * t : 16 + 8 * t, :] = out[x]
                        if t == 2:
                            GX[x, m, c, 0:8, :] = out[x]
            return 0

        def y_back(x, _):
            for t in range(2):
                for c in range(3):
                    out = tent(
                        [GX[x, k % 3, c, pl.ds(8 + 8 * t + k // 3, 8), :] for k in range(-3, 6)]
                    )
                    for m in range(3):
                        at = 16 * m + 8 * t
                        Y[r, x, at : at + 8, 128 * c : 128 * c + 128] = out[m]
            return 0

        lax.fori_loop(0, 3, x_back, 0)
        lax.fori_loop(0, ROWS, y_back, 0)
        return 0

    lax.fori_loop(0, 3, back_step, 0)

    for message in forces:
        message.wait_recv()
    loads[3].wait()
    for k in range(9):
        FS[k, 0, 0:16] = FS[k, 0, 0:16] + FXR[k]
        FS[k, 0:4, 0:8] = FS[k, 0:4, 0:8] + jnp.where(
            lax.broadcasted_iota(jnp.int32, (4, 8, 128), 1) == 0, FYR[k], 0.0
        )
        FS[k, 0, 0:8] = FS[k, 0, 0:8] + jnp.where(row8 == 0, FDR[k], 0.0)
    free = 1.0 - SU[0:4, 0:16].astype(F32)
    load = LO[...].astype(F32) * (-load_force)
    for k in range(9):
        stiff = FS[k, 0:4, 0:16]
        RES[k] = ((load - stiff) if k % 3 == 2 else (0.0 - stiff)) * free

    whole2.wait_recv()
    COMP[...] = jnp.broadcast_to(jnp.sum(AR2[...], axis=0, keepdims=True), (8, 128))

    for message in moves + holds + designs + fields + energies + forces:
        message.wait_send()
    whole1.wait_send()
    whole2.wait_send()


def finish(Y, RES, COMP, BAND, res_out, comp_out, sens_out, AH, AL, OUT, osem):
    res_copy = pltpu.make_async_copy(RES, res_out, osem.at[6])
    res_copy.start()

    def out_copy(g, c):
        return pltpu.make_async_copy(
            OUT.at[pl.ds(6 * g, 6), c],
            sens_out.at[pl.ds(6 * g, 6), :, 128 * c : 128 * c + 128],
            osem.at[3 * g + c],
        )

    scales = [
        jnp.broadcast_to(-slope_scale(thresholds[r]) / COMP[0:1, r : r + 1], (8, 128)) for r in range(3)
    ]

    def combine(x, _):
        parts = {}
        for m in range(3):
            for t in range(2):
                at = 16 * m + 8 * t
                for c in range(3):
                    lanes = slice(128 * c, 128 * c + 128)
                    value = Y[0, x, at : at + 8, lanes] * scales[0]
                    value = value + Y[1, x, at : at + 8, lanes] * scales[1]
                    parts[m, t, c] = value + Y[2, x, at : at + 8, lanes] * scales[2]
        keep(AH, AL, x, parts)
        return 0

    for g in range(2):
        lax.fori_loop(6 * g, 6 * g + 6, combine, 0)
        z = banded(AH, AL, BAND, (2 * g, 2 * g + 1))
        for c in range(3):
            for xr in range(6):
                for m in range(3):
                    for t in range(2):
                        at = 16 * (3 * xr + m) + 8 * t
                        OUT[6 * g + xr, c, pl.ds(24 * t + m, 8, stride=3), :] = z[c][at : at + 8]
            out_copy(g, c).start()
    spot = lax.broadcasted_iota(jnp.int32, (1, 128), 1)
    for r in range(3):
        comp_out[r] = jnp.sum(jnp.where(spot == r, COMP[0:1], 0.0))
    res_copy.wait()
    for g in range(2):
        for c in range(3):
            out_copy(g, c).wait()


def solution(mesh):
    wide, narrow = mesh.shape["wide"], mesh.shape["narrow"]

    def local(design, passive, displacement, support, loading):
        sems = pltpu.SemaphoreType.DMA
        vmem = pl.BlockSpec(memory_space=pltpu.VMEM)
        hbm = pl.BlockSpec(memory_space=pltpu.MemorySpace.HBM)
        passed = (
            jax.ShapeDtypeStruct((3, ROWS, COLS, DEEP), F32),
            jax.ShapeDtypeStruct((9, EX, EY, EZ), F32),
            jax.ShapeDtypeStruct((8, 128), F32),
            jax.ShapeDtypeStruct((256, 256), BF16),
        )
        parts = pl.pallas_call(
            functools.partial(kernel, wide, narrow),
            out_shape=passed,
            in_specs=[hbm] * 5,
            out_specs=(vmem,) * 4,
            scratch_shapes=[
                pltpu.VMEM((ROWS, COLS, DEEP), BF16),
                pltpu.VMEM((ROWS, COLS, DEEP), BF16),
                pltpu.VMEM((18, 64, DEEP), F32),
                pltpu.VMEM((ROWS, 3, 64, 128), F32),
                pltpu.VMEM((ROWS, 3, COLS, 128), jnp.int32),
                pltpu.VMEM((ROWS, 3, 16, DEEP), F32),
                pltpu.VMEM((18, 3, 32, DEEP), F32),
                pltpu.VMEM((3, 18, 3, 24, DEEP), F32),
                pltpu.VMEM((3, 6, 32, 128), F32),
                pltpu.VMEM((3, 6, 24, DEEP), F32),
                pltpu.VMEM((ROWS, 3, 3, 32, 128), F32),
                pltpu.VMEM((12, 24, 16, 128), F32),
                pltpu.VMEM((9, 5, 24, 128), F32),
                pltpu.VMEM((9, 5, 24, 128), F32),
                pltpu.VMEM((9, 16, 128), F32),
                pltpu.VMEM((9, 4, 8, 128), F32),
                pltpu.VMEM((9, 8, 128), F32),
                pltpu.VMEM((9, 5, 24, 128), F32),
                pltpu.VMEM((5, 24, 128), jnp.int32),
                pltpu.VMEM((EX, EY, EZ), jnp.int32),
                pltpu.VMEM((12, 16, 128), F32),
                pltpu.VMEM((3, 4, 16, DEEP), F32),
                pltpu.VMEM((3, 24, DEEP), F32),
                pltpu.VMEM((EZ, DEEP), BF16),
                pltpu.VMEM((DEEP, EZ), BF16),
                pltpu.VMEM((wide // 2, 128), F32),
                pltpu.VMEM((2 * narrow, 128), F32),
                pltpu.SMEM((18,), F32),
                sems((7,)),
                sems((8,)), sems((8,)), sems((3,)), sems((3,)), sems((8,)), sems((8,)),
                sems((8,)), sems((8,)), sems((3,)), sems((3,)), sems((3,)), sems((3,)),
                sems, sems, sems, sems,
            ],
            compiler_params=pltpu.CompilerParams(
                collective_id=0, has_side_effects=True, vmem_limit_bytes=40 << 20
            ),
        )(*(
            pltpu.with_memory_space_constraint(a, pltpu.MemorySpace.HBM)
            for a in (design, passive, displacement.reshape(9, EX, EY, EZ), support, loading)
        ))
        residual, compliance, sensitivity = pl.pallas_call(
            finish,
            out_shape=(
                jax.ShapeDtypeStruct((9, EX, EY, EZ), F32),
                jax.ShapeDtypeStruct((3,), F32),
                jax.ShapeDtypeStruct((ROWS, COLS, DEEP), F32),
            ),
            in_specs=[vmem] * 4,
            out_specs=(hbm, pl.BlockSpec(memory_space=pltpu.SMEM), hbm),
            scratch_shapes=[
                pltpu.VMEM((ROWS, COLS, DEEP), BF16),
                pltpu.VMEM((ROWS, COLS, DEEP), BF16),
                pltpu.VMEM((ROWS, 3, COLS, 128), F32),
                sems((7,)),
            ],
            compiler_params=pltpu.CompilerParams(vmem_limit_bytes=8 << 20),
        )(*parts)
        return residual.reshape(3, 3, EX, EY, EZ), compliance, sensitivity

    in_specs = (
        P("wide", "narrow", None),
        P("wide", "narrow", None),
        P(None, None, "wide", "narrow", None),
        P("wide", "narrow", None),
        P("wide", "narrow", None),
    )
    out_specs = (P(None, None, "wide", "narrow", None), P(), P("wide", "narrow", None))
    return jax.shard_map(local, mesh=mesh, in_specs=in_specs, out_specs=out_specs, check_vma=False)
```

```python
import functools
import math

import jax
import jax.numpy as jnp
import numpy as np
from jax import lax
from jax.experimental import pallas as pl
from jax.experimental.pallas import tpu as pltpu
from jax.sharding import PartitionSpec as P

sharpness = 8.0
thresholds = (0.7, 0.5, 0.3)
stiff_floor = 0.001
load_force = 4.0
poisson = 0.3

F32, BF16 = jnp.float32, jnp.bfloat16
MESH = pl.DeviceIdType.MESH
ROWS, COLS, DEEP = 12, 48, 384
EX, EY, EZ = 4, 16, 128
DIRS = ((1, 0), (-1, 0), (0, 1), (0, -1), (1, 1), (1, -1), (-1, 1), (-1, -1))


def element_matrix():
    inv_root = 1.0 / np.sqrt(3.0)
    elastic = np.full((3, 3), poisson) + np.eye(3) * (1.0 - 2.0 * poisson)
    elastic = np.block(
        [[elastic, np.zeros((3, 3))], [np.zeros((3, 3)), np.eye(3) * (0.5 - poisson)]]
    ) / ((1.0 + poisson) * (1.0 - 2.0 * poisson))
    signs = [(2 * (c // 4) - 1, 2 * (c // 2 % 2) - 1, 2 * (c % 2) - 1) for c in range(8)]
    stiffness = np.zeros((24, 24))
    for ga in (-inv_root, inv_root):
        for gb in (-inv_root, inv_root):
            for gc in (-inv_root, inv_root):
                point = (ga, gb, gc)
                strain = np.zeros((6, 24))
                for c in range(8):
                    d = []
                    for along in range(3):
                        s = signs[c][along] / 4.0
                        for other in range(3):
                            if other != along:
                                s = s * (1.0 + signs[c][other] * point[other])
                        d.append(s)
                    col = 3 * c
                    strain[0, col], strain[1, col + 1], strain[2, col + 2] = d
                    strain[3, col], strain[3, col + 1] = d[1], d[0]
                    strain[4, col + 1], strain[4, col + 2] = d[2], d[1]
                    strain[5, col], strain[5, col + 2] = d[2], d[0]
                stiffness = stiffness + strain.T @ elastic @ strain * 0.125
    return stiffness


def mode_matrix():
    h = np.zeros((8, 8))
    for mode in range(8):
        for c in range(8):
            v = 1.0
            for bit in (4, 2, 1):
                if mode & bit:
                    v *= 1.0 if c & bit else -1.0
            h[mode, c] = v
    full = np.kron(h, np.eye(3))
    k = full @ element_matrix() @ full.T / 64.0
    return [
        [(j, float(k[i, j])) for j in range(24) if abs(k[i, j]) > 1e-9] for i in range(24)
    ]


def tent(values):
    p = [a + b for a, b in zip(values, values[1:])]
    q = [a + b for a, b in zip(p, p[2:])]
    r = [a + b for a, b in zip(q, q[1:])]
    return [a + b for a, b in zip(r, r[2:])]


def inverse_weight(place, extent):
    edge = jnp.minimum(place, extent - 1 - place)
    return jnp.where(
        edge >= 3, 1.0 / 16.0, jnp.where(edge == 2, 1.0 / 15.0, jnp.where(edge == 1, 1.0 / 13.0, 0.1))
    ).astype(F32)


def split(value):
    high = value.astype(BF16)
    return high, (value - high.astype(F32)).astype(BF16)


def times(value, matrix):
    high, low = split(value)
    return jnp.dot(high, matrix, preferred_element_type=F32) + jnp.dot(
        low, matrix, preferred_element_type=F32
    )


def level(bl, eta):
    low = math.tanh(sharpness * eta)
    t = jnp.tanh(bl * sharpness - sharpness * eta)
    return t + low, 1.0 - t * t


def denominator(eta):
    return math.tanh(sharpness * eta) + math.tanh(sharpness * (1.0 - eta))


def slope_scale(eta):
    return sharpness / denominator(eta) ** 3 * 3.0 * (1.0 - stiff_floor) / 27.0


def banded(high, low, band, groups):
    h, l = (
        jnp.concatenate([part[3 * g : 3 * g + 3].reshape(144, DEEP) for g in groups], axis=0)
        for part in (high, low)
    )
    b = band[...]
    first, second = (
        jnp.dot(h[:, k : k + 256], b, preferred_element_type=F32)
        + jnp.dot(l[:, k : k + 256], b, preferred_element_type=F32)
        for k in (0, 128)
    )
    lane = lax.broadcasted_iota(jnp.int32, (144 * len(groups), 128), 1)
    middle = jnp.where(lane < 64, first[:, 128:256], second[:, 0:128])
    return first[:, 0:128], middle, second[:, 128:256]


def keep(AH, AL, x, parts):
    for m in range(3):
        block = jnp.concatenate(
            [jnp.concatenate([parts[m, t, c] for t in range(2)], axis=0) for c in range(3)], axis=1
        )
        high, low = split(block)
        AH[x, 16 * m : 16 * m + 16, :] = high
        AL[x, 16 * m : 16 * m + 16, :] = low


def kernel(
    wide, narrow,
    design, passive, disp, support, loading,
    Y, RES, COMP, BAND,
    AH, AL, D, XF, PA, SW, BL, T, EN, ESP, GX, V, M, FS, FXR, FYR, FDR, U, SU, LO, MOD, S3,
    WT, SPREAD, GATHER, AR1, AR2, RX,
    lsem, dss, drs, mss, mrs, bss, brs, ess, ers, fss, frs, sss, srs, a1s, a1r, a2s, a2r,
):
    w = lax.axis_index("wide")
    n = lax.axis_index("narrow")
    zc, xl, core = w // 4, (w // 2) % 2, w % 2
    count1, count2 = wide // 2, 2 * narrow
    i1 = zc * 2 + core
    i2 = xl * narrow + n

    def within(dw, dn):
        ok = None
        for step, at, count in ((dw, w, wide), (dn, n, narrow)):
            if step:
                cond = at < count - 1 if step > 0 else at > 0
                ok = cond if ok is None else ok & cond
        return ok

    def peer1(k):
        j = (i1 + k) % count1
        return (j // 2) * 4 + xl * 2 + j % 2, n

    def peer2(k):
        j = (i2 + k) % count2
        return zc * 4 + (j // narrow) * 2 + core, j % narrow

    def around(dw, dn):
        return ((w + dw + wide) % wide, (n + dn + narrow) % narrow)

    barrier = pltpu.get_barrier_semaphore()
    total = count1 - 1 + count2 - 1
    for dw, dn in DIRS:
        total = total + within(dw, dn).astype(jnp.int32)

        @pl.when(within(dw, dn))
        def _(dw=dw, dn=dn):
            pl.semaphore_signal(barrier, 1, device_id=around(dw, dn), device_id_type=MESH)

    for k in range(1, count1):
        pl.semaphore_signal(barrier, 1, device_id=peer1(k), device_id_type=MESH)
    for k in range(1, count2):
        pl.semaphore_signal(barrier, 1, device_id=peer2(k), device_id_type=MESH)

    loads = [
        pltpu.make_async_copy(disp, U.at[:, 0:4, 0:16, :], lsem.at[0]),
        pltpu.make_async_copy(support, SU.at[0:4, 0:16, :], lsem.at[1]),
        pltpu.make_async_copy(design, D.at[3:15, 8:56, :], lsem.at[2]),
        pltpu.make_async_copy(loading, LO, lsem.at[3]),
    ] + [
        pltpu.make_async_copy(passive.at[:, :, 128 * c : 128 * c + 128], PA.at[:, c], lsem.at[4 + c])
        for c in range(3)
    ]
    for copy in loads:
        copy.start()

    class Message:
        def __init__(self, src, dst, ss, rs, dw, dn):
            self.to, self.origin = within(dw, dn), within(-dw, -dn)
            self.copy = pltpu.make_async_remote_copy(
                src_ref=src, dst_ref=dst, send_sem=ss, recv_sem=rs,
                device_id=around(dw, dn), device_id_type=MESH,
            )

        def start(self):
            pl.when(self.to)(self.copy.start)

        def wait_send(self):
            pl.when(self.to)(self.copy.wait_send)

        def wait_recv(self):
            pl.when(self.origin)(self.copy.wait_recv)

    def x_part(dw, low, high, depth):
        if dw == 0:
            return pl.ds(low, high - low), pl.ds(low, high - low)
        if dw > 0:
            return pl.ds(high - depth, depth), pl.ds(low - depth, depth)
        return pl.ds(low, depth), pl.ds(high, depth)

    designs, fields, energies = [], [], []
    for d, (dw, dn) in enumerate(DIRS):
        sx, tx = x_part(dw, 0, ROWS, 3)
        tx = pl.ds(tx.start + 3, tx.size)
        sy, ty = x_part(dn, 0, COLS, 3)
        ty = pl.ds(ty.start + 8, ty.size)
        designs.append(
            Message(design.at[sx, sy, :], D.at[tx, ty, :], dss.at[d], drs.at[d], dw, dn)
        )
        sx, tx = x_part(dw, 3, 15, 3)
        sy, ty = x_part(dn, 8, 24, 1)
        fields.append(
            Message(BL.at[sx, :, sy, :], BL.at[tx, :, ty, :], bss.at[d], brs.at[d], dw, dn)
        )
        sx, tx = x_part(dw, 1, 5, 1)
        energies.append(
            Message(EN.at[:, sx, sy, :], EN.at[:, tx, ty, :], ess.at[d], ers.at[d], dw, dn)
        )
    moves, holds, forces = [], [], []
    for d, (dw, dn) in enumerate(((-1, 0), (0, -1), (-1, -1))):
        sx, tx = x_part(dw, 0, 4, 1)
        sy, ty = x_part(dn, 0, 16, 1)
        moves.append(
            Message(disp.at[:, sx, sy, :], U.at[:, tx, ty, :], mss.at[d], mrs.at[d], dw, dn)
        )
        holds.append(
            Message(support.at[sx, sy, :], SU.at[tx, ty, :], sss.at[d], srs.at[d], dw, dn)
        )
    forces.append(Message(FS.at[:, 4, 0:16, :], FXR, fss.at[0], frs.at[0], 1, 0))
    forces.append(
        Message(FS.at[:, 0:4, 16:17, :], FYR.at[:, :, 0:1, :], fss.at[1], frs.at[1], 0, 1)
    )
    forces.append(Message(FS.at[:, 4, 16:17, :], FDR.at[:, 0:1, :], fss.at[2], frs.at[2], 1, 1))

    pl.semaphore_wait(barrier, total)
    for message in moves[1:] + holds[1:] + designs[2:] + moves[:1] + holds[:1] + designs[:2]:
        message.start()

    def near(shape):
        return lax.broadcasted_iota(jnp.int32, shape, 0), lax.broadcasted_iota(jnp.int32, shape, 1)

    a, b = near((256, 256))
    BAND[...] = jnp.maximum(4 - jnp.abs(a - b), 0).astype(F32).astype(BF16)
    a, b = near((EZ, DEEP))
    gap = b - 3 * a
    SPREAD[...] = jnp.where((gap >= 0) & (gap < 3), 1.0, 0.0).astype(BF16)
    a, b = near((DEEP, EZ))
    gap = a - 3 * b
    GATHER[...] = jnp.where((gap >= 0) & (gap < 3), 1.0, 0.0).astype(BF16)
    a, b = near((24, DEEP))
    a = jnp.where(a == 23, -1, a)
    deep = inverse_weight(b, DEEP)
    for m in range(3):
        WT[m] = inverse_weight(n * COLS + 3 * a + m, narrow * COLS) * deep
    for x in range(18):
        RX[x] = inverse_weight(w * ROWS + x - 3, wide * ROWS)

    zero = functools.partial(jnp.zeros, dtype=F32)

    @pl.when(w == 0)
    def _():
        D[0:3] = zero((3, 64, DEEP))
        BL[0:3] = zero((3, 3, 32, DEEP))
        EN[:, 0] = zero((3, 32, 128))
        FXR[...] = zero((9, 16, 128))

    @pl.when(w == wide - 1)
    def _():
        D[15:18] = zero((3, 64, DEEP))
        BL[15:18] = zero((3, 3, 32, DEEP))
        EN[:, 5] = zero((3, 32, 128))
        U[:, 4] = zero((9, 24, 128))

    @pl.when(n == 0)
    def _():
        D[:, 0:8] = zero((18, 8, DEEP))
        BL[:, :, 0:8] = zero((18, 3, 8, DEEP))
        EN[:, :, 0:8] = zero((3, 6, 8, 128))
        FYR[...] = zero((9, 4, 8, 128))

    @pl.when(n == narrow - 1)
    def _():
        D[:, 56:64] = zero((18, 8, DEEP))
        BL[:, :, 24:32] = zero((18, 3, 8, DEEP))
        EN[:, :, 24:32] = zero((3, 6, 8, 128))
        U[:, :, 16:24] = zero((9, 5, 8, 128))

    @pl.when((n == 0) | (w == 0))
    def _():
        FDR[...] = zero((9, 8, 128))

    FS[...] = zero((9, 5, 24, 128))

    for copy in loads[4:]:
        copy.wait()

    def solid_step(x, _):
        for m in range(3):
            for t in range(2):
                for c in range(3):
                    void = PA[x, c, pl.ds(24 * t + m, 8, stride=3), :]
                    rows, lanes = slice(8 * t, 8 * t + 8), slice(128 * c, 128 * c + 128)
                    SW[x, m, rows, lanes] = (1.0 - void.astype(F32)) * (WT[m, rows, lanes] * RX[x + 3])
        return 0

    lax.fori_loop(0, ROWS, solid_step, 0)

    loads[0].wait()
    loads[1].wait()

    def moved(l):
        free = 1.0 - SU[l].astype(F32)
        for k in range(9):
            M[k, l] = U[k, l] * free

    for message in (moves[1], holds[1]):
        message.wait_recv()
    for l in range(4):
        moved(l)

    modes = mode_matrix()
    lane = lax.broadcasted_iota(jnp.int32, (8, 128), 1)

    def energy_step(r, l):
        i = r * 4 + l
        for t in range(2):
            hat = [None] * 24
            for comp in range(3):
                k = r * 3 + comp
                corner = {}
                for p in range(2):
                    for q in range(2):
                        v = M[k, l + p, pl.ds(8 * t + q, 8), :]
                        v1 = jnp.where(lane < 127, pltpu.roll(v, 127, axis=1), 0.0)
                        corner[p, q, 0], corner[p, q, 1] = v + v1, v1 - v
                for s in range(2):
                    y = {}
                    for p in range(2):
                        y[p, 0] = corner[p, 0, s] + corner[p, 1, s]
                        y[p, 1] = corner[p, 1, s] - corner[p, 0, s]
                    for q in range(2):
                        hat[3 * (2 * q + s) + comp] = y[0, q] + y[1, q]
                        hat[3 * (4 + 2 * q + s) + comp] = y[1, q] - y[0, q]
            energy = None
            for row in range(24):
                if not modes[row]:
                    continue
                value = None
                for j, factor in modes[row]:
                    term = hat[j] * factor
                    value = term if value is None else value + term
                V[i, row, 8 * t : 8 * t + 8] = value
                term = value * hat[row]
                energy = term if energy is None else energy + term
            EN[r, 1 + l, 8 + 8 * t : 16 + 8 * t] = energy

    def inner_energies(j, _):
        energy_step(j // 3, j % 3)
        return 0

    def last_energies(r, _):
        energy_step(r, 3)
        return 0

    lax.fori_loop(0, 9, inner_energies, 0)
    for message in (moves[0], holds[0], moves[2], holds[2]):
        message.wait_recv()
    moved(4)
    lax.fori_loop(0, 3, last_energies, 0)
    for message in energies:
        message.start()

    loads[2].wait()
    for message in designs:
        message.wait_recv()

    def x_step(t, _):
        rows = pl.ds(pl.multiple_of(8 * t, 8), 8)
        for c in range(3):
            out = tent([D[x, rows, 128 * c : 128 * c + 128] for x in range(18)])
            for x in range(ROWS):
                XF[x, c, rows, :] = out[x]
        return 0

    lax.fori_loop(0, 8, x_step, 0)

    def y_step(x, _):
        parts = {}
        for t in range(2):
            for c in range(3):
                out = tent([XF[x, c, pl.ds(8 + 24 * t + k, 8, stride=3), :] for k in range(-3, 6)])
                for m in range(3):
                    parts[m, t, c] = out[m]
        keep(AH, AL, x, parts)
        return 0

    lax.fori_loop(0, ROWS, y_step, 0)

    def z_step(groups):
        z = banded(AH, AL, BAND, groups)
        for i, g in enumerate(groups):
            for xr in range(3):
                x = 3 * g + xr
                for m in range(3):
                    at = 144 * i + 16 * (3 * xr + m)
                    for c in range(3):
                        lanes = slice(128 * c, 128 * c + 128)
                        BL[x + 3, m, 8:24, lanes] = z[c][at : at + 16] * SW[x, m, :, lanes]

    z_step((0, 1, 2, 3))
    for message in fields[2:] + fields[:2]:
        message.start()

    def own_step(xe, _):
        sums = [None] * 3
        for xr in range(3):
            for m in range(3):
                bl = BL[3 + 3 * xe + xr, m, 8:24, :]
                for r in range(3):
                    rho, _ = level(bl, thresholds[r])
                    cube = rho * rho * rho
                    sums[r] = cube if sums[r] is None else sums[r] + cube
        for r in range(3):
            S3[r, xe] = sums[r]
        return 0

    lax.fori_loop(0, 4, own_step, 0)
    moduli = times(S3[...].reshape(192, DEEP), GATHER[...]).reshape(12, 16, 128)
    for r in range(3):
        scale = (1.0 - stiff_floor) / 27.0 / denominator(thresholds[r]) ** 3
        MOD[4 * r : 4 * r + 4] = moduli[4 * r : 4 * r + 4] * scale + stiff_floor
    row8 = lax.broadcasted_iota(jnp.int32, (8, 128), 0)
    spot = lax.broadcasted_iota(jnp.int32, (1, 128), 1)
    line = zero((1, 128))
    for r in range(3):
        part = zero((8, 128))
        for l in range(4):
            for t in range(2):
                part = part + MOD[4 * r + l, 8 * t : 8 * t + 8] * EN[r, 1 + l, 8 + 8 * t : 16 + 8 * t]
        part = jnp.sum(jnp.sum(part, axis=0, keepdims=True), axis=1, keepdims=True)
        line = jnp.where(spot == r, part, line)
    AR1[pl.ds(i1, 1), :] = line

    def exchange(buf, ss, rs, me, count, peer):
        def remote(part, device):
            return pltpu.make_async_remote_copy(
                src_ref=part, dst_ref=part, send_sem=ss, recv_sem=rs, device_id=device, device_id_type=MESH
            )

        whole = remote(buf.at[pl.ds(0, count - 1)], peer(1))
        return [remote(buf.at[pl.ds(me, 1)], peer(k)) for k in range(1, count)], whole

    sends1, whole1 = exchange(AR1, a1s, a1r, i1, count1, peer1)
    sends2, whole2 = exchange(AR2, a2s, a2r, i2, count2, peer2)
    for send in sends1:
        send.start()

    def force_step(i, _):
        r, l = i // 4, i % 4
        for t in range(2):
            mod = MOD[i, 8 * t : 8 * t + 8]
            for comp in range(3):
                k = r * 3 + comp

                def mode(p, q, s):
                    row = 3 * (4 * p + 2 * q + s) + comp
                    return V[i, row, 8 * t : 8 * t + 8] * mod if modes[row] else None

                def minus(a, b):
                    return b * -1.0 if a is None else a - b

                def plus(a, b):
                    return b if a is None else a + b

                zz = {}
                for p in range(2):
                    for q in range(2):
                        v0, v1 = mode(p, q, 0), mode(p, q, 1)
                        high = jnp.where(lane > 0, pltpu.roll(plus(v0, v1), 1, axis=1), 0.0)
                        zz[p, q] = minus(v0, v1) + high
                for c in range(2):
                    y0, y1 = [
                        (zz[p, 1] + zz[p, 0]) if c else (zz[p, 0] - zz[p, 1]) for p in range(2)
                    ]
                    rows = pl.ds(8 * t + c, 8)
                    FS[k, l, rows, :] = FS[k, l, rows, :] + (y0 - y1)
                    FS[k, l + 1, rows, :] = FS[k, l + 1, rows, :] + (y0 + y1)
        return 0

    lax.fori_loop(0, 12, force_step, 0)

    block = jnp.concatenate([EN[r, l, 8:24] for r in range(3) for l in range(1, 5)], axis=0)
    ESP[:, 1:5, 0:16] = times(block, SPREAD[...]).reshape(3, 4, 16, DEEP)

    def terms(x, xe, m, bl, rows):
        scale = WT[m, rows] * RX[x]
        for r in range(3):
            rho, slope = level(bl, thresholds[r])
            T[r, x, m, rows] = rho * rho * slope * (ESP[r, xe, rows] * scale)

    def row_terms(x, _):
        for m in range(3):
            terms(x, x // 3, m, BL[x, m, 8:24, :], slice(0, 16))
        return 0

    def column_terms(x, _):
        for m in range(3):
            edge = lax.broadcasted_iota(jnp.int32, (8, DEEP), 0) == 7
            bl = jnp.where(edge, BL[x, m, 0:8, :], BL[x, m, 24:32, :])
            terms(x, x // 3, m, bl, slice(16, 24))
        return 0

    lax.fori_loop(3, 15, row_terms, 0)

    whole1.wait_recv()
    AR2[pl.ds(i2, 1), :] = jnp.sum(AR1[...], axis=0, keepdims=True)
    for send in sends2:
        send.start()
    for message in forces:
        message.start()

    for message in energies:
        message.wait_recv()
    blocks = []
    for r in range(3):
        blocks += [EN[r, 0, 8:24], EN[r, 5, 8:24]]
        for l in range(6):
            blocks.append(jnp.where(row8 == 7, EN[r, l, 0:8], EN[r, l, 24:32]))
    block = times(jnp.concatenate(blocks, axis=0), SPREAD[...])
    for r in range(3):
        ESP[r, 0, 0:16] = block[80 * r : 80 * r + 16]
        ESP[r, 5, 0:16] = block[80 * r + 16 : 80 * r + 32]
        for l in range(6):
            ESP[r, l, 16:24] = block[80 * r + 32 + 8 * l : 80 * r + 40 + 8 * l]
    for message in fields[2:4]:
        message.wait_recv()
    lax.fori_loop(3, 15, column_terms, 0)
    for message in fields[4:]:
        message.wait_recv()
    for l in (0, 15):
        lax.fori_loop(l, l + 3, column_terms, 0)
    for message in fields[:2]:
        message.wait_recv()
    for l in (0, 15):
        lax.fori_loop(l, l + 3, row_terms, 0)

    def back_step(r, _):
        def x_back(m, _):
            for t in range(3):
                for c in range(3):
                    lanes = slice(128 * c, 128 * c + 128)
                    rows = slice(8 * t, 8 * t + 8)
                    out = tent([T[r, x, m, rows, lanes] for x in range(18)])
                    for x in range(ROWS):
                        GX[x, m, c, 8 + 8 * t : 16 + 8 * t, :] = out[x]
                        if t == 2:
                            GX[x, m, c, 0:8, :] = out[x]
            return 0

        def y_back(x, _):
            for t in range(2):
                for c in range(3):
                    out = tent(
                        [GX[x, k % 3, c, pl.ds(8 + 8 * t + k // 3, 8), :] for k in range(-3, 6)]
                    )
                    for m in range(3):
                        at = 16 * m + 8 * t
                        Y[r, x, at : at + 8, 128 * c : 128 * c + 128] = out[m]
            return 0

        lax.fori_loop(0, 3, x_back, 0)
        lax.fori_loop(0, ROWS, y_back, 0)
        return 0

    lax.fori_loop(0, 3, back_step, 0)

    for message in forces:
        message.wait_recv()
    loads[3].wait()
    for k in range(9):
        FS[k, 0, 0:16] = FS[k, 0, 0:16] + FXR[k]
        FS[k, 0:4, 0:8] = FS[k, 0:4, 0:8] + jnp.where(
            lax.broadcasted_iota(jnp.int32, (4, 8, 128), 1) == 0, FYR[k], 0.0
        )
        FS[k, 0, 0:8] = FS[k, 0, 0:8] + jnp.where(row8 == 0, FDR[k], 0.0)
    free = 1.0 - SU[0:4, 0:16].astype(F32)
    load = LO[...].astype(F32) * (-load_force)
    for k in range(9):
        stiff = FS[k, 0:4, 0:16]
        RES[k] = ((load - stiff) if k % 3 == 2 else (0.0 - stiff)) * free

    whole2.wait_recv()
    COMP[...] = jnp.broadcast_to(jnp.sum(AR2[...], axis=0, keepdims=True), (8, 128))

    for message in moves + holds + designs + fields + energies + forces:
        message.wait_send()
    whole1.wait_send()
    whole2.wait_send()


def finish(Y, RES, COMP, BAND, res_out, comp_out, sens_out, AH, AL, OUT, osem):
    res_copy = pltpu.make_async_copy(RES, res_out, osem.at[6])
    res_copy.start()

    def out_copy(g, c):
        return pltpu.make_async_copy(
            OUT.at[pl.ds(6 * g, 6), c],
            sens_out.at[pl.ds(6 * g, 6), :, 128 * c : 128 * c + 128],
            osem.at[3 * g + c],
        )

    scales = [
        jnp.broadcast_to(-slope_scale(thresholds[r]) / COMP[0:1, r : r + 1], (8, 128)) for r in range(3)
    ]

    def combine(x, _):
        parts = {}
        for m in range(3):
            for t in range(2):
                at = 16 * m + 8 * t
                for c in range(3):
                    lanes = slice(128 * c, 128 * c + 128)
                    value = Y[0, x, at : at + 8, lanes] * scales[0]
                    value = value + Y[1, x, at : at + 8, lanes] * scales[1]
                    parts[m, t, c] = value + Y[2, x, at : at + 8, lanes] * scales[2]
        keep(AH, AL, x, parts)
        return 0

    for g in range(2):
        lax.fori_loop(6 * g, 6 * g + 6, combine, 0)
        z = banded(AH, AL, BAND, (2 * g, 2 * g + 1))
        for c in range(3):
            for xr in range(6):
                for m in range(3):
                    for t in range(2):
                        at = 16 * (3 * xr + m) + 8 * t
                        OUT[6 * g + xr, c, pl.ds(24 * t + m, 8, stride=3), :] = z[c][at : at + 8]
            out_copy(g, c).start()
    spot = lax.broadcasted_iota(jnp.int32, (1, 128), 1)
    for r in range(3):
        comp_out[r] = jnp.sum(jnp.where(spot == r, COMP[0:1], 0.0))
    res_copy.wait()
    for g in range(2):
        for c in range(3):
            out_copy(g, c).wait()


def solution(mesh):
    wide, narrow = mesh.shape["wide"], mesh.shape["narrow"]

    def local(design, passive, displacement, support, loading):
        sems = pltpu.SemaphoreType.DMA
        vmem = pl.BlockSpec(memory_space=pltpu.VMEM)
        hbm = pl.BlockSpec(memory_space=pltpu.MemorySpace.HBM)
        passed = (
            jax.ShapeDtypeStruct((3, ROWS, COLS, DEEP), F32),
            jax.ShapeDtypeStruct((9, EX, EY, EZ), F32),
            jax.ShapeDtypeStruct((8, 128), F32),
            jax.ShapeDtypeStruct((256, 256), BF16),
        )
        parts = pl.pallas_call(
            functools.partial(kernel, wide, narrow),
            out_shape=passed,
            in_specs=[hbm] * 5,
            out_specs=(vmem,) * 4,
            scratch_shapes=[
                pltpu.VMEM((ROWS, COLS, DEEP), BF16),
                pltpu.VMEM((ROWS, COLS, DEEP), BF16),
                pltpu.VMEM((18, 64, DEEP), F32),
                pltpu.VMEM((ROWS, 3, 64, 128), F32),
                pltpu.VMEM((ROWS, 3, COLS, 128), jnp.int32),
                pltpu.VMEM((ROWS, 3, 16, DEEP), F32),
                pltpu.VMEM((18, 3, 32, DEEP), F32),
                pltpu.VMEM((3, 18, 3, 24, DEEP), F32),
                pltpu.VMEM((3, 6, 32, 128), F32),
                pltpu.VMEM((3, 6, 24, DEEP), F32),
                pltpu.VMEM((ROWS, 3, 3, 32, 128), F32),
                pltpu.VMEM((12, 24, 16, 128), F32),
                pltpu.VMEM((9, 5, 24, 128), F32),
                pltpu.VMEM((9, 5, 24, 128), F32),
                pltpu.VMEM((9, 16, 128), F32),
                pltpu.VMEM((9, 4, 8, 128), F32),
                pltpu.VMEM((9, 8, 128), F32),
                pltpu.VMEM((9, 5, 24, 128), F32),
                pltpu.VMEM((5, 24, 128), jnp.int32),
                pltpu.VMEM((EX, EY, EZ), jnp.int32),
                pltpu.VMEM((12, 16, 128), F32),
                pltpu.VMEM((3, 4, 16, DEEP), F32),
                pltpu.VMEM((3, 24, DEEP), F32),
                pltpu.VMEM((EZ, DEEP), BF16),
                pltpu.VMEM((DEEP, EZ), BF16),
                pltpu.VMEM((wide // 2, 128), F32),
                pltpu.VMEM((2 * narrow, 128), F32),
                pltpu.SMEM((18,), F32),
                sems((7,)),
                sems((8,)), sems((8,)), sems((3,)), sems((3,)), sems((8,)), sems((8,)),
                sems((8,)), sems((8,)), sems((3,)), sems((3,)), sems((3,)), sems((3,)),
                sems, sems, sems, sems,
            ],
            compiler_params=pltpu.CompilerParams(
                collective_id=0, has_side_effects=True, vmem_limit_bytes=40 << 20
            ),
        )(*(
            pltpu.with_memory_space_constraint(a, pltpu.MemorySpace.HBM)
            for a in (design, passive, displacement.reshape(9, EX, EY, EZ), support, loading)
        ))
        residual, compliance, sensitivity = pl.pallas_call(
            finish,
            out_shape=(
                jax.ShapeDtypeStruct((9, EX, EY, EZ), F32),
                jax.ShapeDtypeStruct((3,), F32),
                jax.ShapeDtypeStruct((ROWS, COLS, DEEP), F32),
            ),
            in_specs=[vmem] * 4,
            out_specs=(hbm, pl.BlockSpec(memory_space=pltpu.SMEM), hbm),
            scratch_shapes=[
                pltpu.VMEM((ROWS, COLS, DEEP), BF16),
                pltpu.VMEM((ROWS, COLS, DEEP), BF16),
                pltpu.VMEM((ROWS, 3, COLS, 128), F32),
                sems((7,)),
            ],
            compiler_params=pltpu.CompilerParams(vmem_limit_bytes=8 << 20),
        )(*parts)
        return residual.reshape(3, 3, EX, EY, EZ), compliance, sensitivity

    in_specs = (
        P("wide", "narrow", None),
        P("wide", "narrow", None),
        P(None, None, "wide", "narrow", None),
        P("wide", "narrow", None),
        P("wide", "narrow", None),
    )
    out_specs = (P(None, None, "wide", "narrow", None), P(), P("wide", "narrow", None))
    return jax.shard_map(local, mesh=mesh, in_specs=in_specs, out_specs=out_specs, check_vma=False)
```
